32 devices in a mesh: dp: 8 (over z, x), tensor: 4 (over y, core).
Axes of the slice: x: 2, y: 2, z: 4, core: 2. Of those that a mesh axis runs over, the one named last changes fastest.
Arguments:
- x_first: bfloat16 [8, 2048, 512], P('dp', 'tensor'), may hold values from -6 to 6
- x_second: bfloat16 [8, 2048, 512], P('dp', 'tensor'), may hold values from -6 to 6
- memory: bfloat16 [8, 2048, 512], P('dp', 'tensor'), may hold values from -6 to 6
- cot_first: bfloat16 [8, 2048, 512], P('dp', 'tensor'), may hold values from -6 to 6
- cot_second: bfloat16 [8, 2048, 512], P('dp', 'tensor'), may hold values from -6 to 6
- seg_ids: int32 [8, 2, 2048], P('dp'), may hold values from 0 to 15, as said below
- lengths: int32 [8, 2], P('dp'), may hold values from 1536 to 2047, as said below
- perm: int32 [8], replicated, may hold values from 0 to 7, as said below
- inverse: int32 [8], replicated, may hold values from 0 to 7, as said below
- gains: float32 [3, 512], replicated, may hold values from 0.1 to 1.9
- w_self_qkv: bfloat16 [512, 3, 512], P(None, None, 'tensor'), may hold values from -0.25 to 0.25
- w_self_out: bfloat16 [512, 512], P('tensor'), may hold values from -2 to 2
- w_cross_q: bfloat16 [512, 512], P(None, 'tensor'), may hold values from -0.25 to 0.25
- w_cross_kv: bfloat16 [512, 2, 512], P(None, None, 'tensor'), may hold values from -0.25 to 0.25
- w_cross_out: bfloat16 [512, 512], P('tensor'), may hold values from -2 to 2
- w_up: bfloat16 [512, 2048], P(None, 'tensor'), may hold values from -0.25 to 0.25
- w_down: bfloat16 [2048, 512], P('tensor'), may hold values from -0.125 to 0.125
Outputs:
- y_first: bfloat16 [8, 2048, 512], P('dp', 'tensor')
- y_second: bfloat16 [8, 2048, 512], P('dp', 'tensor')
- grad_first: bfloat16 [8, 2048, 512], P('dp', 'tensor')
- grad_memory: float32 [8, 2048, 512], P('dp', 'tensor')
- grad_gains: float32 [3, 512], P(None, 'tensor')
- grad_self_qkv: float32 [512, 3, 512], P(None, None, 'tensor')
- grad_self_out: float32 [512, 512], P('tensor')
- grad_cross_q: float32 [512, 512], P(None, 'tensor')
- grad_cross_kv: float32 [512, 2, 512], P(None, None, 'tensor')
- grad_cross_out: float32 [512, 512], P('tensor')
- grad_up: float32 [512, 2048], P(None, 'tensor')
- grad_down: float32 [2048, 512], P('tensor')
The draws below stay inside these ranges and needn't reach their ends.
Inputs may be any that keep to these rules, and one draw needn't show every extreme that they name: `seg_ids`: along the positions of each row, target and memory alike, the ids never fall; the positions below that row's length hold exactly 16 documents numbered 0 to 15, each of one position or more. `lengths`: column 0 counts the used target positions of a row, column 1 its used memory positions; every row has an unused position of each kind. A permutation of 0 to 7: row r of the loader's order goes to balanced slot perm[r], whose memory, segment ids and lengths it uses. inverse[perm[r]] = r for every row r.
All inputs are finite; a program needn't handle non-finite values.
Results may differ from the reference program's by a relative error of at most 0.034.
Values may be sent and summed in bfloat16 or wider, within the bound.
No kernel may reach another device: no remote copies, remote signals or barrier semaphores. Data moves between devices by JAX's collectives and lax.ppermute only.
A program may use at most 192 MiB of HBM per device.

```python
import math
import jax
import jax.numpy as jnp
from jax import lax

D = 512
HEADS = 8
HEAD_DIM = 64
FF = 2048
ROW_LEN = 2048
DOCS = 16
ROWS = 8


def length_rows(key):
    subkey = jax.random.fold_in(key, 5)
    drawn = jax.random.randint(subkey, (ROWS, 2), ROW_LEN * 3 // 4, ROW_LEN, dtype=jnp.int32)
    drawn = drawn.at[0].set(ROW_LEN - 1)
    return drawn.at[1].set(ROW_LEN * 3 // 4)


def draw_lengths(key, part):
    return length_rows(key)


def draw_seg_ids(key, part):
    used_rows = length_rows(key)
    subkey = jax.random.fold_in(key, 9)
    ceiling = max(2, 2 ** 30 // ROW_LEN)
    random_bits = jax.random.randint(subkey, (ROWS, 2, ROW_LEN), 0, ceiling, dtype=jnp.int32)
    positions = jnp.arange(ROW_LEN, dtype=jnp.int32)
    usable = (positions[None, None, :] >= 1) & (positions[None, None, :] < used_rows[:, :, None])
    scores = jnp.where(usable, random_bits * ROW_LEN + positions[None, None, :], -1)
    picked, unused = lax.top_k(scores, DOCS - 1)
    cut_points = picked % ROW_LEN
    counted = positions[None, None, :, None] >= cut_points[:, :, None, :]
    return jnp.sum(counted.astype(jnp.int32), axis=-1).astype(jnp.int32)


def draw_perm(key, part):
    return jax.random.permutation(jax.random.fold_in(key, 11), ROWS).astype(jnp.int32)


def draw_inverse(key, part):
    ordering = draw_perm(key, part)
    return jnp.zeros((ROWS,), jnp.int32).at[ordering].set(jnp.arange(ROWS, dtype=jnp.int32))


def steps_of(stream_key, shape, cuts, low, largest):
    level = 1.0
    for position, parts in cuts:
        draws = jax.random.uniform(jax.random.fold_in(jax.random.fold_in(stream_key, 6), position), (parts,), jnp.float32, low / len(cuts), largest / len(cuts))
        level = level * jnp.repeat(jnp.exp(draws), shape[position] // parts).reshape((-1,) + (1,) * (len(shape) - 1 - position))
    return level


def normal_values(stream_key, dims, spread, limit, shards=(), kind=jnp.bfloat16):
    values = jax.random.normal(stream_key, dims, jnp.float32) * spread
    if len(shards) > 0:
        values = steps_of(stream_key, dims, shards, -0.22, 0.18) * values
    return jnp.clip(values, min=-limit, max=limit).astype(kind)


def setup_inputs(seed: int = 0) -> dict:
    keys = jax.random.split(jax.random.key(seed), 18)
    return {
        "x_first": normal_values(keys[0], (ROWS, ROW_LEN, D), 1.0, 6.0, ((0, 8), (1, 4))),
        "x_second": normal_values(keys[1], (ROWS, ROW_LEN, D), 1.0, 6.0, ((0, 8), (1, 4))),
        "memory": normal_values(keys[2], (ROWS, ROW_LEN, D), 1.0, 6.0, ((0, 8), (1, 4))),
        "cot_first": normal_values(keys[3], (ROWS, ROW_LEN, D), 1.0, 6.0, ((0, 8), (1, 4))),
        "cot_second": normal_values(keys[4], (ROWS, ROW_LEN, D), 1.0, 6.0, ((0, 8), (1, 4))),
        "seg_ids": draw_seg_ids(jax.random.fold_in(keys[17], 71), 0),
        "lengths": draw_lengths(jax.random.fold_in(keys[17], 71), 0),
        "perm": draw_perm(jax.random.fold_in(keys[17], 71), 0),
        "inverse": draw_inverse(jax.random.fold_in(keys[17], 71), 0),
        "gains": jnp.clip(1.0 + 0.18 * jax.random.normal(keys[9], (3, D), jnp.float32), 0.1, 1.9),
        "w_self_qkv": normal_values(keys[10], (D, 3, HEADS * HEAD_DIM), D ** -0.5, 0.25, ((2, 4),)),
        "w_self_out": normal_values(keys[11], (HEADS * HEAD_DIM, D), (2 * D * DOCS // ROW_LEN) ** -0.5, 2.0, ((0, 4),)),
        "w_cross_q": normal_values(keys[12], (D, HEADS * HEAD_DIM), D ** -0.5, 0.25, ((1, 4),)),
        "w_cross_kv": normal_values(keys[13], (D, 2, HEADS * HEAD_DIM), D ** -0.5, 0.25, ((2, 4),)),
        "w_cross_out": normal_values(keys[14], (HEADS * HEAD_DIM, D), (2 * D * DOCS // ROW_LEN) ** -0.5, 2.0, ((0, 4),)),
        "w_up": normal_values(keys[15], (D, FF), D ** -0.5, 0.25, ((1, 4),)),
        "w_down": normal_values(keys[16], (FF, D), FF ** -0.5, 0.125, ((0, 4),)),
    }


EPSILON = 1e-05
NEG_FILL = -1e+30
HIGHEST = lax.Precision.HIGHEST

@jax.custom_vjp
def low(v):
    return lax.optimization_barrier(v.astype(jnp.bfloat16)).astype(jnp.float32)

@jax.custom_vjp
def low_back(v):
    return v

def low_keep(v):
    return (low(v), None)

def low_pass(kept, grad):
    return (grad,)

def back_keep(v):
    return (v, None)

def back_low(kept, grad):
    return (low(grad),)
low.defvjp(low_keep, low_pass)
low_back.defvjp(back_keep, back_low)

def layer_norm(hidden, gain):
    mean_value = lax.optimization_barrier(jnp.mean(hidden, axis=-1, keepdims=True))
    centred = hidden - mean_value
    inv_sigma = lax.rsqrt(lax.optimization_barrier(jnp.mean(centred * centred, axis=-1, keepdims=True)) + EPSILON)
    return centred * inv_sigma * gain

def plain_softmax(scores):
    top_score = lax.optimization_barrier(jnp.max(scores, axis=-1, keepdims=True))
    raised = jnp.exp(scores - top_score)
    return raised / lax.optimization_barrier(jnp.sum(raised, axis=-1, keepdims=True))

def attention(queries, keys_in, values_in, meta_query, meta_key):
    scaling = 1.0 / math.sqrt(queries.shape[-1])
    scores = jnp.einsum('gqhd,gkhd->ghqk', queries, keys_in, precision=HIGHEST) * scaling
    scores = low_back(scores)
    allowed = meta_query[:, None, :, None] == meta_key[:, None, None, :]
    scores = jnp.where(allowed, scores, jnp.full_like(scores, NEG_FILL))
    attn_probs = low(plain_softmax(scores))
    outputs = jnp.einsum('ghqk,gkhd->gqhd', attn_probs, values_in, precision=HIGHEST)
    return low_back(low(outputs.reshape(outputs.shape[0], outputs.shape[1], -1)))

def decoder_step(hidden, memory_kv, meta_target, meta_memory, gains, weights):
    qkv_weight, self_out_weight, cross_q_weight, cross_out_weight, upper_weight, lower_weight = weights
    group_size = hidden.shape[0]
    heads_shape = (group_size, ROW_LEN, HEADS, HEAD_DIM)
    normed = low(layer_norm(hidden, gains[0]))
    packed = low_back(low(jnp.einsum('gld,dcn->glcn', normed, qkv_weight, precision=HIGHEST)))
    attended = attention(packed[:, :, 0].reshape(heads_shape), packed[:, :, 1].reshape(heads_shape), packed[:, :, 2].reshape(heads_shape), meta_target, meta_target)
    hidden = hidden + low_back(jnp.einsum('gln,nd->gld', attended, self_out_weight, precision=HIGHEST))
    normed = low(layer_norm(hidden, gains[1]))
    cross_query = low_back(low(jnp.einsum('gld,dn->gln', normed, cross_q_weight, precision=HIGHEST)))
    attended = attention(cross_query.reshape(heads_shape), memory_kv[:, :, 0].reshape(heads_shape), memory_kv[:, :, 1].reshape(heads_shape), meta_target, meta_memory)
    hidden = hidden + low_back(jnp.einsum('gln,nd->gld', attended, cross_out_weight, precision=HIGHEST))
    normed = low(layer_norm(hidden, gains[2]))
    upper = low_back(jnp.einsum('gld,df->glf', normed, upper_weight, precision=HIGHEST))
    inner = low(jax.nn.gelu(upper, approximate=True))
    return hidden + low_back(jnp.einsum('glf,fd->gld', inner, lower_weight, precision=HIGHEST))

def group_pass(pieces, gains, weights, kv_weight):
    first_group, second_group, memory_group, meta_group = pieces
    memory_kv = low_back(low(jnp.einsum('gld,dcn->glcn', memory_group, kv_weight, precision=HIGHEST)))
    meta_target = meta_group[:, 0]
    meta_memory = meta_group[:, 1]
    out_one = decoder_step(first_group, memory_kv, meta_target, meta_memory, gains, weights)
    out_two = decoder_step(second_group, memory_kv, meta_target, meta_memory, gains, weights)
    return (out_one, out_two)

def reference(x_first, x_second, memory, cot_first, cot_second, seg_ids, lengths, perm, inverse, gains, w_self_qkv, w_self_out, w_cross_q, w_cross_kv, w_cross_out, w_up, w_down):
    positions = jnp.arange(ROW_LEN, dtype=jnp.int32)
    meta = jnp.where(positions[None, None, :] < lengths[:, :, None], seg_ids, jnp.int32(-1)).astype(jnp.int32)
    perm_index = perm.astype(jnp.int32)
    inverse_index = inverse.astype(jnp.int32)
    group_size = math.gcd(ROWS, max(1, 4096 // ROW_LEN))
    group_count = ROWS // group_size
    second_groups = x_second.astype(jnp.float32).reshape(group_count, group_size, ROW_LEN, D)
    meta_groups = meta.reshape(group_count, group_size, 2, ROW_LEN)
    checked = jax.checkpoint(group_pass)

    def forward(first_in, memory_in, gain_in, qkv_weight, self_out_weight, cross_q_weight, kv_weight, cross_out_weight, upper_weight, lower_weight):
        balanced = jnp.take(first_in, inverse_index, axis=0).reshape(group_count, group_size, ROW_LEN, D)
        memory_groups = memory_in.reshape(group_count, group_size, ROW_LEN, D)
        weights = (qkv_weight, self_out_weight, cross_q_weight, cross_out_weight, upper_weight, lower_weight)

        def one_group(pieces):
            return checked(pieces, gain_in, weights, kv_weight)
        out_one, out_two = lax.map(one_group, (balanced, second_groups, memory_groups, meta_groups))
        out_one = jnp.take(out_one.reshape(ROWS, ROW_LEN, D), perm_index, axis=0)
        return (out_one, out_two.reshape(ROWS, ROW_LEN, D))
    (out_one, out_two), pullback = jax.vjp(forward, x_first.astype(jnp.float32), memory.astype(jnp.float32), gains.astype(jnp.float32), w_self_qkv.astype(jnp.float32), w_self_out.astype(jnp.float32), w_cross_q.astype(jnp.float32), w_cross_kv.astype(jnp.float32), w_cross_out.astype(jnp.float32), w_up.astype(jnp.float32), w_down.astype(jnp.float32))
    valid = (positions[None, :] < lengths[:, 0:1]).astype(jnp.float32)
    cot_one = cot_first.astype(jnp.float32) * jnp.take(valid, perm_index, axis=0)[:, :, None]
    cot_two = cot_second.astype(jnp.float32) * valid[:, :, None]
    grads = pullback((cot_one, cot_two))
    return (out_one.astype(jnp.bfloat16), out_two.astype(jnp.bfloat16), grads[0].astype(jnp.bfloat16), grads[1], grads[2], grads[3], grads[4], grads[5], grads[6], grads[7], grads[8], grads[9])
```

```python
import functools
import math

import jax
import jax.numpy as jnp
from jax import lax
from jax.experimental import pallas as pl
from jax.experimental.pallas import tpu as pltpu
from jax.sharding import PartitionSpec as P

HEAD_DIM = 64
EPSILON = 1e-05
NEG_FILL = -1e30
DOCS = 16
PAIR = 2 * HEAD_DIM
BQ = 256
BK = 256
ALIGN = 128
BF = jnp.bfloat16
F32 = jnp.float32
VMEM_BYTES = 56 * 1024 * 1024
LOG2E = 1.4426950408889634

ANY = pl.BlockSpec(memory_space=pl.ANY)
SMEM = pl.BlockSpec(memory_space=pltpu.SMEM)
VM = pl.BlockSpec(memory_space=pltpu.VMEM)


def dot(a, b):
    return lax.dot_general(a, b, (((1,), (0,)), ((), ())), preferred_element_type=F32)


def dot_nt(a, b):
    return lax.dot_general(a, b, (((1,), (1,)), ((), ())), preferred_element_type=F32)


def dot_tn(a, b):
    return lax.dot_general(a, b, (((0,), (0,)), ((), ())), preferred_element_type=F32)


def normalize(hidden):
    centred = hidden - jnp.mean(hidden, axis=-1, keepdims=True)
    inv_sigma = lax.rsqrt(jnp.mean(centred * centred, axis=-1, keepdims=True) + EPSILON)
    return centred * inv_sigma, inv_sigma


def normalize_back(grad_scaled, gain, normal, inv_sigma):
    grad_normal = grad_scaled * gain
    first_mean = jnp.mean(grad_normal, axis=-1, keepdims=True)
    second_mean = jnp.mean(grad_normal * normal, axis=-1, keepdims=True)
    return inv_sigma * (grad_normal - first_mean - normal * second_mean)


def call(body, outs, scratch, name, cost):
    def run(*args, specs):
        moved = sum(a.size * a.dtype.itemsize for a in args)
        return pl.pallas_call(
            body,
            out_shape=outs,
            in_specs=specs,
            out_specs=jax.tree.map(lambda _: VM, outs),
            scratch_shapes=scratch,
            compiler_params=pltpu.CompilerParams(vmem_limit_bytes=VMEM_BYTES),
            cost_estimate=pl.CostEstimate(flops=int(cost * 1.15e9), bytes_accessed=moved, transcendentals=0),
            name=name,
        )(*args)

    return run


def struct(shape, dtype):
    return jax.ShapeDtypeStruct(shape, dtype)


QUERY_AT, KEY_AT, PLACE_AT = 0, DOCS + 2, 2 * (DOCS + 2)


def key_limits(scalars, key_at, length):
    place = lax.broadcasted_iota(jnp.int32, (1, length), 1)
    first = jnp.full((1, length), scalars[key_at], jnp.int32)
    after = jnp.full((1, length), scalars[key_at + 1], jnp.int32)
    for doc in range(1, DOCS + 1):
        inside = place >= scalars[QUERY_AT + doc]
        first = jnp.where(inside, scalars[key_at + doc], first)
        after = jnp.where(inside, scalars[key_at + doc + 1], after)
    return first, after


def window(scalars, key_at, begin):
    low = scalars[key_at]
    high = scalars[key_at + 1]
    for doc in range(1, DOCS + 1):
        low = jnp.where(begin >= scalars[QUERY_AT + doc], scalars[key_at + doc], low)
        high = jnp.where(
            begin + (BQ - 1) >= scalars[QUERY_AT + doc], scalars[key_at + doc + 1], high
        )
    low = (low // ALIGN) * ALIGN
    return low, (high - low + (BK - 1)) // BK


def two_heads(block):
    lane = lax.broadcasted_iota(jnp.int32, block.shape, 1)
    zero = jnp.zeros_like(block)
    return jnp.concatenate(
        [jnp.where(lane < HEAD_DIM, block, zero), jnp.where(lane >= HEAD_DIM, block, zero)], axis=0
    )


def attend_forward(scalars, key_at, q_s, k_s, vt_s, o_s, lse_s, first_s, after_s):
    length = q_s.shape[0]
    scale = LOG2E / math.sqrt(HEAD_DIM)
    first, after = key_limits(scalars, key_at, length)
    first_s[...] = first
    after_s[...] = after
    rows = lax.broadcasted_iota(jnp.int32, (BK, BQ), 0)

    def one_block(index, unused):
        begin = pl.multiple_of(index * BQ, BQ)
        low, count = window(scalars, key_at, begin)
        first_row = first_s[:, pl.ds(begin, BQ)]
        after_row = after_s[:, pl.ds(begin, BQ)]
        for pair in range(q_s.shape[1] // PAIR):
            lanes = slice(pair * PAIR, (pair + 1) * PAIR)
            query = two_heads(q_s[pl.ds(begin, BQ), lanes])

            def step(turn, carry):
                top, total, out = carry
                start = pl.multiple_of(low + turn * BK, ALIGN)
                allowed = (rows >= first_row - start) & (rows < after_row - start)
                allowed = jnp.concatenate([allowed, allowed], axis=1)
                scores = dot_nt(k_s[pl.ds(start, BK), lanes], query) * scale
                scores = jnp.where(allowed, scores, NEG_FILL)
                new_top = jnp.maximum(top, jnp.max(scores, axis=0, keepdims=True))
                shrink = jnp.exp2(top - new_top)
                raised = jnp.exp2(scores - new_top)
                total = total * shrink + jnp.sum(raised, axis=0, keepdims=True)
                low_probs = raised.astype(BF)
                value = vt_s[lanes, pl.ds(start, BK)]
                parts = [
                    dot(value[:HEAD_DIM], low_probs[:, :BQ]),
                    dot(value[HEAD_DIM:], low_probs[:, BQ:]),
                ]
                out = [
                    out[0] * shrink[:, :BQ] + parts[0],
                    out[1] * shrink[:, BQ:] + parts[1],
                ]
                return new_top, total, out

            top, total, out = lax.fori_loop(
                0,
                count,
                step,
                (
                    jnp.full((1, 2 * BQ), NEG_FILL, F32),
                    jnp.zeros((1, 2 * BQ), F32),
                    [jnp.zeros((HEAD_DIM, BQ), F32), jnp.zeros((HEAD_DIM, BQ), F32)],
                ),
            )
            inverse = 1.0 / total
            out = jnp.concatenate([out[0] * inverse[:, :BQ], out[1] * inverse[:, BQ:]], axis=0)
            o_s[pl.ds(begin, BQ), lanes] = out.T.astype(BF)
            log_total = top + jnp.log2(total)
            lse_s[2 * pair : 2 * pair + 1, pl.ds(begin, BQ)] = log_total[:, :BQ]
            lse_s[2 * pair + 1 : 2 * pair + 2, pl.ds(begin, BQ)] = log_total[:, BQ:]
        return unused

    lax.fori_loop(0, length // BQ, one_block, 0)


def attend_backward(
    scalars, key_at, q_s, k_s, kt_s, v_s, o_s, do_s, lse_s, dq_s, dk_s, dv_s, first_s, after_s
):
    length = q_s.shape[0]
    scale = LOG2E / math.sqrt(HEAD_DIM)
    first, after = key_limits(scalars, key_at, length)
    first_s[...] = first
    after_s[...] = after
    rows = lax.broadcasted_iota(jnp.int32, (BK, BQ), 0)
    dk_s[...] = jnp.zeros_like(dk_s)
    dv_s[...] = jnp.zeros_like(dv_s)
    ones = jnp.ones((8, PAIR), F32)

    def one_block(index, unused):
        begin = pl.multiple_of(index * BQ, BQ)
        low, count = window(scalars, key_at, begin)
        first_row = first_s[:, pl.ds(begin, BQ)]
        after_row = after_s[:, pl.ds(begin, BQ)]
        for pair in range(q_s.shape[1] // PAIR):
            lanes = slice(pair * PAIR, (pair + 1) * PAIR)
            query = two_heads(q_s[pl.ds(begin, BQ), lanes])
            grad = two_heads(do_s[pl.ds(begin, BQ), lanes])
            out = o_s[pl.ds(begin, BQ), lanes].astype(F32)
            product = grad.astype(F32) * jnp.concatenate([out, out], axis=0)
            centre = lax.dot_general(
                ones,
                product,
                (((1,), (1,)), ((), ())),
                precision=lax.Precision.HIGHEST,
                preferred_element_type=F32,
            )[:1]
            log_total = jnp.concatenate(
                [
                    lse_s[2 * pair : 2 * pair + 1, pl.ds(begin, BQ)],
                    lse_s[2 * pair + 1 : 2 * pair + 2, pl.ds(begin, BQ)],
                ],
                axis=1,
            )

            def step(turn, carry):
                start = pl.multiple_of(low + turn * BK, ALIGN)
                allowed = (rows >= first_row - start) & (rows < after_row - start)
                allowed = jnp.concatenate([allowed, allowed], axis=1)
                keys = k_s[pl.ds(start, BK), lanes]
                scores = dot_nt(keys, query) * scale
                probs = jnp.exp2(jnp.where(allowed, scores, NEG_FILL) - log_total)
                dprobs = dot_nt(v_s[pl.ds(start, BK), lanes], grad)
                dscores = (probs * (dprobs - centre)).astype(BF)
                dv_s[pl.ds(start, BK), lanes] += dot(probs.astype(BF), grad)
                dk_s[pl.ds(start, BK), lanes] += dot(dscores, query)
                kt = kt_s[lanes, pl.ds(start, BK)]
                return [
                    carry[0] + dot(kt[:HEAD_DIM], dscores[:, :BQ]),
                    carry[1] + dot(kt[HEAD_DIM:], dscores[:, BQ:]),
                ]

            dq = lax.fori_loop(
                0,
                count,
                step,
                [jnp.zeros((HEAD_DIM, BQ), F32), jnp.zeros((HEAD_DIM, BQ), F32)],
            )
            dq = jnp.concatenate(dq, axis=0) * (1.0 / math.sqrt(HEAD_DIM))
            dq_s[pl.ds(begin, BQ), lanes] = dq.T.astype(BF)
        return unused

    lax.fori_loop(0, length // BQ, one_block, 0)


def block_of(scalars, slot, size):
    return pl.multiple_of(scalars[PLACE_AT + slot] * size, size)


def self_forward_body(
    scalars, x0, x1, x2, x3, gains, w0, w1, q_o, k_o, v_o, o_o, lse_o, k_s, vt_s, o_s, first_s, after_s
):
    size = x0.shape[0]
    length = q_o.shape[0]
    width = w0.shape[1] // 3
    gain = gains[0:1, :]
    k_s[pl.ds(length, ALIGN), :] = jnp.zeros((ALIGN, k_s.shape[1]), BF)
    vt_s[:, pl.ds(length, ALIGN)] = jnp.zeros((vt_s.shape[0], ALIGN), BF)
    for slot, x in enumerate((x0, x1, x2, x3)):
        place = block_of(scalars, slot, size)
        normal, unused = normalize(x[...].astype(F32))
        normed = (normal * gain).astype(BF)
        for half, w in enumerate((w0, w1)):
            lanes = slice(half * width, (half + 1) * width)
            packed = dot(normed, w[...]).astype(BF)
            q_o[pl.ds(place, size), lanes] = packed[:, :width]
            k_s[pl.ds(place, size), lanes] = packed[:, width : 2 * width]
            v_o[pl.ds(place, size), lanes] = packed[:, 2 * width :]
            vt_s[lanes, pl.ds(place, size)] = packed[:, 2 * width :].T
    k_o[...] = k_s[pl.ds(0, length), :]
    attend_forward(scalars, QUERY_AT, q_o, k_s, vt_s, o_s, lse_o, first_s, after_s)
    for slot in range(4):
        place = block_of(scalars, slot, size)
        o_o[slot] = o_s[pl.ds(place, size), :]


def cross_forward_body(
    scalars, cq0, cq1, m0, m1, m2, m3, w0, w1, k_o, v_o, o_o, lse_o, q_s, k_s, vt_s, o_s, first_s, after_s
):
    size = m0.shape[0]
    length = q_s.shape[0]
    width = w0.shape[1] // 2
    k_s[pl.ds(length, ALIGN), :] = jnp.zeros((ALIGN, k_s.shape[1]), BF)
    vt_s[:, pl.ds(length, ALIGN)] = jnp.zeros((vt_s.shape[0], ALIGN), BF)
    for slot, memory in enumerate((m0, m1, m2, m3)):
        place = block_of(scalars, slot, size)
        for half, w in enumerate((w0, w1)):
            lanes = slice(half * width, (half + 1) * width)
            packed = dot(memory[...], w[...]).astype(BF)
            k_s[pl.ds(place, size), lanes] = packed[:, :width]
            v_o[pl.ds(place, size), lanes] = packed[:, width:]
            vt_s[lanes, pl.ds(place, size)] = packed[:, width:].T
        source = cq0 if slot < 2 else cq1
        q_s[pl.ds(place, size), :] = source[pl.ds((slot % 2) * size, size), :]
    k_o[...] = k_s[pl.ds(0, length), :]
    attend_forward(scalars, KEY_AT, q_s, k_s, vt_s, o_s, lse_o, first_s, after_s)
    for slot in range(4):
        place = block_of(scalars, slot, size)
        o_o[slot] = o_s[pl.ds(place, size), :]


def load_padded(length, k, v, k_s, v_s, kt_s):
    k_s[pl.ds(0, length), :] = k[...]
    k_s[pl.ds(length, ALIGN), :] = jnp.zeros((ALIGN, k_s.shape[1]), BF)
    v_s[pl.ds(0, length), :] = v[...]
    v_s[pl.ds(length, ALIGN), :] = jnp.zeros((ALIGN, v_s.shape[1]), BF)
    kt_s[:, pl.ds(length, ALIGN)] = jnp.zeros((kt_s.shape[0], ALIGN), BF)
    for begin in range(0, length, 512):
        kt_s[:, begin : begin + 512] = k[begin : begin + 512, :].T


def cross_backward_body(
    scalars, cq0, cq1, k, v, o, lse, da0, da1, dq_o, dk_o, dv_o,
    q_s, k_s, kt_s, v_s, o_s, do_s, dq_s, dk_s, dv_s, first_s, after_s,
):
    size = o.shape[1]
    length = k.shape[0]
    load_padded(length, k, v, k_s, v_s, kt_s)
    for slot in range(4):
        place = block_of(scalars, slot, size)
        within = pl.ds((slot % 2) * size, size)
        q_s[pl.ds(place, size), :] = (cq0 if slot < 2 else cq1)[within, :]
        do_s[pl.ds(place, size), :] = (da0 if slot < 2 else da1)[within, :]
        o_s[pl.ds(place, size), :] = o[slot]
    attend_backward(
        scalars, KEY_AT, q_s, k_s, kt_s, v_s, o_s, do_s, lse, dq_s, dk_s, dv_s, first_s, after_s
    )
    for slot in range(4):
        place = block_of(scalars, slot, size)
        dq_o[slot] = dq_s[pl.ds(place, size), :]
    dk_o[...] = (dk_s[pl.ds(0, length), :] * (1.0 / math.sqrt(HEAD_DIM))).astype(BF)
    dv_o[...] = dv_s[pl.ds(0, length), :].astype(BF)


def self_backward_body(
    scalars, q, k, v, o, lse, da0, da1, w0, w1, dqkv_o, dn_o,
    k_s, kt_s, v_s, o_s, do_s, dq_s, dk_s, dv_s, first_s, after_s,
):
    size = o.shape[1]
    length = k.shape[0]
    width = w0.shape[1] // 3
    load_padded(length, k, v, k_s, v_s, kt_s)
    for slot in range(4):
        place = block_of(scalars, slot, size)
        within = pl.ds((slot % 2) * size, size)
        do_s[pl.ds(place, size), :] = (da0 if slot < 2 else da1)[within, :]
        o_s[pl.ds(place, size), :] = o[slot]
    attend_backward(
        scalars, QUERY_AT, q, k_s, kt_s, v_s, o_s, do_s, lse, dq_s, dk_s, dv_s, first_s, after_s
    )
    for slot in range(4):
        place = block_of(scalars, slot, size)
        total = jnp.zeros((size, w0.shape[0]), F32)
        for half, w in enumerate((w0, w1)):
            lanes = slice(half * width, (half + 1) * width)
            part = jnp.concatenate(
                [
                    dq_s[pl.ds(place, size), lanes],
                    (dk_s[pl.ds(place, size), lanes] * (1.0 / math.sqrt(HEAD_DIM))).astype(BF),
                    dv_s[pl.ds(place, size), lanes].astype(BF),
                ],
                axis=1,
            )
            dqkv_o[half, slot] = part
            total += dot_nt(part, w[...])
        dn_o[slot] = total.astype(BF)


def after_self_body(x0, x1, a0, a1, w0, w1, w2, w3, u0, u1, u2, u3, gains, h_o, cq0_o, cq1_o):
    size = x0.shape[0]
    for slot, x in enumerate((x0, x1)):
        here = pl.ds(slot * size, size)
        hidden = x[...].astype(F32)
        mine, other = a0[slot], a1[slot]
        width = w0.shape[0]
        hidden += dot(mine[:, :width], w0[...]) + dot(mine[:, width:], w1[...])
        hidden += dot(other[:, :width], w2[...]) + dot(other[:, width:], w3[...])
        h_o[here, :] = hidden
        normal, unused = normalize(hidden)
        normed = (normal * gains[1:2, :]).astype(BF)
        cq0_o[here, :] = jnp.concatenate([dot(normed, u0[...]), dot(normed, u1[...])], axis=1).astype(BF)
        cq1_o[here, :] = jnp.concatenate([dot(normed, u2[...]), dot(normed, u3[...])], axis=1).astype(BF)


GELU_C = math.sqrt(2.0 / math.pi)


def middle_body(
    scalars, h, a0, a1, w0, w1, w2, w3, up0, up1, up2, up3, dn0, dn1, dn2, dn3, gains, cot0, cot1,
    y_o, dh_o, da0_o, da1_o, grads_o, gain_o,
    h_s, n_s, g_s, acc_s, dn_s,
):
    size = cot0.shape[0]
    used = scalars[QUERY_AT + DOCS]
    heads = (w0, w1, w2, w3)
    width = w0.shape[0]
    units = up0.shape[1]
    for slot, cot in enumerate((cot0, cot1)):
        here = pl.ds(slot * size, size)
        mine, other = a0[slot], a1[slot]
        hidden = h[here, :] + dot(mine[:, :width], w0[...]) + dot(mine[:, width:], w1[...])
        hidden += dot(other[:, :width], w2[...]) + dot(other[:, width:], w3[...])
        h_s[here, :] = hidden
        normal, unused = normalize(hidden)
        n_s[here, :] = (normal * gains[2:3, :]).astype(BF)
        place = lax.broadcasted_iota(jnp.int32, (size, 1), 0) + scalars[PLACE_AT + slot] * size
        g_s[here, :] = jnp.where(place < used, cot[...].astype(F32), 0.0).astype(BF)
    acc_s[...] = jnp.zeros_like(acc_s)
    dn_s[...] = jnp.zeros_like(dn_s)
    for shard, (up, down) in enumerate(((up0, dn0), (up1, dn1), (up2, dn2), (up3, dn3))):
        w_up = up[...]
        w_down = down[...]
        grad_up = jnp.zeros(w_up.shape, F32)
        grad_down = jnp.zeros(w_down.shape, F32)
        for begin in range(0, 2 * size, size):
            here = pl.ds(begin, size)
            normed = n_s[here, :]
            grad = g_s[here, :]
            upper = dot(normed, w_up)
            square = upper * upper
            inner_arg = GELU_C * upper * (1.0 + 0.044715 * square)
            bent = jnp.tanh(inner_arg)
            half = 0.5 * (1.0 + bent)
            inner = (upper * half).astype(BF)
            slope = half + 0.5 * upper * (1.0 - bent * bent) * (GELU_C * (1.0 + 3.0 * 0.044715 * square))
            acc_s[here, :] += dot(inner, w_down)
            d_upper = (dot_nt(grad, w_down) * slope).astype(BF)
            dn_s[here, :] += dot_nt(d_upper, w_up)
            grad_up += dot_tn(normed, d_upper)
            grad_down += dot_tn(inner, grad)
        grads_o[shard, 0:units, :] = grad_up.astype(BF)
        grads_o[shard, units : 2 * units, :] = grad_down.astype(BF)
    gain_total = jnp.zeros((1, h_s.shape[1]), F32)
    grad_heads = [jnp.zeros((width, h_s.shape[1]), F32) for unused in range(4)]
    for slot, cot in enumerate((cot0, cot1)):
        here = pl.ds(slot * size, size)
        hidden = h_s[here, :]
        y_o[slot] = (hidden + acc_s[here, :]).astype(BF)
        normal, inv_sigma = normalize(hidden)
        dn = dn_s[here, :]
        gain_total += jnp.sum(dn * normal, axis=0, keepdims=True)
        dh = g_s[here, :].astype(F32) + normalize_back(dn, gains[2:3, :], normal, inv_sigma)
        dh_o[here, :] = dh
        low = dh.astype(BF)
        da0_o[here, :] = jnp.concatenate([dot_nt(low, w0[...]), dot_nt(low, w1[...])], axis=1).astype(BF)
        da1_o[here, :] = jnp.concatenate([dot_nt(low, w2[...]), dot_nt(low, w3[...])], axis=1).astype(BF)
        mine, other = a0[slot], a1[slot]
        parts = (mine[:, :width], mine[:, width:], other[:, :width], other[:, width:])
        grad_heads = [total + dot_tn(part, low) for total, part in zip(grad_heads, parts)]
    for shard in range(4):
        grads_o[shard, 2 * units : 2 * units + width, :] = grad_heads[shard].astype(BF)
    gain_o[...] = jnp.broadcast_to(gain_total, gain_o.shape)


def between_body(
    h, dh2, a0, a1, dq0, dq1, w0, w1, w2, w3, u0, u1, u2, u3, gains,
    dh_o, da0_o, da1_o, grads_o, gain_o,
):
    size = a0.shape[1]
    width = w0.shape[0]
    wide = h.shape[1]
    gain_total = jnp.zeros((1, wide), F32)
    grad_out = [jnp.zeros((width, wide), F32) for unused in range(4)]
    grad_query = [jnp.zeros((wide, width), F32) for unused in range(4)]
    for slot in range(2):
        here = pl.ds(slot * size, size)
        normal, inv_sigma = normalize(h[here, :])
        normed = (normal * gains[1:2, :]).astype(BF)
        mine, other = dq0[slot], dq1[slot]
        pieces = (mine[:, :width], mine[:, width:], other[:, :width], other[:, width:])
        dn = jnp.zeros((size, wide), F32)
        for piece, u in zip(pieces, (u0, u1, u2, u3)):
            dn += dot_nt(piece, u[...])
        grad_query = [total + dot_tn(normed, piece) for total, piece in zip(grad_query, pieces)]
        gain_total += jnp.sum(dn * normal, axis=0, keepdims=True)
        dh = dh2[here, :] + normalize_back(dn, gains[1:2, :], normal, inv_sigma)
        dh_o[here, :] = dh
        low = dh.astype(BF)
        da0_o[here, :] = jnp.concatenate([dot_nt(low, w0[...]), dot_nt(low, w1[...])], axis=1).astype(BF)
        da1_o[here, :] = jnp.concatenate([dot_nt(low, w2[...]), dot_nt(low, w3[...])], axis=1).astype(BF)
        mine, other = a0[slot], a1[slot]
        parts = (mine[:, :width], mine[:, width:], other[:, :width], other[:, width:])
        grad_out = [total + dot_tn(part, low) for total, part in zip(grad_out, parts)]
    for shard in range(4):
        grads_o[shard, 0:wide, :] = grad_query[shard].astype(BF)
        for part in range(wide // width):
            grads_o[shard, wide + part * width : wide + (part + 1) * width, :] = grad_out[shard][
                :, part * width : (part + 1) * width
            ].astype(BF)
    gain_o[...] = jnp.broadcast_to(gain_total, gain_o.shape)


def memory_back_body(scalars, dk, dv, m0, m1, m2, m3, w0, w1, dm_o, grads_o):
    size = m0.shape[0]
    width = w0.shape[1] // 2
    wide = m0.shape[1]
    totals = [jnp.zeros((wide, 2 * width), F32) for unused in range(2)]
    for slot, memory in enumerate((m0, m1, m2, m3)):
        place = block_of(scalars, slot, size)
        total = jnp.zeros((size, wide), F32)
        for half, w in enumerate((w0, w1)):
            lanes = slice(half * width, (half + 1) * width)
            part = jnp.concatenate([dk[pl.ds(place, size), lanes], dv[pl.ds(place, size), lanes]], axis=1)
            total += dot_nt(part, w[...])
            totals[half] += dot_tn(memory[...], part)
        dm_o[slot] = total.astype(BF)
    for half in range(2):
        grads_o[half, 0:wide, :] = totals[half][:, :width].astype(BF)
        grads_o[half, wide : 2 * wide, :] = totals[half][:, width:].astype(BF)


def qkv_grad_body(dqkv, dn, x0, x1, x2, x3, gains, grads_o, gain_o):
    width = dqkv.shape[3] // 3
    wide = x0.shape[1]
    totals = [jnp.zeros((wide, 3 * width), F32) for unused in range(2)]
    gain_total = jnp.zeros((1, wide), F32)
    for slot, x in enumerate((x0, x1, x2, x3)):
        normal, unused = normalize(x[...].astype(F32))
        normed = (normal * gains[0:1, :]).astype(BF)
        gain_total += jnp.sum(dn[slot].astype(F32) * normal, axis=0, keepdims=True)
        for half in range(2):
            totals[half] += dot_tn(normed, dqkv[half, slot])
    for half in range(2):
        for part in range(3):
            grads_o[half, part * wide : (part + 1) * wide, :] = totals[half][
                :, part * width : (part + 1) * width
            ].astype(BF)
    gain_o[...] = jnp.broadcast_to(gain_total, gain_o.shape)


def input_grad_body(dn0, dn1, x0, x1, dh, gains, g_o):
    size = x0.shape[0]
    for slot, x in enumerate((x0, x1)):
        here = pl.ds(slot * size, size)
        normal, inv_sigma = normalize(x[...].astype(F32))
        dn = dn0[slot].astype(F32) + dn1[slot].astype(F32)
        g_o[slot] = (dh[here, :] + normalize_back(dn, gains[0:1, :], normal, inv_sigma)).astype(BF)


def pick_body(order, source, out):
    out[...] = source[...]


def pick(array, order):
    count = array.shape[0]
    rest = array.shape[1:]
    return pl.pallas_call(
        pick_body,
        out_shape=struct(array.shape, array.dtype),
        grid_spec=pltpu.PrefetchScalarGridSpec(
            num_scalar_prefetch=1,
            grid=(count,),
            in_specs=[pl.BlockSpec((1,) + rest, lambda i, order: (order[i], 0, 0))],
            out_specs=pl.BlockSpec((1,) + rest, lambda i, order: (i, 0, 0)),
        ),
        name="pick",
    )(order, array)


def permute_rows(block, order):
    count = order.shape[0]
    spread = lax.all_to_all(block, "dp", split_axis=0, concat_axis=0, tiled=True)
    picked = pick(spread.reshape(count, -1, block.shape[1]), order)
    return lax.all_to_all(
        picked.reshape(block.shape), "dp", split_axis=0, concat_axis=0, tiled=True
    )


def swap_chip(array):
    return lax.ppermute(array, "tensor", [(i, i ^ 2) for i in range(4)])


def swap_core(array):
    return lax.ppermute(array, "tensor", [(i, i ^ 1) for i in range(4)])


def sum_over_rows(array):
    count = lax.axis_size("dp")
    me = lax.axis_index("dp")
    part = array
    bits = []
    bit = 1
    while bit < count:
        bits.append(bit)
        bit *= 2
    for bit in bits:
        pairs = [(i, i ^ bit) for i in range(count)]
        half = part.shape[0] // 2
        upper = (me & bit) != 0
        keep = jnp.where(upper, part[half:], part[:half])
        give = jnp.where(upper, part[:half], part[half:])
        got = lax.ppermute(give.astype(BF), "dp", pairs)
        part = keep + got.astype(F32)
    part = part.astype(BF)
    for bit in reversed(bits):
        pairs = [(i, i ^ bit) for i in range(count)]
        upper = (me & bit) != 0
        got = lax.ppermute(part, "dp", pairs)
        part = jnp.concatenate([jnp.where(upper, got, part), jnp.where(upper, part, got)], axis=0)
    return part


def on_device(
    x_first,
    x_second,
    memory,
    cot_first,
    cot_second,
    seg_ids,
    lengths,
    perm,
    inverse,
    gains,
    w_self_qkv,
    w_self_out,
    w_cross_q,
    w_cross_kv,
    w_cross_out,
    w_up,
    w_down,
):
    length = seg_ids.shape[2]
    size = x_first.shape[1]
    wide = x_first.shape[2]
    width = w_self_out.shape[0]
    units = w_up.shape[1]
    mine = 2 * size
    heads = 2 * width
    me = lax.axis_index("tensor")
    row = lax.axis_index("dp")
    rows = perm.shape[0]
    first_step = me < 2

    def both(one, two):
        return jnp.where(first_step, one, two)

    x_first, x_second, memory = x_first[0], x_second[0], memory[0]
    cot_first, cot_second = cot_first[0], cot_second[0]
    x_own = both(x_first, x_second)
    x_got = swap_chip(both(x_second, x_first))
    wqkv_own = w_self_qkv.reshape(wide, -1)
    wqkv_got = swap_chip(wqkv_own)
    place = jnp.arange(length, dtype=jnp.int32)
    meta = jnp.where(place[None, :] < lengths[0][:, None], seg_ids[0], DOCS)
    docs = jnp.arange(DOCS + 2, dtype=jnp.int32)
    cuts = jnp.sum((meta[:, None, :] < docs[None, :, None]).astype(jnp.int32), axis=-1)
    packed = jnp.pad(cuts.reshape(1, -1), ((0, 0), (0, 128 - 2 * (DOCS + 2))))
    everyone = lax.all_to_all(
        jnp.broadcast_to(packed, (rows, 128)), "dp", split_axis=0, concat_axis=0, tiled=True
    )
    theirs = lax.dynamic_slice(everyone, (perm[row], 0), (1, 2 * (DOCS + 2)))[0]
    cuts = both(theirs, cuts.reshape(-1))
    places = jnp.stack([me, me ^ 2, me ^ 1, me ^ 3]).astype(jnp.int32)
    scalars = jnp.concatenate([cuts, places])

    memory_one = permute_rows(memory, perm)
    x_sib0, x_sib1 = swap_core(x_own), swap_core(x_got)

    def four(own):
        got = swap_chip(own)
        return own, got, swap_core(own), swap_core(got)

    q, k, v, a, lse = call(
        self_forward_body,
        (
            struct((length, heads), BF),
            struct((length, heads), BF),
            struct((length, heads), BF),
            struct((4, size, heads), BF),
            struct((heads // HEAD_DIM, length), F32),
        ),
        [
            pltpu.VMEM((length + ALIGN, heads), BF),
            pltpu.VMEM((heads, length + ALIGN), BF),
            pltpu.VMEM((length, heads), BF),
            pltpu.VMEM((1, length), jnp.int32),
            pltpu.VMEM((1, length), jnp.int32),
        ],
        "self_forward",
        27,
    )(
        scalars, x_own, x_got, x_sib0, x_sib1, gains, wqkv_own, wqkv_got, specs=[SMEM] + [VM] * 7
    )
    wso = four(w_self_out)
    wcq = four(w_cross_q)
    a_mine, a_got = a[:2], swap_core(a[2:])
    h1, cq_mine, cq_send = call(
        after_self_body,
        (struct((mine, wide), F32), struct((mine, heads), BF), struct((mine, heads), BF)),
        [],
        "after_self",
        6,
    )(x_own, x_got, a_mine, a_got, *wso, *wcq, gains, specs=[VM] * 13)
    cq_got = swap_core(cq_send)

    m_own = both(memory_one, memory)
    m_got = swap_chip(both(memory, memory_one))
    m_sib0, m_sib1 = swap_core(m_own), swap_core(m_got)
    wkv_own = w_cross_kv.reshape(wide, -1)
    wkv_got = swap_chip(wkv_own)
    ck, cv, b, lse_b = call(
        cross_forward_body,
        (
            struct((length, heads), BF),
            struct((length, heads), BF),
            struct((4, size, heads), BF),
            struct((heads // HEAD_DIM, length), F32),
        ),
        [
            pltpu.VMEM((length, heads), BF),
            pltpu.VMEM((length + ALIGN, heads), BF),
            pltpu.VMEM((heads, length + ALIGN), BF),
            pltpu.VMEM((length, heads), BF),
            pltpu.VMEM((1, length), jnp.int32),
            pltpu.VMEM((1, length), jnp.int32),
        ],
        "cross_forward",
        24,
    )(
        scalars,
        cq_mine,
        cq_got,
        m_own,
        m_got,
        m_sib0,
        m_sib1,
        wkv_own,
        wkv_got,
        specs=[SMEM] + [VM] * 8,
    )
    wco = four(w_cross_out)
    wup = four(w_up)
    wdn = four(w_down)
    cot_own = both(cot_first, cot_second)
    cot_got = swap_chip(both(cot_second, cot_first))
    b_mine, b_got = b[:2], swap_core(b[2:])
    y, dh2, db_mine, db_send, grads_one, gain_three = call(
        middle_body,
        (
            struct((2, size, wide), BF),
            struct((mine, wide), F32),
            struct((mine, heads), BF),
            struct((mine, heads), BF),
            struct((4, 2 * units + width, wide), BF),
            struct((8, wide), F32),
        ),
        [
            pltpu.VMEM((mine, wide), F32),
            pltpu.VMEM((mine, wide), BF),
            pltpu.VMEM((mine, wide), BF),
            pltpu.VMEM((mine, wide), F32),
            pltpu.VMEM((mine, wide), F32),
        ],
        "middle",
        25,
    )(
        scalars,
        h1,
        b_mine,
        b_got,
        *wco,
        *wup,
        *wdn,
        gains,
        cot_own,
        cot_got,
        specs=[SMEM] + [VM] * 18,
    )
    db_got = swap_core(db_send)
    padded = [
        pltpu.VMEM((length + ALIGN, heads), BF),
        pltpu.VMEM((heads, length + ALIGN), BF),
        pltpu.VMEM((length + ALIGN, heads), BF),
        pltpu.VMEM((length, heads), BF),
        pltpu.VMEM((length, heads), BF),
        pltpu.VMEM((length, heads), BF),
        pltpu.VMEM((length + ALIGN, heads), F32),
        pltpu.VMEM((length + ALIGN, heads), F32),
        pltpu.VMEM((1, length), jnp.int32),
        pltpu.VMEM((1, length), jnp.int32),
    ]
    dcq, dck, dcv = call(
        cross_backward_body,
        (
            struct((4, size, heads), BF),
            struct((length, heads), BF),
            struct((length, heads), BF),
        ),
        [pltpu.VMEM((length, heads), BF)] + padded,
        "cross_backward",
        29,
    )(
        scalars, cq_mine, cq_got, ck, cv, b, lse_b, db_mine, db_got, specs=[SMEM] + [VM] * 8
    )
    dcq_mine, dcq_got = dcq[:2], swap_core(dcq[2:])
    dh1, da_mine, da_send, grads_two, gain_two = call(
        between_body,
        (
            struct((mine, wide), F32),
            struct((mine, heads), BF),
            struct((mine, heads), BF),
            struct((4, 2 * wide, width), BF),
            struct((8, wide), F32),
        ),
        [],
        "between",
        8,
    )(
        h1, dh2, a_mine, a_got, dcq_mine, dcq_got, *wso, *wcq, gains, specs=[VM] * 15
    )
    da_got = swap_core(da_send)
    dm, grads_kv = call(
        memory_back_body,
        (struct((4, size, wide), BF), struct((2, 2 * wide, width), BF)),
        [],
        "memory_back",
        6,
    )(
        scalars, dck, dcv, m_own, m_got, m_sib0, m_sib1, wkv_own, wkv_got, specs=[SMEM] + [VM] * 8
    )
    dqkv, dn = call(
        self_backward_body,
        (struct((2, 4, size, 3 * width), BF), struct((4, size, wide), BF)),
        padded,
        "self_backward",
        33,
    )(
        scalars, q, k, v, a, lse, da_mine, da_got, wqkv_own, wqkv_got, specs=[SMEM] + [VM] * 9
    )
    dn_got = swap_core(dn[2:])
    grads_qkv, gain_one = call(
        qkv_grad_body,
        (struct((2, 3 * wide, width), BF), struct((8, wide), F32)),
        [],
        "qkv_grad",
        7,
    )(dqkv, dn, x_own, x_got, x_sib0, x_sib1, gains, specs=[VM] * 7)
    grad_in = call(
        input_grad_body, struct((2, size, wide), BF), [], "input_grad", 5
    )(dn[:2], dn_got, x_own, x_got, dh1, gains, specs=[VM] * 6)

    y_got = swap_chip(y[1])
    y_first = both(y[0], y_got)
    y_second = both(y_got, y[0])
    grad_got = swap_chip(grad_in[1])
    grad_first = both(grad_in[0], grad_got)
    dm_sum = (dm[:2].astype(F32) + swap_core(dm[2:]).astype(F32)).astype(BF)
    dm_got = swap_chip(dm_sum[1])
    dm_one = both(dm_sum[0], dm_got)
    dm_two = both(dm_got, dm_sum[0])
    grad_memory = dm_two.astype(F32) + permute_rows(dm_one, inverse).astype(F32)

    def over_chip(own_two):
        return own_two[0].astype(F32) + swap_chip(own_two[1]).astype(F32)

    def over_core(four_parts):
        got = swap_core(four_parts[2:])
        return (four_parts[:2].astype(F32) + got.astype(F32)).astype(BF)

    total_one = sum_over_rows(over_chip(over_core(grads_one)))
    total_two = sum_over_rows(
        over_chip(jnp.concatenate([over_core(grads_two), grads_kv], axis=1))
    )
    gain_all = jnp.stack([gain_one[0], gain_two[0], gain_three[0]])
    gain_all = jnp.pad(gain_all, ((0, 29), (0, 0)))
    gain_all = (gain_all + swap_core(gain_all)).astype(BF).reshape(-1, width)
    gain_rows = gain_all.shape[0]
    last = jnp.concatenate([grads_qkv, jnp.stack([gain_all, gain_all])], axis=1)
    total_three = sum_over_rows(over_chip(last))

    total_one = total_one.astype(F32)
    grad_up = total_one[:units]
    grad_down = total_one[units : 2 * units]
    grad_cross_out = total_one[2 * units :]
    total_two = total_two.astype(F32)
    grad_cross_q = total_two[:wide]
    grad_self_out = jnp.concatenate(
        [total_two[wide + i * width : wide + (i + 1) * width] for i in range(wide // width)], axis=1
    )
    grad_kv = jnp.stack([total_two[2 * wide : 3 * wide], total_two[3 * wide :]], axis=1)
    total_three = total_three.astype(F32)
    grad_qkv = jnp.stack([total_three[i * wide : (i + 1) * wide] for i in range(3)], axis=1)
    gain_total = total_three[3 * wide : 3 * wide + gain_rows].reshape(-1, wide)[:3]
    grad_gains = lax.dynamic_slice(gain_total, (0, me * width), (3, width))
    return (
        y_first[None],
        y_second[None],
        grad_first[None],
        grad_memory[None],
        grad_gains,
        grad_qkv,
        grad_self_out,
        grad_cross_q,
        grad_kv,
        grad_cross_out,
        grad_up,
        grad_down,
    )


def solution(mesh):
    in_specs = (
        P("dp", "tensor", None),
        P("dp", "tensor", None),
        P("dp", "tensor", None),
        P("dp", "tensor", None),
        P("dp", "tensor", None),
        P("dp", None, None),
        P("dp", None),
        P(),
        P(),
        P(),
        P(None, None, "tensor"),
        P("tensor", None),
        P(None, "tensor"),
        P(None, None, "tensor"),
        P("tensor", None),
        P(None, "tensor"),
        P("tensor", None),
    )
    out_specs = (
        P("dp", "tensor", None),
        P("dp", "tensor", None),
        P("dp", "tensor", None),
        P("dp", "tensor", None),
        P(None, "tensor"),
        P(None, None, "tensor"),
        P("tensor", None),
        P(None, "tensor"),
        P(None, None, "tensor"),
        P("tensor", None),
        P(None, "tensor"),
        P("tensor", None),
    )
    return jax.shard_map(
        on_device, mesh=mesh, in_specs=in_specs, out_specs=out_specs, check_vma=False
    )
```

```python
import functools
import math

import jax
import jax.numpy as jnp
from jax import lax
from jax.experimental import pallas as pl
from jax.experimental.pallas import tpu as pltpu
from jax.sharding import PartitionSpec as P

HEAD_DIM = 64
EPSILON = 1e-05
NEG_FILL = -1e30
DOCS = 16
PAIR = 2 * HEAD_DIM
BQ = 256
BK = 256
FORWARD_BK = 512
ALIGN = 128
BF = jnp.bfloat16
F32 = jnp.float32
VMEM_BYTES = 56 * 1024 * 1024
LOG2E = 1.4426950408889634

ANY = pl.BlockSpec(memory_space=pl.ANY)
SMEM = pl.BlockSpec(memory_space=pltpu.SMEM)
VM = pl.BlockSpec(memory_space=pltpu.VMEM)


def dot(a, b):
    return lax.dot_general(a, b, (((1,), (0,)), ((), ())), preferred_element_type=F32)


def dot_nt(a, b):
    return lax.dot_general(a, b, (((1,), (1,)), ((), ())), preferred_element_type=F32)


def dot_tn(a, b):
    return lax.dot_general(a, b, (((0,), (0,)), ((), ())), preferred_element_type=F32)


def normalize(hidden):
    centred = hidden - jnp.mean(hidden, axis=-1, keepdims=True)
    inv_sigma = lax.rsqrt(jnp.mean(centred * centred, axis=-1, keepdims=True) + EPSILON)
    return centred * inv_sigma, inv_sigma


def normalize_back(grad_scaled, gain, normal, inv_sigma):
    grad_normal = grad_scaled * gain
    first_mean = jnp.mean(grad_normal, axis=-1, keepdims=True)
    second_mean = jnp.mean(grad_normal * normal, axis=-1, keepdims=True)
    return inv_sigma * (grad_normal - first_mean - normal * second_mean)


def call(body, outs, scratch, name, cost, grid=()):
    def run(*args, specs):
        moved = sum(a.size * a.dtype.itemsize for a in args)
        return pl.pallas_call(
            body,
            out_shape=outs,
            grid=grid,
            in_specs=specs,
            out_specs=jax.tree.map(lambda _: VM, outs),
            scratch_shapes=scratch,
            compiler_params=pltpu.CompilerParams(vmem_limit_bytes=VMEM_BYTES),
            cost_estimate=pl.CostEstimate(flops=int(cost * 1.15e9), bytes_accessed=moved, transcendentals=0),
            name=name,
        )(*args)

    return run


def struct(shape, dtype):
    return jax.ShapeDtypeStruct(shape, dtype)


QUERY_AT, KEY_AT, PLACE_AT = 0, DOCS + 2, 2 * (DOCS + 2)
ROW_AT = PLACE_AT + 4


def key_limits(scalars, key_at, length):
    place = lax.broadcasted_iota(jnp.int32, (1, length), 1)
    first = jnp.full((1, length), scalars[key_at], jnp.int32)
    after = jnp.full((1, length), scalars[key_at + 1], jnp.int32)
    for doc in range(1, DOCS + 1):
        inside = place >= scalars[QUERY_AT + doc]
        first = jnp.where(inside, scalars[key_at + doc], first)
        after = jnp.where(inside, scalars[key_at + doc + 1], after)
    return first, after


def window(scalars, key_at, begin, size):
    low = scalars[key_at]
    high = scalars[key_at + 1]
    for doc in range(1, DOCS + 1):
        low = jnp.where(begin >= scalars[QUERY_AT + doc], scalars[key_at + doc], low)
        high = jnp.where(
            begin + (BQ - 1) >= scalars[QUERY_AT + doc], scalars[key_at + doc + 1], high
        )
    low = (low // ALIGN) * ALIGN
    return low, (high - low + (size - 1)) // size


def two_heads(block):
    lane = lax.broadcasted_iota(jnp.int32, block.shape, 1)
    zero = jnp.zeros_like(block)
    return jnp.concatenate(
        [jnp.where(lane < HEAD_DIM, block, zero), jnp.where(lane >= HEAD_DIM, block, zero)], axis=0
    )


def attend_forward(scalars, key_at, pairs, q_s, k_s, vt_s, o_s, lse_s, first_s, after_s):
    length = q_s.shape[1]
    scale = LOG2E / math.sqrt(HEAD_DIM)
    first, after = key_limits(scalars, key_at, length)
    first_s[...] = first
    after_s[...] = after
    rows = lax.broadcasted_iota(jnp.int32, (FORWARD_BK, BQ), 0)

    def one_block(index, unused):
        begin = pl.multiple_of(index * BQ, BQ)
        low, count = window(scalars, key_at, begin, FORWARD_BK)
        first_row = first_s[:, pl.ds(begin, BQ)]
        after_row = after_s[:, pl.ds(begin, BQ)]
        queries = [two_heads(q_s[pair, pl.ds(begin, BQ), :]) for pair in pairs]

        def step(turn, carry):
            start = pl.multiple_of(low + turn * FORWARD_BK, ALIGN)
            allowed = (rows >= first_row - start) & (rows < after_row - start)
            allowed = jnp.concatenate([allowed, allowed], axis=1)
            results = []
            for pair, query, (top, total, out) in zip(pairs, queries, carry):
                scores = dot_nt(k_s[pair, pl.ds(start, FORWARD_BK), :], query) * scale
                scores = jnp.where(allowed, scores, NEG_FILL)
                new_top = jnp.maximum(top, jnp.max(scores, axis=0, keepdims=True))
                shrink = jnp.exp2(top - new_top)
                raised = jnp.exp2(scores - new_top)
                total = total * shrink + jnp.sum(raised, axis=0, keepdims=True)
                low_probs = raised.astype(BF)
                value = vt_s[pair, :, pl.ds(start, FORWARD_BK)]
                out = [
                    out[0] * shrink[:, :BQ] + dot(value[:HEAD_DIM], low_probs[:, :BQ]),
                    out[1] * shrink[:, BQ:] + dot(value[HEAD_DIM:], low_probs[:, BQ:]),
                ]
                results.append((new_top, total, out))
            return results

        zero = jnp.zeros((HEAD_DIM, BQ), F32)
        fresh = (jnp.full((1, 2 * BQ), NEG_FILL, F32), jnp.zeros((1, 2 * BQ), F32), [zero, zero])
        results = lax.fori_loop(0, count, step, [fresh for unused_pair in pairs])
        for pair, (top, total, out) in zip(pairs, results):
            inverse = 1.0 / total
            out = jnp.concatenate([out[0] * inverse[:, :BQ], out[1] * inverse[:, BQ:]], axis=0)
            o_s[pl.ds(begin, BQ), pair * PAIR : (pair + 1) * PAIR] = out.T.astype(BF)
            log_total = top + jnp.log2(total)
            lse_s[pair, 0:1, pl.ds(begin, BQ)] = log_total[:, :BQ]
            lse_s[pair, 1:2, pl.ds(begin, BQ)] = log_total[:, BQ:]
        return unused

    lax.fori_loop(0, length // BQ, one_block, 0)


def attend_backward(
    scalars, key_at, pairs, q_s, k_s, kt_s, v_s, o_s, do_s, lse_s, dq_s, dk_s, dv_s, first_s, after_s
):
    length = q_s.shape[1]
    scale = LOG2E / math.sqrt(HEAD_DIM)
    first, after = key_limits(scalars, key_at, length)
    first_s[...] = first
    after_s[...] = after
    rows = lax.broadcasted_iota(jnp.int32, (BK, BQ), 0)
    dk_s[...] = jnp.zeros_like(dk_s)
    dv_s[...] = jnp.zeros_like(dv_s)
    ones = jnp.ones((8, PAIR), F32)

    def one_block(index, unused):
        begin = pl.multiple_of(index * BQ, BQ)
        low, count = window(scalars, key_at, begin, BK)
        first_row = first_s[:, pl.ds(begin, BQ)]
        after_row = after_s[:, pl.ds(begin, BQ)]
        fixed = []
        for pair in pairs:
            query = two_heads(q_s[pair, pl.ds(begin, BQ), :])
            grad = two_heads(do_s[pair, pl.ds(begin, BQ), :])
            out = o_s[pair, pl.ds(begin, BQ), :].astype(F32)
            product = grad.astype(F32) * jnp.concatenate([out, out], axis=0)
            centre = lax.dot_general(
                ones,
                product,
                (((1,), (1,)), ((), ())),
                precision=lax.Precision.HIGHEST,
                preferred_element_type=F32,
            )[:1]
            log_total = jnp.concatenate(
                [lse_s[pair, 0:1, pl.ds(begin, BQ)], lse_s[pair, 1:2, pl.ds(begin, BQ)]], axis=1
            )
            fixed.append((query, grad, centre, log_total))

        def step(turn, carry):
            start = pl.multiple_of(low + turn * BK, ALIGN)
            allowed = (rows >= first_row - start) & (rows < after_row - start)
            allowed = jnp.concatenate([allowed, allowed], axis=1)
            results = []
            for pair, (query, grad, centre, log_total), dq in zip(pairs, fixed, carry):
                scores = dot_nt(k_s[pair, pl.ds(start, BK), :], query) * scale
                probs = jnp.exp2(jnp.where(allowed, scores, NEG_FILL) - log_total)
                dprobs = dot_nt(v_s[pair, pl.ds(start, BK), :], grad)
                dscores = (probs * (dprobs - centre)).astype(BF)
                dv_s[pair, pl.ds(start, BK), :] += dot(probs.astype(BF), grad)
                dk_s[pair, pl.ds(start, BK), :] += dot(dscores, query)
                kt = kt_s[pair, :, pl.ds(start, BK)]
                results.append(
                    [
                        dq[0] + dot(kt[:HEAD_DIM], dscores[:, :BQ]),
                        dq[1] + dot(kt[HEAD_DIM:], dscores[:, BQ:]),
                    ]
                )
            return results

        zero = jnp.zeros((HEAD_DIM, BQ), F32)
        results = lax.fori_loop(0, count, step, [[zero, zero] for unused_pair in pairs])
        for pair, dq in zip(pairs, results):
            dq = jnp.concatenate(dq, axis=0) * (1.0 / math.sqrt(HEAD_DIM))
            dq_s[pair, pl.ds(begin, BQ), :] = dq.T.astype(BF)
        return unused

    lax.fori_loop(0, length // BQ, one_block, 0)


def block_of(scalars, slot, size):
    return pl.multiple_of(scalars[PLACE_AT + slot] * size, size)


def clear_padding(length, k_s, t_s, v_s=None):
    pairs, padded = k_s.shape[:2]
    extra = padded - length
    k_s[:, pl.ds(length, extra), :] = jnp.zeros((pairs, extra, PAIR), BF)
    t_s[:, :, pl.ds(length, extra)] = jnp.zeros((pairs, PAIR, extra), BF)
    if v_s is not None:
        v_s[:, pl.ds(length, extra), :] = jnp.zeros((pairs, extra, PAIR), BF)


def hand_out(scalars, o_s, mine_o, send_o):
    size = mine_o.shape[1]
    for slot in range(4):
        place = block_of(scalars, slot, size)
        (mine_o if slot < 2 else send_o)[slot % 2] = o_s[pl.ds(place, size), :]


def self_forward_body(
    scalars, x0, x1, x2, x3, gains, w0, w1, q_o, k_o, v_o, mine_o, send_o, lse_o, k_s, vt_s, o_s, first_s, after_s
):
    size = x0.shape[0]
    length = q_o.shape[1]
    gain = gains[0:1, :]
    clear_padding(length, k_s, vt_s)
    for slot, x in enumerate((x0, x1, x2, x3)):
        place = block_of(scalars, slot, size)
        normal, unused = normalize(x[...].astype(F32))
        normed = (normal * gain).astype(BF)
        for pair, w in enumerate((w0, w1)):
            packed = dot(normed, w[...]).astype(BF)
            keys, values = packed[:, PAIR : 2 * PAIR], packed[:, 2 * PAIR :]
            q_o[pair, pl.ds(place, size), :] = packed[:, :PAIR]
            k_s[pair, pl.ds(place, size), :] = keys
            k_o[pair, pl.ds(place, size), :] = keys
            v_o[pair, pl.ds(place, size), :] = values
            vt_s[pair, :, pl.ds(place, size)] = values.T
    attend_forward(scalars, QUERY_AT, (0, 1), q_o, k_s, vt_s, o_s, lse_o, first_s, after_s)
    hand_out(scalars, o_s, mine_o, send_o)


def cross_forward_body(
    scalars, cq0, cq1, m0, m1, m2, m3, w0, w1, q_o, k_o, v_o, mine_o, send_o, lse_o, k_s, vt_s, o_s, first_s, after_s
):
    size = m0.shape[0]
    length = q_o.shape[1]
    clear_padding(length, k_s, vt_s)
    for slot, memory in enumerate((m0, m1, m2, m3)):
        place = block_of(scalars, slot, size)
        source = cq0 if slot < 2 else cq1
        for pair, w in enumerate((w0, w1)):
            packed = dot(memory[...], wide_rows(w, 0, memory.shape[1], 2)).astype(BF)
            keys, values = packed[:, :PAIR], packed[:, PAIR:]
            k_s[pair, pl.ds(place, size), :] = keys
            k_o[pair, pl.ds(place, size), :] = keys
            v_o[pair, pl.ds(place, size), :] = values
            vt_s[pair, :, pl.ds(place, size)] = values.T
            q_o[pair, pl.ds(place, size), :] = source[
                pl.ds((slot % 2) * size, size), pair * PAIR : (pair + 1) * PAIR
            ]
    attend_forward(scalars, KEY_AT, (0, 1), q_o, k_s, vt_s, o_s, lse_o, first_s, after_s)
    hand_out(scalars, o_s, mine_o, send_o)


def load_backward(scalars, pairs, k, v, a0, a1, da0, da1, k_s, kt_s, v_s, o_s, do_s):
    size = a0.shape[1]
    length = k.shape[1]
    clear_padding(length, k_s, kt_s, v_s)
    for pair in range(pairs):
        k_s[pair, pl.ds(0, length), :] = k[pair]
        v_s[pair, pl.ds(0, length), :] = v[pair]
        lanes = slice(pair * PAIR, (pair + 1) * PAIR)
        for begin in range(0, length, 512):
            kt_s[pair, :, begin : begin + 512] = k[pair, begin : begin + 512, :].T
        for slot in range(4):
            place = block_of(scalars, slot, size)
            within = pl.ds((slot % 2) * size, size)
            do_s[pair, pl.ds(place, size), :] = (da0 if slot < 2 else da1)[within, lanes]
            o_s[pair, pl.ds(place, size), :] = (a0 if slot < 2 else a1)[slot % 2, :, lanes]


def cross_backward_body(
    scalars, q, k, v, a0, a1, lse, da0, da1, mine_o, send_o, dk_o, dv_o,
    k_s, kt_s, v_s, o_s, do_s, dq_s, dk_s, dv_s, first_s, after_s,
):
    size = a0.shape[1]
    length = k.shape[1]
    load_backward(scalars, 2, k, v, a0, a1, da0, da1, k_s, kt_s, v_s, o_s, do_s)
    attend_backward(
        scalars, KEY_AT, (0, 1), q, k_s, kt_s, v_s, o_s, do_s, lse, dq_s, dk_s, dv_s, first_s, after_s
    )
    for slot in range(4):
        place = block_of(scalars, slot, size)
        for pair in range(2):
            (mine_o if slot < 2 else send_o)[slot % 2, :, pair * PAIR : (pair + 1) * PAIR] = dq_s[
                pair, pl.ds(place, size), :
            ]
    dk_o[...] = (dk_s[:, pl.ds(0, length), :] * (1.0 / math.sqrt(HEAD_DIM))).astype(BF)
    dv_o[...] = dv_s[:, pl.ds(0, length), :].astype(BF)


def self_backward_body(
    scalars, q, k, v, a0, a1, lse, da0, da1, dqkv_o,
    k_s, kt_s, v_s, o_s, do_s, dq_s, dk_s, dv_s, first_s, after_s,
):
    size = a0.shape[1]
    load_backward(scalars, 1, k, v, a0, a1, da0, da1, k_s, kt_s, v_s, o_s, do_s)
    attend_backward(
        scalars, QUERY_AT, (0,), q, k_s, kt_s, v_s, o_s, do_s, lse, dq_s, dk_s, dv_s, first_s, after_s
    )
    for slot in range(4):
        place = block_of(scalars, slot, size)
        dqkv_o[slot, :, 0:PAIR] = dq_s[0, pl.ds(place, size), :]
        dqkv_o[slot, :, PAIR : 2 * PAIR] = (
            dk_s[0, pl.ds(place, size), :] * (1.0 / math.sqrt(HEAD_DIM))
        ).astype(BF)
        dqkv_o[slot, :, 2 * PAIR :] = dv_s[0, pl.ds(place, size), :].astype(BF)


def wide_rows(ref, begin, rows, count):
    return jnp.concatenate(
        [ref[begin + i * rows : begin + (i + 1) * rows, :] for i in range(count)], axis=1
    )


def after_self_body(x0, x1, a0, a1, p0, p1, p2, p3, gains, h_o, cq0_o, cq1_o):
    size, wide = x0.shape
    packs = (p0, p1, p2, p3)
    w0, w1, w2, w3 = [wide_rows(p, 0, PAIR, wide // PAIR) for p in packs]
    u0, u1, u2, u3 = [p[wide : 2 * wide, :] for p in packs]
    for slot, x in enumerate((x0, x1)):
        here = pl.ds(slot * size, size)
        hidden = x[...].astype(F32)
        mine, other = a0[slot], a1[slot]
        width = w0.shape[0]
        hidden += dot(mine[:, :width], w0) + dot(mine[:, width:], w1)
        hidden += dot(other[:, :width], w2) + dot(other[:, width:], w3)
        h_o[here, :] = hidden
        normal, unused = normalize(hidden)
        normed = (normal * gains[1:2, :]).astype(BF)
        cq0_o[here, :] = jnp.concatenate([dot(normed, u0), dot(normed, u1)], axis=1).astype(BF)
        cq1_o[here, :] = jnp.concatenate([dot(normed, u2), dot(normed, u3)], axis=1).astype(BF)


GELU_C = math.sqrt(2.0 / math.pi)


def middle_body(
    scalars, h, a0, a1, p0, p1, p2, p3, ud0, ud1, ud2, ud3, gains, cot0, cot1,
    y0_o, y1_o, dh_o, da0_o, da1_o, up_keep_o, up_give_o, keep_o, give_o, gain_o,
    h_s, n_s, g_s, acc_s, dn_s,
):
    size = cot0.shape[0]
    used = scalars[QUERY_AT + DOCS]
    wide = h.shape[1]
    width = PAIR
    units = ud0.shape[0] * PAIR // (2 * wide)
    w0, w1, w2, w3 = [wide_rows(p, 0, width, wide // PAIR) for p in (p0, p1, p2, p3)]
    for slot, cot in enumerate((cot0, cot1)):
        here = pl.ds(slot * size, size)
        mine, other = a0[slot], a1[slot]
        hidden = h[here, :] + dot(mine[:, :width], w0) + dot(mine[:, width:], w1)
        hidden += dot(other[:, :width], w2) + dot(other[:, width:], w3)
        h_s[here, :] = hidden
        normal, unused = normalize(hidden)
        n_s[here, :] = (normal * gains[2:3, :]).astype(BF)
        place = lax.broadcasted_iota(jnp.int32, (size, 1), 0) + scalars[PLACE_AT + slot] * size
        g_s[here, :] = jnp.where(place < used, cot[...].astype(F32), 0.0).astype(BF)
    acc_s[...] = jnp.zeros_like(acc_s)
    dn_s[...] = jnp.zeros_like(dn_s)
    for shard, ud in enumerate((ud0, ud1, ud2, ud3)):
        w_up = wide_rows(ud, 0, wide, units // PAIR)
        w_down = wide_rows(ud, wide * units // PAIR, units, wide // PAIR)
        grad_up = jnp.zeros(w_up.shape, F32)
        grad_down = jnp.zeros(w_down.shape, F32)
        for begin in range(0, 2 * size, size):
            here = pl.ds(begin, size)
            normed = n_s[here, :]
            grad = g_s[here, :]
            upper = dot(normed, w_up)
            square = upper * upper
            inner_arg = GELU_C * upper * (1.0 + 0.044715 * square)
            bent = jnp.tanh(inner_arg)
            half = 0.5 * (1.0 + bent)
            inner = (upper * half).astype(BF)
            slope = half + 0.5 * upper * (1.0 - bent * bent) * (GELU_C * (1.0 + 3.0 * 0.044715 * square))
            acc_s[here, :] += dot(inner, w_down)
            d_upper = (dot_nt(grad, w_down) * slope).astype(BF)
            dn_s[here, :] += dot_nt(d_upper, w_up)
            grad_up += dot_tn(normed, d_upper)
            grad_down += dot_tn(inner, grad)
        (up_keep_o if shard < 2 else up_give_o)[shard % 2] = grad_up.astype(BF)
        (keep_o if shard < 2 else give_o)[shard % 2, 0:units, :] = grad_down.astype(BF)
    gain_total = jnp.zeros((1, h_s.shape[1]), F32)
    grad_heads = [jnp.zeros((width, h_s.shape[1]), F32) for unused in range(4)]
    for slot, y_o in enumerate((y0_o, y1_o)):
        here = pl.ds(slot * size, size)
        hidden = h_s[here, :]
        y_o[...] = (hidden + acc_s[here, :]).astype(BF)
        normal, inv_sigma = normalize(hidden)
        dn = dn_s[here, :]
        gain_total += jnp.sum(dn * normal, axis=0, keepdims=True)
        dh = g_s[here, :].astype(F32) + normalize_back(dn, gains[2:3, :], normal, inv_sigma)
        dh_o[here, :] = dh
        low = dh.astype(BF)
        da0_o[here, :] = jnp.concatenate([dot_nt(low, w0), dot_nt(low, w1)], axis=1).astype(BF)
        da1_o[here, :] = jnp.concatenate([dot_nt(low, w2), dot_nt(low, w3)], axis=1).astype(BF)
        mine, other = a0[slot], a1[slot]
        parts = (mine[:, :width], mine[:, width:], other[:, :width], other[:, width:])
        grad_heads = [total + dot_tn(part, low) for total, part in zip(grad_heads, parts)]
    for shard in range(4):
        out = keep_o if shard < 2 else give_o
        out[shard % 2, units : units + width, :] = grad_heads[shard].astype(BF)
    gain_o[...] = jnp.broadcast_to(gain_total, gain_o.shape)


def between_body(
    h, dh2, a0, a1, dq0, dq1, p0, p1, p2, p3, gains,
    dh_o, da0_o, da1_o, keep_o, give_o, gain_o,
):
    size = a0.shape[1]
    width = PAIR
    wide = h.shape[1]
    packs = (p0, p1, p2, p3)
    w0, w1, w2, w3 = [wide_rows(p, 0, width, wide // PAIR) for p in packs]
    u0, u1, u2, u3 = [p[wide : 2 * wide, :] for p in packs]
    gain_total = jnp.zeros((1, wide), F32)
    grad_out = [jnp.zeros((width, wide), F32) for unused in range(4)]
    grad_query = [jnp.zeros((wide, width), F32) for unused in range(4)]
    for slot in range(2):
        here = pl.ds(slot * size, size)
        normal, inv_sigma = normalize(h[here, :])
        normed = (normal * gains[1:2, :]).astype(BF)
        mine, other = dq0[slot], dq1[slot]
        pieces = (mine[:, :width], mine[:, width:], other[:, :width], other[:, width:])
        dn = jnp.zeros((size, wide), F32)
        for piece, u in zip(pieces, (u0, u1, u2, u3)):
            dn += dot_nt(piece, u)
        grad_query = [total + dot_tn(normed, piece) for total, piece in zip(grad_query, pieces)]
        gain_total += jnp.sum(dn * normal, axis=0, keepdims=True)
        dh = dh2[here, :] + normalize_back(dn, gains[1:2, :], normal, inv_sigma)
        dh_o[here, :] = dh
        low = dh.astype(BF)
        da0_o[here, :] = jnp.concatenate([dot_nt(low, w0), dot_nt(low, w1)], axis=1).astype(BF)
        da1_o[here, :] = jnp.concatenate([dot_nt(low, w2), dot_nt(low, w3)], axis=1).astype(BF)
        mine, other = a0[slot], a1[slot]
        parts = (mine[:, :width], mine[:, width:], other[:, :width], other[:, width:])
        grad_out = [total + dot_tn(part, low) for total, part in zip(grad_out, parts)]
    for shard in range(4):
        out = keep_o if shard < 2 else give_o
        out[shard % 2, 0:wide, :] = grad_query[shard].astype(BF)
        for part in range(wide // width):
            out[shard % 2, wide + part * width : wide + (part + 1) * width, :] = grad_out[shard][
                :, part * width : (part + 1) * width
            ].astype(BF)
    gain_o[...] = jnp.broadcast_to(gain_total, gain_o.shape)


def memory_back_body(scalars, dk, dv, m0, m1, m2, m3, w0, w1, mine_o, send_o, keep_o, give_o):
    size = m0.shape[0]
    wide = m0.shape[1]
    totals = [jnp.zeros((wide, 2 * PAIR), F32) for unused in range(2)]
    for slot, memory in enumerate((m0, m1, m2, m3)):
        place = block_of(scalars, slot, size)
        total = jnp.zeros((size, wide), F32)
        for pair, w in enumerate((w0, w1)):
            part = jnp.concatenate([dk[pair, pl.ds(place, size), :], dv[pair, pl.ds(place, size), :]], axis=1)
            total += dot_nt(part, wide_rows(w, 0, memory.shape[1], 2))
            totals[pair] += dot_tn(memory[...], part)
        (mine_o if slot < 2 else send_o)[slot % 2] = total.astype(BF)
    for total, out in zip(totals, (keep_o, give_o)):
        out[0:wide, :] = total[:, :PAIR].astype(BF)
        out[wide : 2 * wide, :] = total[:, PAIR:].astype(BF)


def qkv_part(dqkv, x_refs, gains, w):
    wide = x_refs[0].shape[1]
    total = jnp.zeros((wide, 3 * PAIR), F32)
    for slot, x in enumerate(x_refs):
        normal, unused = normalize(x[...].astype(F32))
        total += dot_tn((normal * gains[0:1, :]).astype(BF), dqkv[slot])
    gain = lax.dot_general(
        jnp.ones((8, 3 * PAIR), F32),
        total * w[...].astype(F32),
        (((1,), (1,)), ((), ())),
        precision=lax.Precision.HIGHEST,
        preferred_element_type=F32,
    )
    return total, gain


def qkv_give_body(dqkv, x0, x1, x2, x3, gains, w, give_o, gain_o):
    wide = x0.shape[1]
    total, gain = qkv_part(dqkv, (x0, x1, x2, x3), gains, w)
    for part in range(3):
        give_o[part * wide : (part + 1) * wide, :] = total[:, part * PAIR : (part + 1) * PAIR].astype(BF)
    gain_o[...] = gain


def qkv_keep_body(dqkv, x0, x1, x2, x3, gains, w, got, gain_one, gain_two, gain_three, keep_o, gain_o):
    wide = x0.shape[1]
    total, gain = qkv_part(dqkv, (x0, x1, x2, x3), gains, w)
    for part in range(3):
        here = slice(part * wide, (part + 1) * wide)
        keep_o[here, :] = (total[:, part * PAIR : (part + 1) * PAIR] + got[here, :].astype(F32)).astype(BF)
    gain = (gain + gain_one[...]) / gains[0:1, :]
    gain_o[...] = jnp.concatenate(
        [gain[:1], gain_two[:1, :], gain_three[:1, :], jnp.zeros((5, wide), F32)], axis=0
    )


def back_to_input_body(dqkv0, dqkv1, w0, w1, mine_o, send_o):
    for slot in range(4):
        dn = dot_nt(dqkv0[slot], w0[...]) + dot_nt(dqkv1[slot], w1[...])
        (mine_o if slot < 2 else send_o)[slot % 2] = dn.astype(BF)


def input_grad_body(dn0, dn1, x0, x1, dh, gains, g0_o, g1_o):
    size = x0.shape[0]
    for slot, (x, g_o) in enumerate(((x0, g0_o), (x1, g1_o))):
        here = pl.ds(slot * size, size)
        normal, inv_sigma = normalize(x[...].astype(F32))
        dn = dn0[slot].astype(F32) + dn1[slot].astype(F32)
        g_o[...] = (dh[here, :] + normalize_back(dn, gains[0:1, :], normal, inv_sigma)).astype(BF)


def pick_body(order, source, out):
    def one(i, unused):
        out[i] = source[order[i]]
        return unused

    lax.fori_loop(0, source.shape[0], one, 0)


def pick(array, order):
    return call(pick_body, struct(array.shape, array.dtype), [], "pick", 1)(
        order, array, specs=[SMEM, VM]
    )


def pick_memory_body(order, source, out, digits_o):
    count, share = out.shape[:2]

    def one(i, unused):
        out[i] = source[order[i], 0:share, :]
        return unused

    lax.fori_loop(0, count, one, 0)
    digits_o[...] = source[order[order[count]], share:, :]


def spread_rows(block):
    return lax.all_to_all(block, "dp", split_axis=0, concat_axis=0, tiled=True)


def swap_chip(array):
    return lax.ppermute(array, "tensor", [(i, i ^ 2) for i in range(4)])


def swap_core(array):
    return lax.ppermute(array, "tensor", [(i, i ^ 1) for i in range(4)])


def pack_body(*refs):
    out = refs[-1]
    at = 0
    for ref in refs[:-1]:
        rows, lanes = ref.shape
        for begin in range(0, lanes, PAIR):
            out[at : at + rows, :] = ref[:, begin : begin + PAIR]
            at += rows


def pack(*arrays):
    rows = sum(a.size for a in arrays) // PAIR
    return call(pack_body, struct((rows, PAIR), arrays[0].dtype), [], "pack", 1)(
        *arrays, specs=[VM] * len(arrays)
    )


def swap_row(array, bit):
    return lax.ppermute(array, "dp", [(i, i ^ bit) for i in range(lax.axis_size("dp"))])


def halves(array, upper):
    half = array.shape[0] // 2
    low, high = array[:half], array[half:]
    return jnp.where(upper, high, low), jnp.where(upper, low, high).astype(BF)


def rest_groups():
    count = lax.axis_size("dp")
    return [[i for i in range(count) if i % 2 == part] for part in range(2)]


def rest_sends(arrays):
    group = lax.axis_size("dp") // 2
    width = arrays[0].shape[1]
    joint = jnp.concatenate([a.reshape(group, -1, width) for a in arrays], axis=1)
    me = lax.axis_index("dp") // 2

    def piece(index):
        return lax.dynamic_index_in_dim(joint, index, 0, keepdims=False)

    if group != 4:
        return piece(me), [joint.reshape(-1, width)]
    return piece(me), [piece(me ^ k) for k in (1, 2, 3)]


def rest_move(sends):
    if len(sends) == 3:
        return [swap_row(send, 2 * k) for k, send in zip((1, 2, 3), sends)]
    group = lax.axis_size("dp") // 2
    spread = lax.all_to_all(
        sends[0], "dp", split_axis=0, concat_axis=0, axis_index_groups=rest_groups(), tiled=True
    )
    return [spread.reshape(group, -1, spread.shape[1])]


def add_all(own, got):
    if got[0].ndim == own.ndim:
        return sum([g.astype(F32) for g in got], own.astype(F32))
    return jnp.sum(got[0].astype(F32), axis=0)


def rest_collect(piece):
    if lax.axis_size("dp") == 8:
        return [piece] + [swap_row(piece, 2 * k) for k in (1, 2, 3)]
    return [lax.all_gather(piece, "dp", axis=0, axis_index_groups=rest_groups(), tiled=True)]


def assemble_body(order, *refs):
    out = refs[-1]
    for index, ref in enumerate(refs[:-1]):
        out[order[index]] = ref[...]


def rest_assemble(pieces):
    if len(pieces) == 1:
        return pieces[0]
    me = lax.axis_index("dp") // 2
    order = (jnp.arange(4, dtype=jnp.int32) ^ me).astype(jnp.int32)
    return call(assemble_body, struct((4,) + pieces[0].shape, BF), [], "assemble", 1)(
        order, *pieces, specs=[SMEM] + [VM] * 4
    ).reshape(-1, pieces[0].shape[1])


def finish_one_body(flag, half, other, up_o, down_o, co_o):
    upper = flag[0] != 0
    low = jnp.where(upper, other[...], half[...]).astype(F32)
    high = jnp.where(upper, half[...], other[...]).astype(F32)
    units = up_o.shape[0]
    split = units // 2
    rest = low.shape[0] - split
    up_o[0:split, :] = low[:split]
    up_o[split:units, :] = high[:split]
    down_o[0:rest, :] = low[split:]
    left = down_o.shape[0] - rest
    down_o[rest:, :] = high[split : split + left]
    co_o[...] = high[split + left :]


def finish_rest_body(flag, half, other, cq_o, so_o, k_o, v_o, q3_o, k3_o, v3_o, gain_o, two_s, three_s):
    upper = flag[0] != 0
    group = half.shape[0]
    two, three = two_s.shape[0] // (2 * group), three_s.shape[0] // (2 * group)
    gain = jnp.zeros(gain_o.shape, F32)
    for index in range(group):
        low = jnp.where(upper, other[index], half[index]).astype(F32)
        high = jnp.where(upper, half[index], other[index]).astype(F32)
        for at, piece in ((index, low), (group + index, high)):
            two_s[at * two : (at + 1) * two, :] = piece[0:two]
            three_s[at * three : (at + 1) * three, :] = piece[two : two + three]
            gain += piece[two + three :]
    wide = cq_o.shape[0]
    cq_o[...] = two_s[0:wide, :]
    for i in range(wide // PAIR):
        so_o[:, i * PAIR : (i + 1) * PAIR] = two_s[wide + i * PAIR : wide + (i + 1) * PAIR, :]
    k_o[...] = two_s[2 * wide : 3 * wide, :]
    v_o[...] = two_s[3 * wide :, :]
    for i, out in enumerate((q3_o, k3_o, v3_o)):
        out[...] = three_s[i * wide : (i + 1) * wide, :]
    gain_o[...] = gain


def on_device(
    x_first,
    x_second,
    memory,
    cot_first,
    cot_second,
    seg_ids,
    lengths,
    perm,
    inverse,
    gains,
    w_self_qkv,
    w_self_out,
    w_cross_q,
    w_cross_kv,
    w_cross_out,
    w_up,
    w_down,
):
    length = seg_ids.shape[2]
    size = x_first.shape[1]
    wide = x_first.shape[2]
    width = w_self_out.shape[0]
    units = w_up.shape[1]
    mine = 2 * size
    heads = 2 * width
    me = lax.axis_index("tensor")
    row = lax.axis_index("dp")
    rows = perm.shape[0]
    share = size // rows
    first_step = me < 2
    upper = (row & 1) != 0

    def both(one, two):
        return jnp.where(first_step, one, two)

    def stage(**values):
        return lax.optimization_barrier(values)

    pair_array = struct((2, length, PAIR), BF)
    out_half = struct((2, size, heads), BF)
    lse_array = struct((2, 2, length), F32)
    limits = [pltpu.VMEM((1, length), jnp.int32), pltpu.VMEM((1, length), jnp.int32)]
    forward_scratch = [
        pltpu.VMEM((2, length + FORWARD_BK - ALIGN, PAIR), BF),
        pltpu.VMEM((2, PAIR, length + FORWARD_BK - ALIGN), BF),
        pltpu.VMEM((length, heads), BF),
    ] + limits
    whole = pl.BlockSpec(memory_space=pltpu.VMEM)

    def part_of(rows_of_block, index):
        return pl.BlockSpec((rows_of_block, PAIR), lambda i: (index, 0))

    x_first, x_second, memory = x_first[0], x_second[0], memory[0]
    x_got = swap_chip(both(x_second, x_first))
    wqkv_own = w_self_qkv.reshape(wide, -1)
    wqkv_got = swap_chip(wqkv_own)
    x_own = both(x_first, x_second)
    place = jnp.arange(length, dtype=jnp.int32)
    meta = jnp.where(place[None, :] < lengths[0][:, None], seg_ids[0], DOCS)
    docs = jnp.arange(DOCS + 2, dtype=jnp.int32)
    cuts = jnp.sum((meta[:, None, :] < docs[None, :, None]).astype(jnp.int32), axis=-1).reshape(-1)
    digits = jnp.stack([cuts // 64, cuts % 64]).astype(BF)
    digits = jnp.pad(digits, ((0, 14), (0, wide - cuts.shape[0])))
    payload = jnp.concatenate(
        [memory.reshape(rows, share, wide), jnp.broadcast_to(digits[None], (rows, 16, wide))], axis=1
    )
    x_sib0 = swap_core(x_own)
    pack_a = pack(w_self_out, w_cross_q, w_cross_kv.reshape(wide, -1), w_cross_out)
    pack_b = pack(w_up, w_down)
    spread = spread_rows(payload.reshape(-1, wide)).reshape(payload.shape)
    cot_own = both(cot_first[0], cot_second[0])
    cot_send = both(cot_second[0], cot_first[0])
    x_got, pack_a, pack_b, cot_own, cot_send = lax.optimization_barrier(
        (x_got, pack_a, pack_b, cot_own, cot_send)
    )
    x_sib1 = swap_core(x_got)
    s = stage(
        spread=spread,
        x_got=x_got,
        x_sib1=x_sib1,
        wqkv_own=wqkv_own,
        pack_a=pack_a,
        pack_b=pack_b,
        cot_own=cot_own,
        cot_send=cot_send,
        x_sib0=x_sib0,
        cuts=cuts,
        memory=memory,
    )
    pack_a, pack_b, cot_own, cot_send = [s[n] for n in ("pack_a", "pack_b", "cot_own", "cot_send")]
    x_sib0, cuts, memory = s["x_sib0"], s["cuts"], s["memory"]
    x_got, x_sib1, wqkv_own = s["x_got"], s["x_sib1"], s["wqkv_own"]
    picked, digits = call(
        pick_memory_body,
        (struct((rows, share, wide), BF), struct((16, wide), BF)),
        [],
        "pick_memory",
        1,
    )(jnp.concatenate([perm, row[None].astype(jnp.int32)]), s["spread"], specs=[SMEM, VM])
    digits = digits[:2, : cuts.shape[0]].astype(jnp.int32)
    cuts = both(digits[0] * 64 + digits[1], cuts)
    places = jnp.stack([me, me ^ 2, me ^ 1, me ^ 3]).astype(jnp.int32)
    s = stage(
        scalars=jnp.concatenate([cuts, places]),
        x0=x_own,
        x1=x_got,
        x2=x_sib0,
        x3=x_sib1,
        w0=wqkv_own,
        w1=wqkv_got,
        picked=picked,
        pack_a=pack_a,
        pack_b=pack_b,
        cot_own=cot_own,
        cot_send=cot_send,
        memory=memory,
    )
    scalars = s["scalars"]
    xs = (s["x0"], s["x1"], s["x2"], s["x3"])
    wqkv = (s["w0"], s["w1"])
    memory = s["memory"]

    memory_one = spread_rows(s["picked"].reshape(memory.shape))
    q, k, v, a_mine, a_send, lse = call(
        self_forward_body,
        (pair_array, pair_array, pair_array, out_half, out_half, lse_array),
        forward_scratch,
        "self_forward",
        27,
    )(scalars, *xs, gains, *wqkv, specs=[SMEM] + [VM] * 7)
    pack_a, pack_b = s["pack_a"], s["pack_b"]
    s = stage(
        q=q,
        k=k,
        v=v,
        a_mine=a_mine,
        a_send=a_send,
        lse=lse,
        memory_one=memory_one,
        a_got=swap_chip(pack_a),
        cot_got=swap_chip(s["cot_send"]),
        pack_a2=swap_core(pack_a),
        pack_b2=swap_core(pack_b),
    )
    q, k, v, a_mine, a_send, lse = [s[n] for n in ("q", "k", "v", "a_mine", "a_send", "lse")]
    pack_a1, pack_a2, pack_b2, cot_got = s["a_got"], s["pack_a2"], s["pack_b2"], s["cot_got"]
    memory_one = s["memory_one"]
    m_got = swap_chip(both(memory, memory_one))
    s = stage(
        a_got=swap_core(a_send),
        pack_a3=swap_core(pack_a1),
        m_own=both(memory_one, memory),
    )
    a_got, m_own = s["a_got"], s["m_own"]
    packs_a = (pack_a, pack_a1, pack_a2, s["pack_a3"])

    so_cq = part_of(2 * wide, 0)
    h1, cq_mine, cq_send = call(
        after_self_body,
        (struct((mine, wide), F32), struct((mine, heads), BF), struct((mine, heads), BF)),
        [],
        "after_self",
        6,
        (1,),
    )(
        *xs[:2], a_mine, a_got, *packs_a, gains, specs=[whole] * 4 + [so_cq] * 4 + [whole]
    )
    h1, m_got = lax.optimization_barrier((h1, m_got))
    s = stage(
        h1=h1,
        cq_mine=cq_mine,
        cq_got=swap_core(cq_send),
        m1=m_got,
        m2=swap_core(m_own),
        m3=swap_core(m_got),
        pack_b=pack_b,
    )
    h1, cq_mine, cq_got, pack_b = s["h1"], s["cq_mine"], s["cq_got"], s["pack_b"]
    ms = (m_own, s["m1"], s["m2"], s["m3"])

    kv = part_of(2 * wide, 1)
    cq, ck, cv, b_mine, b_send, lse_b = call(
        cross_forward_body,
        (pair_array, pair_array, pair_array, out_half, out_half, lse_array),
        forward_scratch,
        "cross_forward",
        24,
        (1,),
    )(
        scalars,
        cq_mine,
        cq_got,
        *ms,
        pack_a,
        pack_a1,
        specs=[SMEM] + [whole] * 6 + [kv] * 2,
    )
    s = stage(
        cq=cq,
        ck=ck,
        cv=cv,
        b_mine=b_mine,
        b_send=b_send,
        lse_b=lse_b,
        pack_b1=swap_chip(pack_b),
    )
    cq, ck, cv, b_mine, b_send, lse_b = [
        s[n] for n in ("cq", "ck", "cv", "b_mine", "b_send", "lse_b")
    ]
    pack_b1 = s["pack_b1"]
    s = stage(b_got=swap_core(b_send), pack_b3=swap_core(pack_b1))

    co = part_of(wide, 4)
    rows_b = units + width
    (
        y_own, y_send, dh2, db_mine, db_send, up_keep, up_give, down_keep, down_give, gain_three,
    ) = call(
        middle_body,
        (
            struct((size, wide), BF),
            struct((size, wide), BF),
            struct((mine, wide), F32),
            struct((mine, heads), BF),
            struct((mine, heads), BF),
            struct((2, wide, units), BF),
            struct((2, wide, units), BF),
            struct((2, rows_b, wide), BF),
            struct((2, rows_b, wide), BF),
            struct((8, wide), F32),
        ),
        [
            pltpu.VMEM((mine, wide), F32),
            pltpu.VMEM((mine, wide), BF),
            pltpu.VMEM((mine, wide), BF),
            pltpu.VMEM((mine, wide), F32),
            pltpu.VMEM((mine, wide), F32),
        ],
        "middle",
        25,
        (1,),
    )(
        scalars,
        h1,
        b_mine,
        s["b_got"],
        *packs_a,
        pack_b,
        pack_b1,
        pack_b2,
        s["pack_b3"],
        gains,
        cot_own,
        cot_got,
        specs=[SMEM] + [whole] * 3 + [co] * 4 + [whole] * 7,
    )

    def over_core(keep, got):
        own = keep[0].astype(F32) + got[0].astype(F32)
        other = keep[1].astype(F32) + got[1].astype(F32)
        return own, other.astype(BF)

    up_got, down_got = swap_core(up_give), swap_core(down_give)
    up_own, up_send = over_core(up_keep, up_got)
    half_b = rows_b // 2
    down_sum = down_keep.astype(F32) + down_got.astype(F32)
    down_low, down_high = down_sum[:, :half_b], down_sum[:, half_b:]
    down_mine = jnp.where(upper, down_high, down_low)
    down_send = jnp.where(upper, down_low, down_high).astype(BF)
    s = stage(
        y_own=y_own,
        y_send=y_send,
        dh2=dh2,
        db_mine=db_mine,
        db_got=swap_core(db_send),
        up_own=up_own,
        up_send=up_send,
        down_mine=down_mine,
        down_send=down_send,
        gain_three=gain_three,
    )
    y_own, dh2, up_own, down_mine = s["y_own"], s["dh2"], s["up_own"], s["down_mine"]
    gain_three = s["gain_three"]

    def backward_scratch(pairs):
        return [
            pltpu.VMEM((pairs, length + BK - ALIGN, PAIR), BF),
            pltpu.VMEM((pairs, PAIR, length + BK - ALIGN), BF),
            pltpu.VMEM((pairs, length + BK - ALIGN, PAIR), BF),
            pltpu.VMEM((pairs, length, PAIR), BF),
            pltpu.VMEM((pairs, length, PAIR), BF),
            pltpu.VMEM((pairs, length, PAIR), BF),
            pltpu.VMEM((pairs, length + BK - ALIGN, PAIR), F32),
            pltpu.VMEM((pairs, length + BK - ALIGN, PAIR), F32),
        ] + limits

    dcq_mine, dcq_send, dck, dcv = call(
        cross_backward_body,
        (out_half, out_half, pair_array, pair_array),
        backward_scratch(2),
        "cross_backward",
        27,
    )(
        scalars, cq, ck, cv, b_mine, b_send, lse_b, s["db_mine"], s["db_got"],
        specs=[SMEM] + [VM] * 8,
    )
    s = stage(
        dcq_mine=dcq_mine,
        dcq_send=dcq_send,
        dck=dck,
        dcv=dcv,
        up_got=swap_chip(s["up_send"]),
        y_got=swap_chip(s["y_send"]),
        down_got=swap_row(s["down_send"], 1),
        up_own=up_own,
        down_mine=down_mine,
        y_own=y_own,
    )
    dcq_mine, dcq_send, y_got, y_own = s["dcq_mine"], s["dcq_send"], s["y_got"], s["y_own"]
    up_keep, up_send = halves(s["up_own"] + s["up_got"].astype(F32), upper)
    down_own = s["down_mine"][0] + s["down_got"][0].astype(F32)
    down_send = (s["down_mine"][1] + s["down_got"][1].astype(F32)).astype(BF)
    dm_mine, dm_send, keep_kv, give_kv = call(
        memory_back_body,
        (
            struct((2, size, wide), BF),
            struct((2, size, wide), BF),
            struct((2 * wide, width), BF),
            struct((2 * wide, width), BF),
        ),
        [],
        "memory_back",
        6,
        (1,),
    )(
        scalars, s["dck"], s["dcv"], *ms, pack_a, pack_a1, specs=[SMEM] + [whole] * 6 + [kv] * 2
    )
    s = stage(
        dcq_got=swap_core(dcq_send),
        up_keep=up_keep,
        up_send=up_send,
        down_own=down_own,
        down_send=down_send,
        dm_mine=dm_mine,
        dm_send=dm_send,
        keep_kv=keep_kv,
        give_kv=give_kv,
        y_first=both(y_own, y_got),
        y_second=both(y_got, y_own),
    )
    up_keep, down_own, dm_mine = s["up_keep"], s["down_own"], s["dm_mine"]
    keep_kv, give_kv = s["keep_kv"], s["give_kv"]
    y_first, y_second = s["y_first"], s["y_second"]

    dh1, da_mine, da_send, keep_two, give_two, gain_two = call(
        between_body,
        (
            struct((mine, wide), F32),
            struct((mine, heads), BF),
            struct((mine, heads), BF),
            struct((2, 2 * wide, width), BF),
            struct((2, 2 * wide, width), BF),
            struct((8, wide), F32),
        ),
        [],
        "between",
        8,
        (1,),
    )(
        h1, dh2, a_mine, a_got, dcq_mine, s["dcq_got"], *packs_a, gains,
        specs=[whole] * 6 + [so_cq] * 4 + [whole],
    )
    s = stage(
        dh1=dh1,
        da_mine=da_mine,
        da_send=da_send,
        keep_two=keep_two,
        give_two=give_two,
        gain_two=gain_two,
        dm_core=swap_core(s["dm_send"]),
        dm_mine=dm_mine,
        up_got=swap_row(s["up_send"], 1),
        down_got=swap_chip(s["down_send"]),
        up_keep=up_keep,
        down_own=down_own,
    )
    dh1, da_mine, gain_two = s["dh1"], s["da_mine"], s["gain_two"]
    one_half = jnp.concatenate(
        [
            s["up_keep"] + s["up_got"].astype(F32),
            s["down_own"] + s["down_got"].astype(F32),
        ],
        axis=0,
    ).astype(BF)
    one_half = lax.psum(one_half, "dp", axis_index_groups=rest_groups())
    dm_own, dm_other = [
        (s["dm_mine"][i].astype(F32) + s["dm_core"][i].astype(F32)).astype(BF) for i in range(2)
    ]
    two_own, two_send = over_core(s["keep_two"], swap_core(s["give_two"]))
    s = stage(
        da_got=swap_core(s["da_send"]),
        da_mine=da_mine,
        dm_own=dm_own,
        dm_other=dm_other,
        two_own=two_own,
        two_send=jnp.concatenate([two_send, give_kv], axis=0),
    )
    two_own, dm_own = s["two_own"], s["dm_own"]
    da_mine, da_got = s["da_mine"], s["da_got"]

    def self_backward(pair, da_mine, da_got):
        third = pl.BlockSpec((1, length, PAIR), lambda i: (pair, 0, 0))
        lanes = pl.BlockSpec((2, size, PAIR), lambda i: (0, 0, pair))
        flat = pl.BlockSpec((mine, PAIR), lambda i: (0, pair))
        sums = pl.BlockSpec((1, 2, length), lambda i: (pair, 0, 0))
        return call(
            self_backward_body,
            struct((4, size, 3 * PAIR), BF),
            backward_scratch(1),
            "self_backward",
            17,
            (1,),
        )(
            scalars,
            q,
            k,
            v,
            a_mine,
            a_send,
            lse,
            da_mine,
            da_got,
            specs=[SMEM, third, third, third, lanes, lanes, sums, flat, flat],
        )

    qkv_gradient = struct((3 * wide, width), BF)
    gain_row = struct((8, wide), F32)
    dqkv1 = self_backward(1, da_mine, da_got)
    give_qkv, gain_one = call(qkv_give_body, (qkv_gradient, gain_row), [], "qkv_give", 5)(
        dqkv1, *xs, gains, wqkv[1], specs=[VM] * 7
    )
    s = stage(
        dqkv1=dqkv1,
        give_qkv=give_qkv,
        gain_one=gain_one,
        two_got=swap_chip(s["two_send"]),
        two_own=two_own,
        dm_got=swap_chip(s["dm_other"]),
        dm_own=dm_own,
        keep_kv=keep_kv,
        da_mine=da_mine,
        da_got=da_got,
    )
    dqkv1, da_mine, da_got, gain_one = [s[n] for n in ("dqkv1", "da_mine", "da_got", "gain_one")]
    two_total = jnp.concatenate(
        [
            s["two_own"] + s["two_got"][: 2 * wide].astype(F32),
            s["keep_kv"].astype(F32) + s["two_got"][2 * wide :].astype(F32),
        ],
        axis=0,
    )
    two_keep, two_send = halves(two_total, upper)
    s = stage(
        dm_one=both(s["dm_own"], s["dm_got"]),
        two_keep=two_keep,
        two_send=two_send,
        dm_two=both(s["dm_got"], s["dm_own"]),
        give_qkv=s["give_qkv"],
    )
    dm_two, two_keep = s["dm_two"], s["two_keep"]

    qkv_got = swap_chip(s["give_qkv"])
    s = stage(
        dqkv0=self_backward(0, da_mine, da_got),
        qkv_got=qkv_got,
        dm_spread=spread_rows(s["dm_one"]),
        two_got=swap_row(s["two_send"], 1),
        two_keep=two_keep,
        dm_two=dm_two,
    )
    dqkv0, qkv_got, dm_two = s["dqkv0"], s["qkv_got"], s["dm_two"]
    s = stage(
        dm_picked=pick(s["dm_spread"].reshape(rows, -1, wide), inverse),
        two_half=s["two_keep"] + s["two_got"].astype(F32),
    )
    two_half = s["two_half"]
    dm_back = spread_rows(s["dm_picked"].reshape(memory.shape))
    keep_qkv, gain_all = call(qkv_keep_body, (qkv_gradient, gain_row), [], "qkv_keep", 5)(
        dqkv0, *xs, gains, wqkv[0], qkv_got, gain_one, gain_two, gain_three, specs=[VM] * 11
    )
    s = stage(keep_qkv=keep_qkv, gain_all=gain_all, one_half=one_half, two_half=two_half)
    one_half, two_half = s["one_half"], s["two_half"]
    three_keep, three_send = halves(s["keep_qkv"], upper)
    s = stage(
        three_keep=three_keep,
        three_send=three_send,
        two_half=two_half,
        gain_all=s["gain_all"],
    )

    dn_mine, dn_send = call(
        back_to_input_body,
        (struct((2, size, wide), BF), struct((2, size, wide), BF)),
        [],
        "back_to_input",
        4,
    )(dqkv0, dqkv1, *wqkv, specs=[VM] * 4)
    s = stage(
        three_got=swap_row(s["three_send"], 1),
        three_keep=s["three_keep"],
        two_half=s["two_half"],
        gain_all=s["gain_all"] + swap_core(s["gain_all"]),
        dn_mine=dn_mine,
        dn_send=dn_send,
        one_half=one_half,
        dm_back=dm_back,
    )
    one_half, dn_mine, dm_back = s["one_half"], s["dn_mine"], s["dm_back"]
    three_half = s["three_keep"].astype(F32) + s["three_got"].astype(F32)
    share_two, share_three = s["two_half"].shape[0], three_half.shape[0]
    last_own, last_sends = rest_sends(
        [piece.astype(BF) for piece in (s["two_half"], three_half)]
    )
    s = stage(
        last_own=last_own,
        last_sends=last_sends,
        gain_all=s["gain_all"],
        dn_got=swap_core(s["dn_send"]),
    )
    grad_own, grad_send = call(
        input_grad_body,
        (struct((size, wide), BF), struct((size, wide), BF)),
        [],
        "input_grad",
        5,
    )(dn_mine, s["dn_got"], *xs[:2], dh1, gains, specs=[VM] * 6)
    s = stage(
        last_own=s["last_own"],
        last_got=rest_move(s["last_sends"]),
        gain_all=s["gain_all"] + swap_chip(s["gain_all"]),
        grad_own=grad_own,
        grad_send=grad_send,
        one_half=one_half,
    )
    one_half, grad_own = s["one_half"], s["grad_own"]
    grad_got = swap_chip(s["grad_send"])
    one_other = swap_row(one_half, 1)
    gain_rows = 8 * wide // width
    last = jnp.concatenate(
        [
            add_all(s["last_own"], s["last_got"]).astype(BF),
            s["gain_all"].astype(BF).reshape(gain_rows, width),
        ],
        axis=0,
    )
    s = stage(pieces=rest_collect(last), one_half=one_half, one_other=one_other)
    half = rest_assemble(s["pieces"])
    other = swap_row(half, 1)
    flag = (row & 1)[None].astype(jnp.int32)
    grad_up, grad_down, grad_cross_out = call(
        finish_one_body,
        (struct((wide, units), F32), struct((units, wide), F32), struct((width, wide), F32)),
        [],
        "finish_one",
        2,
    )(flag, s["one_half"], s["one_other"], specs=[SMEM, VM, VM])
    slab = struct((wide, width), F32)
    group = (rows // 2, last.shape[0], width)
    grad_cross_q, grad_self_out, kv0, kv1, q0, q1, q2, gain_total = call(
        finish_rest_body,
        (slab, struct((width, wide), F32), slab, slab, slab, slab, slab)
        + (struct((gain_rows, width), F32),),
        [pltpu.VMEM((4 * wide, width), F32), pltpu.VMEM((3 * wide, width), F32)],
        "finish_rest",
        2,
    )(flag, half.reshape(group), other.reshape(group), specs=[SMEM, VM, VM])
    grad_kv = jnp.stack([kv0, kv1], axis=1)
    grad_qkv = jnp.stack([q0, q1, q2], axis=1)
    gain_total = gain_total.reshape(-1, wide)[:3]
    grad_gains = lax.dynamic_slice(gain_total, (0, me * width), (3, width))
    grad_first = both(grad_own, grad_got)
    grad_memory = dm_two.astype(F32) + dm_back.astype(F32)
    return (
        y_first[None],
        y_second[None],
        grad_first[None],
        grad_memory[None],
        grad_gains,
        grad_qkv,
        grad_self_out,
        grad_cross_q,
        grad_kv,
        grad_cross_out,
        grad_up,
        grad_down,
    )


def solution(mesh):
    in_specs = (
        P("dp", "tensor", None),
        P("dp", "tensor", None),
        P("dp", "tensor", None),
        P("dp", "tensor", None),
        P("dp", "tensor", None),
        P("dp", None, None),
        P("dp", None),
        P(),
        P(),
        P(),
        P(None, None, "tensor"),
        P("tensor", None),
        P(None, "tensor"),
        P(None, None, "tensor"),
        P("tensor", None),
        P(None, "tensor"),
        P("tensor", None),
    )
    out_specs = (
        P("dp", "tensor", None),
        P("dp", "tensor", None),
        P("dp", "tensor", None),
        P("dp", "tensor", None),
        P(None, "tensor"),
        P(None, None, "tensor"),
        P("tensor", None),
        P(None, "tensor"),
        P(None, None, "tensor"),
        P("tensor", None),
        P(None, "tensor"),
        P("tensor", None),
    )
    return jax.shard_map(
        on_device, mesh=mesh, in_specs=in_specs, out_specs=out_specs, check_vma=False
    )
```

```python
import functools
import math

import jax
import jax.numpy as jnp
from jax import lax
from jax.experimental import pallas as pl
from jax.experimental.pallas import tpu as pltpu
from jax.sharding import PartitionSpec as P

HEAD_DIM = 64
EPSILON = 1e-05
NEG_FILL = -1e30
DOCS = 16
PAIR = 2 * HEAD_DIM
BQ = 256
BK = 256
SELF_BK = 640
CROSS_BK = 512
ALIGN = 128
BF = jnp.bfloat16
F32 = jnp.float32
VMEM_BYTES = 56 * 1024 * 1024
LOG2E = 1.4426950408889634

ANY = pl.BlockSpec(memory_space=pl.ANY)
SMEM = pl.BlockSpec(memory_space=pltpu.SMEM)
VM = pl.BlockSpec(memory_space=pltpu.VMEM)


def dot(a, b):
    return lax.dot_general(a, b, (((1,), (0,)), ((), ())), preferred_element_type=F32)


def dot_nt(a, b):
    return lax.dot_general(a, b, (((1,), (1,)), ((), ())), preferred_element_type=F32)


def dot_tn(a, b):
    return lax.dot_general(a, b, (((0,), (0,)), ((), ())), preferred_element_type=F32)


def normalize(hidden):
    centred = hidden - jnp.mean(hidden, axis=-1, keepdims=True)
    inv_sigma = lax.rsqrt(jnp.mean(centred * centred, axis=-1, keepdims=True) + EPSILON)
    return centred * inv_sigma, inv_sigma


def normalize_back(grad_scaled, gain, normal, inv_sigma):
    grad_normal = grad_scaled * gain
    first_mean = jnp.mean(grad_normal, axis=-1, keepdims=True)
    second_mean = jnp.mean(grad_normal * normal, axis=-1, keepdims=True)
    return inv_sigma * (grad_normal - first_mean - normal * second_mean)


def call(body, outs, scratch, name, cost, grid=()):
    def run(*args, specs):
        moved = sum(a.size * a.dtype.itemsize for a in args)
        return pl.pallas_call(
            body,
            out_shape=outs,
            grid=grid,
            in_specs=specs,
            out_specs=jax.tree.map(lambda _: VM, outs),
            scratch_shapes=scratch,
            compiler_params=pltpu.CompilerParams(vmem_limit_bytes=VMEM_BYTES),
            cost_estimate=pl.CostEstimate(flops=int(cost * 1.15e9), bytes_accessed=moved, transcendentals=0),
            name=name,
        )(*args)

    return run


def struct(shape, dtype):
    return jax.ShapeDtypeStruct(shape, dtype)


QUERY_AT, KEY_AT, PLACE_AT = 0, DOCS + 2, 2 * (DOCS + 2)
ROW_AT = PLACE_AT + 4


def key_limits(scalars, key_at, length):
    place = lax.broadcasted_iota(jnp.int32, (1, length), 1)
    first = jnp.full((1, length), scalars[key_at], jnp.int32)
    after = jnp.full((1, length), scalars[key_at + 1], jnp.int32)
    for doc in range(1, DOCS + 1):
        inside = place >= scalars[QUERY_AT + doc]
        first = jnp.where(inside, scalars[key_at + doc], first)
        after = jnp.where(inside, scalars[key_at + doc + 1], after)
    return first, after


def window(scalars, key_at, begin, size):
    low = scalars[key_at]
    high = scalars[key_at + 1]
    for doc in range(1, DOCS + 1):
        low = jnp.where(begin >= scalars[QUERY_AT + doc], scalars[key_at + doc], low)
        high = jnp.where(
            begin + (BQ - 1) >= scalars[QUERY_AT + doc], scalars[key_at + doc + 1], high
        )
    low = (low // ALIGN) * ALIGN
    return low, (high - low + (size - 1)) // size


def two_heads(block):
    lane = lax.broadcasted_iota(jnp.int32, block.shape, 1)
    zero = jnp.zeros_like(block)
    return jnp.concatenate(
        [jnp.where(lane < HEAD_DIM, block, zero), jnp.where(lane >= HEAD_DIM, block, zero)], axis=0
    )


def attend_forward(scalars, key_at, key_block, pairs, q_s, k_s, vt_s, o_s, lse_s, first_s, after_s):
    length = q_s.shape[1]
    scale = LOG2E / math.sqrt(HEAD_DIM)
    first, after = key_limits(scalars, key_at, length)
    first_s[...] = first
    after_s[...] = after
    rows = lax.broadcasted_iota(jnp.int32, (key_block, BQ), 0)

    def one_block(index, unused):
        begin = pl.multiple_of(index * BQ, BQ)
        low, count = window(scalars, key_at, begin, key_block)
        first_row = first_s[:, pl.ds(begin, BQ)]
        after_row = after_s[:, pl.ds(begin, BQ)]
        queries = [two_heads(q_s[pair, pl.ds(begin, BQ), :]) for pair in pairs]

        def step(turn, carry):
            start = pl.multiple_of(low + turn * key_block, ALIGN)
            allowed = (rows >= first_row - start) & (rows < after_row - start)
            allowed = jnp.concatenate([allowed, allowed], axis=1)
            results = []
            for pair, query, (top, total, out) in zip(pairs, queries, carry):
                scores = dot_nt(k_s[pair, pl.ds(start, key_block), :], query) * scale
                scores = jnp.where(allowed, scores, NEG_FILL)
                new_top = jnp.maximum(top, jnp.max(scores, axis=0, keepdims=True))
                shrink = jnp.exp2(top - new_top)
                raised = jnp.exp2(scores - new_top)
                total = total * shrink + jnp.sum(raised, axis=0, keepdims=True)
                low_probs = raised.astype(BF)
                value = vt_s[pair, :, pl.ds(start, key_block)]
                out = [
                    out[0] * shrink[:, :BQ] + dot(value[:HEAD_DIM], low_probs[:, :BQ]),
                    out[1] * shrink[:, BQ:] + dot(value[HEAD_DIM:], low_probs[:, BQ:]),
                ]
                results.append((new_top, total, out))
            return results

        zero = jnp.zeros((HEAD_DIM, BQ), F32)
        fresh = (jnp.full((1, 2 * BQ), NEG_FILL, F32), jnp.zeros((1, 2 * BQ), F32), [zero, zero])
        results = lax.fori_loop(0, count, step, [fresh for unused_pair in pairs])
        for pair, (top, total, out) in zip(pairs, results):
            inverse = 1.0 / total
            out = jnp.concatenate([out[0] * inverse[:, :BQ], out[1] * inverse[:, BQ:]], axis=0)
            o_s[pl.ds(begin, BQ), pair * PAIR : (pair + 1) * PAIR] = out.T.astype(BF)
            log_total = top + jnp.log2(total)
            lse_s[pair, 0:1, pl.ds(begin, BQ)] = log_total[:, :BQ]
            lse_s[pair, 1:2, pl.ds(begin, BQ)] = log_total[:, BQ:]
        return unused

    lax.fori_loop(0, length // BQ, one_block, 0)


def attend_backward(
    scalars, key_at, pairs, q_s, k_s, kt_s, v_s, o_s, do_s, lse_s, dq_s, dk_s, dv_s, first_s, after_s
):
    length = q_s.shape[1]
    scale = LOG2E / math.sqrt(HEAD_DIM)
    first, after = key_limits(scalars, key_at, length)
    first_s[...] = first
    after_s[...] = after
    rows = lax.broadcasted_iota(jnp.int32, (BK, BQ), 0)
    dk_s[...] = jnp.zeros_like(dk_s)
    dv_s[...] = jnp.zeros_like(dv_s)
    ones = jnp.ones((8, PAIR), F32)

    def one_block(index, unused):
        begin = pl.multiple_of(index * BQ, BQ)
        low, count = window(scalars, key_at, begin, BK)
        first_row = first_s[:, pl.ds(begin, BQ)]
        after_row = after_s[:, pl.ds(begin, BQ)]
        fixed = []
        for pair in pairs:
            query = two_heads(q_s[pair, pl.ds(begin, BQ), :])
            grad = two_heads(do_s[pair, pl.ds(begin, BQ), :])
            out = o_s[pair, pl.ds(begin, BQ), :].astype(F32)
            product = grad.astype(F32) * jnp.concatenate([out, out], axis=0)
            centre = lax.dot_general(
                ones,
                product,
                (((1,), (1,)), ((), ())),
                precision=lax.Precision.HIGHEST,
                preferred_element_type=F32,
            )[:1]
            log_total = jnp.concatenate(
                [lse_s[pair, 0:1, pl.ds(begin, BQ)], lse_s[pair, 1:2, pl.ds(begin, BQ)]], axis=1
            )
            fixed.append((query, grad, centre, log_total))

        def step(turn, carry):
            start = pl.multiple_of(low + turn * BK, ALIGN)
            allowed = (rows >= first_row - start) & (rows < after_row - start)
            allowed = jnp.concatenate([allowed, allowed], axis=1)
            results = []
            for pair, (query, grad, centre, log_total), dq in zip(pairs, fixed, carry):
                scores = dot_nt(k_s[pair, pl.ds(start, BK), :], query) * scale
                probs = jnp.exp2(jnp.where(allowed, scores, NEG_FILL) - log_total)
                dprobs = dot_nt(v_s[pair, pl.ds(start, BK), :], grad)
                dscores = (probs * (dprobs - centre)).astype(BF)
                dv_s[pair, pl.ds(start, BK), :] += dot(probs.astype(BF), grad)
                dk_s[pair, pl.ds(start, BK), :] += dot(dscores, query)
                kt = kt_s[pair, :, pl.ds(start, BK)]
                results.append(
                    [
                        dq[0] + dot(kt[:HEAD_DIM], dscores[:, :BQ]),
                        dq[1] + dot(kt[HEAD_DIM:], dscores[:, BQ:]),
                    ]
                )
            return results

        zero = jnp.zeros((HEAD_DIM, BQ), F32)
        results = lax.fori_loop(0, count, step, [[zero, zero] for unused_pair in pairs])
        for pair, dq in zip(pairs, results):
            dq = jnp.concatenate(dq, axis=0) * (1.0 / math.sqrt(HEAD_DIM))
            dq_s[pair, pl.ds(begin, BQ), :] = dq.T.astype(BF)
        return unused

    lax.fori_loop(0, length // BQ, one_block, 0)


def block_of(scalars, slot, size):
    return pl.multiple_of(scalars[PLACE_AT + slot] * size, size)


def clear_padding(length, k_s, t_s, v_s=None):
    pairs, padded = k_s.shape[:2]
    extra = padded - length
    k_s[:, pl.ds(length, extra), :] = jnp.zeros((pairs, extra, PAIR), BF)
    t_s[:, :, pl.ds(length, extra)] = jnp.zeros((pairs, PAIR, extra), BF)
    if v_s is not None:
        v_s[:, pl.ds(length, extra), :] = jnp.zeros((pairs, extra, PAIR), BF)


def hand_out(scalars, o_s, mine_o, send_o):
    size = mine_o.shape[1]
    for slot in range(4):
        place = block_of(scalars, slot, size)
        (mine_o if slot < 2 else send_o)[slot % 2] = o_s[pl.ds(place, size), :]


def self_forward_body(
    scalars, x0, x1, x2, x3, gains, w0, w1, q_o, k_o, v_o, mine_o, send_o, lse_o, k_s, vt_s, o_s, first_s, after_s
):
    size = x0.shape[0]
    length = q_o.shape[1]
    gain = gains[0:1, :]
    clear_padding(length, k_s, vt_s)
    for slot, x in enumerate((x0, x1, x2, x3)):
        place = block_of(scalars, slot, size)
        normal, unused = normalize(x[...].astype(F32))
        normed = (normal * gain).astype(BF)
        for pair, w in enumerate((w0, w1)):
            packed = dot(normed, w[...]).astype(BF)
            keys, values = packed[:, PAIR : 2 * PAIR], packed[:, 2 * PAIR :]
            q_o[pair, pl.ds(place, size), :] = packed[:, :PAIR]
            k_s[pair, pl.ds(place, size), :] = keys
            k_o[pair, pl.ds(place, size), :] = keys
            v_o[pair, pl.ds(place, size), :] = values
            vt_s[pair, :, pl.ds(place, size)] = values.T
    attend_forward(scalars, QUERY_AT, SELF_BK, (0, 1), q_o, k_s, vt_s, o_s, lse_o, first_s, after_s)
    hand_out(scalars, o_s, mine_o, send_o)


def cross_forward_body(
    scalars, cq0, cq1, m0, m1, m2, m3, w0, w1, q_o, k_o, v_o, mine_o, send_o, lse_o, k_s, vt_s, o_s, first_s, after_s
):
    size = m0.shape[0]
    length = q_o.shape[1]
    clear_padding(length, k_s, vt_s)
    for slot, memory in enumerate((m0, m1, m2, m3)):
        place = block_of(scalars, slot, size)
        source = cq0 if slot < 2 else cq1
        for pair, w in enumerate((w0, w1)):
            packed = dot(memory[...], wide_rows(w, 0, memory.shape[1], 2)).astype(BF)
            keys, values = packed[:, :PAIR], packed[:, PAIR:]
            k_s[pair, pl.ds(place, size), :] = keys
            k_o[pair, pl.ds(place, size), :] = keys
            v_o[pair, pl.ds(place, size), :] = values
            vt_s[pair, :, pl.ds(place, size)] = values.T
            q_o[pair, pl.ds(place, size), :] = source[
                pl.ds((slot % 2) * size, size), pair * PAIR : (pair + 1) * PAIR
            ]
    attend_forward(scalars, KEY_AT, CROSS_BK, (0, 1), q_o, k_s, vt_s, o_s, lse_o, first_s, after_s)
    hand_out(scalars, o_s, mine_o, send_o)


def load_backward(scalars, pairs, k, v, a0, a1, da0, da1, k_s, kt_s, v_s, o_s, do_s):
    size = a0.shape[1]
    length = k.shape[1]
    clear_padding(length, k_s, kt_s, v_s)
    for pair in range(pairs):
        k_s[pair, pl.ds(0, length), :] = k[pair]
        v_s[pair, pl.ds(0, length), :] = v[pair]
        lanes = slice(pair * PAIR, (pair + 1) * PAIR)
        for begin in range(0, length, 512):
            kt_s[pair, :, begin : begin + 512] = k[pair, begin : begin + 512, :].T
        for slot in range(4):
            place = block_of(scalars, slot, size)
            within = pl.ds((slot % 2) * size, size)
            do_s[pair, pl.ds(place, size), :] = (da0 if slot < 2 else da1)[within, lanes]
            o_s[pair, pl.ds(place, size), :] = (a0 if slot < 2 else a1)[slot % 2, :, lanes]


def cross_backward_body(
    scalars, q, k, v, a0, a1, lse, da0, da1, mine_o, send_o, dk_o, dv_o,
    k_s, kt_s, v_s, o_s, do_s, dq_s, dk_s, dv_s, first_s, after_s,
):
    size = a0.shape[1]
    length = k.shape[1]
    load_backward(scalars, 2, k, v, a0, a1, da0, da1, k_s, kt_s, v_s, o_s, do_s)
    attend_backward(
        scalars, KEY_AT, (0, 1), q, k_s, kt_s, v_s, o_s, do_s, lse, dq_s, dk_s, dv_s, first_s, after_s
    )
    for slot in range(4):
        place = block_of(scalars, slot, size)
        for pair in range(2):
            (mine_o if slot < 2 else send_o)[slot % 2, :, pair * PAIR : (pair + 1) * PAIR] = dq_s[
                pair, pl.ds(place, size), :
            ]
    dk_o[...] = (dk_s[:, pl.ds(0, length), :] * (1.0 / math.sqrt(HEAD_DIM))).astype(BF)
    dv_o[...] = dv_s[:, pl.ds(0, length), :].astype(BF)


def self_backward_body(
    scalars, q, k, v, a0, a1, lse, da0, da1, dqkv0_o, dqkv1_o,
    k_s, kt_s, v_s, o_s, do_s, dq_s, dk_s, dv_s, first_s, after_s,
):
    size = a0.shape[1]
    load_backward(scalars, 2, k, v, a0, a1, da0, da1, k_s, kt_s, v_s, o_s, do_s)
    attend_backward(
        scalars, QUERY_AT, (0, 1), q, k_s, kt_s, v_s, o_s, do_s, lse, dq_s, dk_s, dv_s, first_s, after_s
    )
    for pair, out in enumerate((dqkv0_o, dqkv1_o)):
        for slot in range(4):
            place = block_of(scalars, slot, size)
            out[slot, :, 0:PAIR] = dq_s[pair, pl.ds(place, size), :]
            out[slot, :, PAIR : 2 * PAIR] = (
                dk_s[pair, pl.ds(place, size), :] * (1.0 / math.sqrt(HEAD_DIM))
            ).astype(BF)
            out[slot, :, 2 * PAIR :] = dv_s[pair, pl.ds(place, size), :].astype(BF)


def wide_rows(ref, begin, rows, count):
    return jnp.concatenate(
        [ref[begin + i * rows : begin + (i + 1) * rows, :] for i in range(count)], axis=1
    )


def after_self_body(x0, x1, a0, a1, p0, p1, p2, p3, gains, h_o, cq0_o, cq1_o):
    size, wide = x0.shape
    packs = (p0, p1, p2, p3)
    w0, w1, w2, w3 = [wide_rows(p, 0, PAIR, wide // PAIR) for p in packs]
    u0, u1, u2, u3 = [p[wide : 2 * wide, :] for p in packs]
    for slot, x in enumerate((x0, x1)):
        here = pl.ds(slot * size, size)
        hidden = x[...].astype(F32)
        mine, other = a0[slot], a1[slot]
        width = w0.shape[0]
        hidden += dot(mine[:, :width], w0) + dot(mine[:, width:], w1)
        hidden += dot(other[:, :width], w2) + dot(other[:, width:], w3)
        h_o[here, :] = hidden
        normal, unused = normalize(hidden)
        normed = (normal * gains[1:2, :]).astype(BF)
        cq0_o[here, :] = jnp.concatenate([dot(normed, u0), dot(normed, u1)], axis=1).astype(BF)
        cq1_o[here, :] = jnp.concatenate([dot(normed, u2), dot(normed, u3)], axis=1).astype(BF)


GELU_C = math.sqrt(2.0 / math.pi)


def middle_body(
    scalars, h, a0, a1, p0, p1, p2, p3, ud0, ud1, ud2, ud3, gains, cot0, cot1,
    y0_o, y1_o, dh_o, da0_o, da1_o, keep_o, give_o, gain_o,
    h_s, n_s, g_s, acc_s, dn_s,
):
    size = cot0.shape[0]
    used = scalars[QUERY_AT + DOCS]
    wide = h.shape[1]
    width = PAIR
    units = ud0.shape[0] * PAIR // (2 * wide)
    w0, w1, w2, w3 = [wide_rows(p, 0, width, wide // PAIR) for p in (p0, p1, p2, p3)]
    for slot, cot in enumerate((cot0, cot1)):
        here = pl.ds(slot * size, size)
        mine, other = a0[slot], a1[slot]
        hidden = h[here, :] + dot(mine[:, :width], w0) + dot(mine[:, width:], w1)
        hidden += dot(other[:, :width], w2) + dot(other[:, width:], w3)
        h_s[here, :] = hidden
        normal, unused = normalize(hidden)
        n_s[here, :] = (normal * gains[2:3, :]).astype(BF)
        place = lax.broadcasted_iota(jnp.int32, (size, 1), 0) + scalars[PLACE_AT + slot] * size
        g_s[here, :] = jnp.where(place < used, cot[...].astype(F32), 0.0).astype(BF)
    acc_s[...] = jnp.zeros_like(acc_s)
    dn_s[...] = jnp.zeros_like(dn_s)
    for shard, ud in enumerate((ud0, ud1, ud2, ud3)):
        w_up = wide_rows(ud, 0, wide, units // PAIR)
        w_down = wide_rows(ud, wide * units // PAIR, units, wide // PAIR)
        grad_up = jnp.zeros(w_up.shape, F32)
        grad_down = jnp.zeros(w_down.shape, F32)
        for begin in range(0, 2 * size, size):
            here = pl.ds(begin, size)
            normed = n_s[here, :]
            grad = g_s[here, :]
            upper = dot(normed, w_up)
            square = upper * upper
            inner_arg = GELU_C * upper * (1.0 + 0.044715 * square)
            bent = jnp.tanh(inner_arg)
            half = 0.5 * (1.0 + bent)
            inner = (upper * half).astype(BF)
            slope = half + 0.5 * upper * (1.0 - bent * bent) * (GELU_C * (1.0 + 3.0 * 0.044715 * square))
            acc_s[here, :] += dot(inner, w_down)
            d_upper = (dot_nt(grad, w_down) * slope).astype(BF)
            dn_s[here, :] += dot_nt(d_upper, w_up)
            grad_up += dot_tn(normed, d_upper)
            grad_down += dot_tn(inner, grad)
        out = keep_o if shard < 2 else give_o
        out[shard % 2, 0:wide, :] = grad_up.astype(BF)
        out[shard % 2, wide : wide + units, :] = grad_down.astype(BF)
    gain_total = jnp.zeros((1, h_s.shape[1]), F32)
    grad_heads = [jnp.zeros((width, h_s.shape[1]), F32) for unused in range(4)]
    for slot, y_o in enumerate((y0_o, y1_o)):
        here = pl.ds(slot * size, size)
        hidden = h_s[here, :]
        y_o[...] = (hidden + acc_s[here, :]).astype(BF)
        normal, inv_sigma = normalize(hidden)
        dn = dn_s[here, :]
        gain_total += jnp.sum(dn * normal, axis=0, keepdims=True)
        dh = g_s[here, :].astype(F32) + normalize_back(dn, gains[2:3, :], normal, inv_sigma)
        dh_o[here, :] = dh
        low = dh.astype(BF)
        da0_o[here, :] = jnp.concatenate([dot_nt(low, w0), dot_nt(low, w1)], axis=1).astype(BF)
        da1_o[here, :] = jnp.concatenate([dot_nt(low, w2), dot_nt(low, w3)], axis=1).astype(BF)
        mine, other = a0[slot], a1[slot]
        parts = (mine[:, :width], mine[:, width:], other[:, :width], other[:, width:])
        grad_heads = [total + dot_tn(part, low) for total, part in zip(grad_heads, parts)]
    for shard in range(4):
        out = keep_o if shard < 2 else give_o
        out[shard % 2, wide + units : wide + units + width, :] = grad_heads[shard].astype(BF)
    gain_o[...] = jnp.broadcast_to(gain_total, gain_o.shape)


def between_body(
    h, dh2, a0, a1, dq0, dq1, p0, p1, p2, p3, gains,
    dh_o, da0_o, da1_o, keep_o, give_o, gain_o,
):
    size = a0.shape[1]
    width = PAIR
    wide = h.shape[1]
    packs = (p0, p1, p2, p3)
    w0, w1, w2, w3 = [wide_rows(p, 0, width, wide // PAIR) for p in packs]
    u0, u1, u2, u3 = [p[wide : 2 * wide, :] for p in packs]
    gain_total = jnp.zeros((1, wide), F32)
    grad_out = [jnp.zeros((width, wide), F32) for unused in range(4)]
    grad_query = [jnp.zeros((wide, width), F32) for unused in range(4)]
    for slot in range(2):
        here = pl.ds(slot * size, size)
        normal, inv_sigma = normalize(h[here, :])
        normed = (normal * gains[1:2, :]).astype(BF)
        mine, other = dq0[slot], dq1[slot]
        pieces = (mine[:, :width], mine[:, width:], other[:, :width], other[:, width:])
        dn = jnp.zeros((size, wide), F32)
        for piece, u in zip(pieces, (u0, u1, u2, u3)):
            dn += dot_nt(piece, u)
        grad_query = [total + dot_tn(normed, piece) for total, piece in zip(grad_query, pieces)]
        gain_total += jnp.sum(dn * normal, axis=0, keepdims=True)
        dh = dh2[here, :] + normalize_back(dn, gains[1:2, :], normal, inv_sigma)
        dh_o[here, :] = dh
        low = dh.astype(BF)
        da0_o[here, :] = jnp.concatenate([dot_nt(low, w0), dot_nt(low, w1)], axis=1).astype(BF)
        da1_o[here, :] = jnp.concatenate([dot_nt(low, w2), dot_nt(low, w3)], axis=1).astype(BF)
        mine, other = a0[slot], a1[slot]
        parts = (mine[:, :width], mine[:, width:], other[:, :width], other[:, width:])
        grad_out = [total + dot_tn(part, low) for total, part in zip(grad_out, parts)]
    for shard in range(4):
        out = keep_o if shard < 2 else give_o
        out[shard % 2, 0:wide, :] = grad_query[shard].astype(BF)
        for part in range(wide // width):
            out[shard % 2, wide + part * width : wide + (part + 1) * width, :] = grad_out[shard][
                :, part * width : (part + 1) * width
            ].astype(BF)
    gain_o[...] = jnp.broadcast_to(gain_total, gain_o.shape)


def memory_back_body(scalars, dk, dv, m0, m1, m2, m3, w0, w1, mine_o, send_o, keep_o, give_o):
    size = m0.shape[0]
    wide = m0.shape[1]
    totals = [jnp.zeros((wide, 2 * PAIR), F32) for unused in range(2)]
    for slot, memory in enumerate((m0, m1, m2, m3)):
        place = block_of(scalars, slot, size)
        total = jnp.zeros((size, wide), F32)
        for pair, w in enumerate((w0, w1)):
            part = jnp.concatenate([dk[pair, pl.ds(place, size), :], dv[pair, pl.ds(place, size), :]], axis=1)
            total += dot_nt(part, wide_rows(w, 0, memory.shape[1], 2))
            totals[pair] += dot_tn(memory[...], part)
        (mine_o if slot < 2 else send_o)[slot % 2] = total.astype(BF)
    for total, out in zip(totals, (keep_o, give_o)):
        out[0:wide, :] = total[:, :PAIR].astype(BF)
        out[wide : 2 * wide, :] = total[:, PAIR:].astype(BF)


def qkv_grad_body(
    dqkv0, dqkv1, x0, x1, x2, x3, gains, w0, w1, gain_two, gain_three, keep_o, give_o, gain_o
):
    wide = x0.shape[1]
    totals = [jnp.zeros((wide, 3 * PAIR), F32) for unused in range(2)]
    for slot, x in enumerate((x0, x1, x2, x3)):
        normal, unused = normalize(x[...].astype(F32))
        normed = (normal * gains[0:1, :]).astype(BF)
        totals = [t + dot_tn(normed, d[slot]) for t, d in zip(totals, (dqkv0, dqkv1))]
    for part in range(3):
        here = slice(part * wide, (part + 1) * wide)
        lanes = slice(part * PAIR, (part + 1) * PAIR)
        keep_o[here, :] = totals[0][:, lanes]
        give_o[here, :] = totals[1][:, lanes].astype(BF)
    product = totals[0] * w0[...].astype(F32) + totals[1] * w1[...].astype(F32)
    gain = lax.dot_general(
        jnp.ones((8, 3 * PAIR), F32),
        product,
        (((1,), (1,)), ((), ())),
        precision=lax.Precision.HIGHEST,
        preferred_element_type=F32,
    ) / gains[0:1, :]
    gain_o[...] = jnp.concatenate(
        [gain[:1], gain_two[:1, :], gain_three[:1, :], jnp.zeros((5, wide), F32)], axis=0
    )


def back_to_input_body(dqkv0, dqkv1, w0, w1, mine_o, send_o):
    for slot in range(4):
        dn = dot_nt(dqkv0[slot], w0[...]) + dot_nt(dqkv1[slot], w1[...])
        (mine_o if slot < 2 else send_o)[slot % 2] = dn.astype(BF)


def input_grad_body(dn0, dn1, x0, x1, dh, gains, g0_o, g1_o):
    size = x0.shape[0]
    for slot, (x, g_o) in enumerate(((x0, g0_o), (x1, g1_o))):
        here = pl.ds(slot * size, size)
        normal, inv_sigma = normalize(x[...].astype(F32))
        dn = dn0[slot].astype(F32) + dn1[slot].astype(F32)
        g_o[...] = (dh[here, :] + normalize_back(dn, gains[0:1, :], normal, inv_sigma)).astype(BF)


def pick_body(order, source, out):
    def one(i, unused):
        out[i] = source[order[i]]
        return unused

    lax.fori_loop(0, source.shape[0], one, 0)


def pick(array, order):
    return call(pick_body, struct(array.shape, array.dtype), [], "pick", 1)(
        order, array, specs=[SMEM, VM]
    )


def pick_memory_body(order, source, out, digits_o):
    count, share = out.shape[:2]

    def one(i, unused):
        out[i] = source[order[i], 0:share, :]
        return unused

    lax.fori_loop(0, count, one, 0)
    digits_o[...] = source[order[order[count]], share:, :]


def spread_rows(block):
    return lax.all_to_all(block, "dp", split_axis=0, concat_axis=0, tiled=True)


def swap_chip(array):
    return lax.ppermute(array, "tensor", [(i, i ^ 2) for i in range(4)])


def swap_core(array):
    return lax.ppermute(array, "tensor", [(i, i ^ 1) for i in range(4)])


def pack_body(*refs):
    out = refs[-1]
    at = 0
    for ref in refs[:-1]:
        rows, lanes = ref.shape
        for begin in range(0, lanes, PAIR):
            out[at : at + rows, :] = ref[:, begin : begin + PAIR]
            at += rows


def pack(*arrays):
    rows = sum(a.size for a in arrays) // PAIR
    return call(pack_body, struct((rows, PAIR), arrays[0].dtype), [], "pack", 2)(
        *arrays, specs=[VM] * len(arrays)
    )


def swap_row(array, bit):
    return lax.ppermute(array, "dp", [(i, i ^ bit) for i in range(lax.axis_size("dp"))])


def halves(array, upper):
    half = array.shape[0] // 2
    low, high = array[:half], array[half:]
    return jnp.where(upper, high, low), jnp.where(upper, low, high).astype(BF)


def rest_groups():
    count = lax.axis_size("dp")
    return [[i for i in range(count) if i % 2 == part] for part in range(2)]


def rest_sends(arrays):
    group = lax.axis_size("dp") // 2
    width = arrays[0].shape[1]
    joint = jnp.concatenate([a.reshape(group, -1, width) for a in arrays], axis=1)
    me = lax.axis_index("dp") // 2

    def piece(index):
        return lax.dynamic_index_in_dim(joint, index, 0, keepdims=False)

    if group != 4:
        return piece(me), [joint.reshape(-1, width)]
    return piece(me), [piece(me ^ k) for k in (1, 2, 3)]


def rest_move(sends):
    if len(sends) == 3:
        return [swap_row(send, 2 * k) for k, send in zip((1, 2, 3), sends)]
    group = lax.axis_size("dp") // 2
    spread = lax.all_to_all(
        sends[0], "dp", split_axis=0, concat_axis=0, axis_index_groups=rest_groups(), tiled=True
    )
    return [spread.reshape(group, -1, spread.shape[1])]


def add_all(own, got):
    if got[0].ndim == own.ndim:
        return sum([g.astype(F32) for g in got], own.astype(F32))
    return jnp.sum(got[0].astype(F32), axis=0)


def rest_collect(piece):
    if lax.axis_size("dp") == 8:
        return [piece] + [swap_row(piece, 2 * k) for k in (1, 2, 3)]
    return [lax.all_gather(piece, "dp", axis=0, axis_index_groups=rest_groups(), tiled=True)]


def assemble_body(order, *refs):
    out = refs[-1]
    for index, ref in enumerate(refs[:-1]):
        out[order[index]] = ref[...]


def rest_assemble(pieces):
    if len(pieces) == 1:
        return pieces[0]
    me = lax.axis_index("dp") // 2
    order = (jnp.arange(4, dtype=jnp.int32) ^ me).astype(jnp.int32)
    return call(assemble_body, struct((4,) + pieces[0].shape, BF), [], "assemble", 1)(
        order, *pieces, specs=[SMEM] + [VM] * 4
    ).reshape(-1, pieces[0].shape[1])


def finish_one_body(flag, half, other, up_o, down_o, co_o):
    upper = flag[0] != 0
    low = jnp.where(upper, other[...], half[...]).astype(F32)
    high = jnp.where(upper, half[...], other[...]).astype(F32)
    wide, units = up_o.shape[0], down_o.shape[0]
    split = low.shape[0] - wide
    up_o[...] = low[:wide]
    down_o[0:split, :] = low[wide:]
    down_o[split:, :] = high[: units - split]
    co_o[...] = high[units - split :]


def finish_rest_body(flag, half, other, cq_o, so_o, kv_o, qkv_o, gain_o, two_s):
    upper = flag[0] != 0
    group = half.shape[0]
    two, three = two_s.shape[0] // (2 * group), qkv_o.shape[0] // (2 * group)
    gain = jnp.zeros(gain_o.shape, F32)
    for index in range(group):
        low = jnp.where(upper, other[index], half[index]).astype(F32)
        high = jnp.where(upper, half[index], other[index]).astype(F32)
        for at, piece in ((index, low), (group + index, high)):
            two_s[at * two : (at + 1) * two, :] = piece[0:two]
            qkv_o[at * three : (at + 1) * three, :] = piece[two : two + three]
            gain += piece[two + three :]
    wide = cq_o.shape[0]
    cq_o[...] = two_s[0:wide, :]
    for i in range(wide // PAIR):
        so_o[:, i * PAIR : (i + 1) * PAIR] = two_s[wide + i * PAIR : wide + (i + 1) * PAIR, :]
    kv_o[pl.ds(0, wide, stride=2), :] = two_s[2 * wide : 3 * wide, :]
    kv_o[pl.ds(1, wide, stride=2), :] = two_s[3 * wide :, :]
    gain_o[...] = gain


def on_device(
    x_first,
    x_second,
    memory,
    cot_first,
    cot_second,
    seg_ids,
    lengths,
    perm,
    inverse,
    gains,
    w_self_qkv,
    w_self_out,
    w_cross_q,
    w_cross_kv,
    w_cross_out,
    w_up,
    w_down,
):
    length = seg_ids.shape[2]
    size = x_first.shape[1]
    wide = x_first.shape[2]
    width = w_self_out.shape[0]
    units = w_up.shape[1]
    mine = 2 * size
    heads = 2 * width
    me = lax.axis_index("tensor")
    row = lax.axis_index("dp")
    rows = perm.shape[0]
    share = size // rows
    first_step = me < 2
    upper = (row & 1) != 0

    def both(one, two):
        return jnp.where(first_step, one, two)

    def stage(**values):
        return lax.optimization_barrier(values)

    pair_array = struct((2, length, PAIR), BF)
    out_half = struct((2, size, heads), BF)
    lse_array = struct((2, 2, length), F32)
    limits = [pltpu.VMEM((1, length), jnp.int32), pltpu.VMEM((1, length), jnp.int32)]
    def forward_scratch(key_block):
        return [
            pltpu.VMEM((2, length + key_block - ALIGN, PAIR), BF),
            pltpu.VMEM((2, PAIR, length + key_block - ALIGN), BF),
            pltpu.VMEM((length, heads), BF),
        ] + limits

    whole = pl.BlockSpec(memory_space=pltpu.VMEM)

    def part_of(rows_of_block, index):
        return pl.BlockSpec((rows_of_block, PAIR), lambda i: (index, 0))

    x_first, x_second, memory = x_first[0], x_second[0], memory[0]
    x_got = swap_chip(both(x_second, x_first))
    wqkv_own = w_self_qkv.reshape(wide, -1)
    wqkv_got = swap_chip(wqkv_own)
    x_own = both(x_first, x_second)
    place = jnp.arange(length, dtype=jnp.int32)
    meta = jnp.where(place[None, :] < lengths[0][:, None], seg_ids[0], DOCS)
    docs = jnp.arange(DOCS + 2, dtype=jnp.int32)
    cuts = jnp.sum((meta[:, None, :] < docs[None, :, None]).astype(jnp.int32), axis=-1).reshape(-1)
    digits = jnp.stack([cuts // 64, cuts % 64]).astype(BF)
    digits = jnp.pad(digits, ((0, 14), (0, wide - cuts.shape[0])))
    payload = jnp.concatenate(
        [memory.reshape(rows, share, wide), jnp.broadcast_to(digits[None], (rows, 16, wide))], axis=1
    )
    x_sib0 = swap_core(x_own)
    pack_a = pack(w_self_out, w_cross_q, w_cross_kv.reshape(wide, -1), w_cross_out)
    pack_b = pack(w_up, w_down)
    spread = spread_rows(payload.reshape(-1, wide)).reshape(payload.shape)
    cot_own = both(cot_first[0], cot_second[0])
    cot_send = both(cot_second[0], cot_first[0])
    x_sib1 = swap_core(x_got)
    s = stage(
        x_got=x_got,
        x_sib1=x_sib1,
        wqkv_own=wqkv_own,
        wqkv_got=wqkv_got,
        pack_a=pack_a,
        pack_b=pack_b,
        cot_own=cot_own,
        cot_send=cot_send,
        x_sib0=x_sib0,
        cuts=cuts,
        memory=memory,
    )
    pack_a, pack_b, cot_own, cot_send = [s[n] for n in ("pack_a", "pack_b", "cot_own", "cot_send")]
    x_sib0, cuts, memory = s["x_sib0"], s["cuts"], s["memory"]
    x_got, x_sib1, wqkv_own, wqkv_got = [s[n] for n in ("x_got", "x_sib1", "wqkv_own", "wqkv_got")]
    picked, digits = call(
        pick_memory_body,
        (struct((rows, share, wide), BF), struct((16, wide), BF)),
        [],
        "pick_memory",
        2,
    )(jnp.concatenate([perm, row[None].astype(jnp.int32)]), spread, specs=[SMEM, VM])
    digits = digits[:2, : cuts.shape[0]].astype(jnp.int32)
    cuts = both(digits[0] * 64 + digits[1], cuts)
    places = jnp.stack([me, me ^ 2, me ^ 1, me ^ 3]).astype(jnp.int32)
    s = stage(
        scalars=jnp.concatenate([cuts, places]),
        x0=x_own,
        x1=x_got,
        x2=x_sib0,
        x3=x_sib1,
        w0=wqkv_own,
        w1=wqkv_got,
        picked=picked,
        pack_a=pack_a,
        pack_b=pack_b,
        cot_own=cot_own,
        cot_send=cot_send,
        memory=memory,
    )
    scalars = s["scalars"]
    xs = (s["x0"], s["x1"], s["x2"], s["x3"])
    wqkv = (s["w0"], s["w1"])
    memory = s["memory"]

    memory_one = spread_rows(picked.reshape(memory.shape))
    q, k, v, a_mine, a_send, lse = call(
        self_forward_body,
        (pair_array, pair_array, pair_array, out_half, out_half, lse_array),
        forward_scratch(SELF_BK),
        "self_forward",
        4,
    )(scalars, *xs, gains, *wqkv, specs=[SMEM] + [VM] * 7)
    pack_a, pack_b = s["pack_a"], s["pack_b"]
    s = stage(
        q=q,
        k=k,
        v=v,
        a_mine=a_mine,
        a_send=a_send,
        lse=lse,
        memory_one=memory_one,
        a_got=swap_chip(pack_a),
        cot_got=swap_chip(s["cot_send"]),
        pack_a2=swap_core(pack_a),
        pack_b2=swap_core(pack_b),
    )
    q, k, v, a_mine, a_send, lse = [s[n] for n in ("q", "k", "v", "a_mine", "a_send", "lse")]
    pack_a1, pack_a2, pack_b2, cot_got = s["a_got"], s["pack_a2"], s["pack_b2"], s["cot_got"]
    memory_one = s["memory_one"]
    m_got = swap_chip(both(memory, memory_one))
    s = stage(
        a_got=swap_core(a_send),
        pack_a3=swap_core(pack_a1),
        m_own=both(memory_one, memory),
    )
    a_got, m_own = s["a_got"], s["m_own"]
    packs_a = (pack_a, pack_a1, pack_a2, s["pack_a3"])

    so_cq = part_of(2 * wide, 0)
    h1, cq_mine, cq_send = call(
        after_self_body,
        (struct((mine, wide), F32), struct((mine, heads), BF), struct((mine, heads), BF)),
        [],
        "after_self",
        6,
        (1,),
    )(
        *xs[:2], a_mine, a_got, *packs_a, gains, specs=[whole] * 4 + [so_cq] * 4 + [whole]
    )
    h1, m_got = lax.optimization_barrier((h1, m_got))
    s = stage(
        h1=h1,
        cq_mine=cq_mine,
        cq_got=swap_core(cq_send),
        m1=m_got,
        m2=swap_core(m_own),
        m3=swap_core(m_got),
        pack_b=pack_b,
    )
    h1, cq_mine, cq_got, pack_b = s["h1"], s["cq_mine"], s["cq_got"], s["pack_b"]
    ms = (m_own, s["m1"], s["m2"], s["m3"])

    kv = part_of(2 * wide, 1)
    cq, ck, cv, b_mine, b_send, lse_b = call(
        cross_forward_body,
        (pair_array, pair_array, pair_array, out_half, out_half, lse_array),
        forward_scratch(CROSS_BK),
        "cross_forward",
        24,
        (1,),
    )(
        scalars,
        cq_mine,
        cq_got,
        *ms,
        pack_a,
        pack_a1,
        specs=[SMEM] + [whole] * 6 + [kv] * 2,
    )
    s = stage(
        cq=cq,
        ck=ck,
        cv=cv,
        b_mine=b_mine,
        b_send=b_send,
        lse_b=lse_b,
        pack_b1=swap_chip(pack_b),
    )
    cq, ck, cv, b_mine, b_send, lse_b = [
        s[n] for n in ("cq", "ck", "cv", "b_mine", "b_send", "lse_b")
    ]
    pack_b1 = s["pack_b1"]
    s = stage(b_got=swap_core(b_send), pack_b3=swap_core(pack_b1))

    co = part_of(wide, 4)
    rows_one = wide + units + width
    (
        y_own, y_send, dh2, db_mine, db_send, one_keep, one_give, gain_three,
    ) = call(
        middle_body,
        (
            struct((size, wide), BF),
            struct((size, wide), BF),
            struct((mine, wide), F32),
            struct((mine, heads), BF),
            struct((mine, heads), BF),
            struct((2, rows_one, wide), BF),
            struct((2, rows_one, wide), BF),
            struct((8, wide), F32),
        ),
        [
            pltpu.VMEM((mine, wide), F32),
            pltpu.VMEM((mine, wide), BF),
            pltpu.VMEM((mine, wide), BF),
            pltpu.VMEM((mine, wide), F32),
            pltpu.VMEM((mine, wide), F32),
        ],
        "middle",
        25,
        (1,),
    )(
        scalars,
        h1,
        b_mine,
        s["b_got"],
        *packs_a,
        pack_b,
        pack_b1,
        pack_b2,
        s["pack_b3"],
        gains,
        cot_own,
        cot_got,
        specs=[SMEM] + [whole] * 3 + [co] * 4 + [whole] * 7,
    )

    def over_core(keep, got):
        own = keep[0].astype(F32) + got[0].astype(F32)
        other = keep[1].astype(F32) + got[1].astype(F32)
        return own, other.astype(BF)

    one_own, one_send = over_core(one_keep, swap_core(one_give))
    s = stage(
        y_own=y_own,
        y_send=y_send,
        dh2=dh2,
        db_mine=db_mine,
        db_got=swap_core(db_send),
        one_own=one_own,
        one_send=one_send,
        gain_three=gain_three,
    )
    y_own, y_send, dh2, one_own = s["y_own"], s["y_send"], s["dh2"], s["one_own"]
    gain_three = s["gain_three"]

    backward_scratch = [
        pltpu.VMEM((2, length + BK - ALIGN, PAIR), BF),
        pltpu.VMEM((2, PAIR, length + BK - ALIGN), BF),
        pltpu.VMEM((2, length + BK - ALIGN, PAIR), BF),
        pltpu.VMEM((2, length, PAIR), BF),
        pltpu.VMEM((2, length, PAIR), BF),
        pltpu.VMEM((2, length, PAIR), BF),
        pltpu.VMEM((2, length + BK - ALIGN, PAIR), F32),
        pltpu.VMEM((2, length + BK - ALIGN, PAIR), F32),
    ] + limits
    dcq_mine, dcq_send, dck, dcv = call(
        cross_backward_body,
        (out_half, out_half, pair_array, pair_array),
        backward_scratch,
        "cross_backward",
        27,
    )(
        scalars, cq, ck, cv, b_mine, b_send, lse_b, s["db_mine"], s["db_got"],
        specs=[SMEM] + [VM] * 8,
    )
    s = stage(
        dcq_mine=dcq_mine,
        dcq_send=dcq_send,
        dck=dck,
        dcv=dcv,
        one_got=swap_chip(s["one_send"]),
        one_own=one_own,
    )
    dcq_mine = s["dcq_mine"]
    one_keep, one_send = halves(s["one_own"] + s["one_got"].astype(F32), upper)
    one_got = swap_row(one_send, 1)
    dm_mine, dm_send, keep_kv, give_kv = call(
        memory_back_body,
        (
            struct((2, size, wide), BF),
            struct((2, size, wide), BF),
            struct((2 * wide, width), BF),
            struct((2 * wide, width), BF),
        ),
        [],
        "memory_back",
        6,
        (1,),
    )(
        scalars, s["dck"], s["dcv"], *ms, pack_a, pack_a1, specs=[SMEM] + [whole] * 6 + [kv] * 2
    )
    dm_core = swap_core(dm_send)
    dm_own, dm_other = [
        (dm_mine[i].astype(F32) + dm_core[i].astype(F32)).astype(BF) for i in range(2)
    ]
    s = stage(
        dcq_got=swap_core(s["dcq_send"]),
        one_keep=one_keep,
        dm_own=dm_own,
        dm_other=dm_other,
        keep_kv=keep_kv,
        give_kv=give_kv,
    )
    one_keep, dm_own, keep_kv, give_kv = [s[n] for n in ("one_keep", "dm_own", "keep_kv", "give_kv")]

    dh1, da_mine, da_send, keep_two, give_two, gain_two = call(
        between_body,
        (
            struct((mine, wide), F32),
            struct((mine, heads), BF),
            struct((mine, heads), BF),
            struct((2, 2 * wide, width), BF),
            struct((2, 2 * wide, width), BF),
            struct((8, wide), F32),
        ),
        [],
        "between",
        3,
        (1,),
    )(
        h1, dh2, a_mine, a_got, dcq_mine, s["dcq_got"], *packs_a, gains,
        specs=[whole] * 6 + [so_cq] * 4 + [whole],
    )
    s = stage(
        dh1=dh1,
        da_mine=da_mine,
        da_send=da_send,
        keep_two=keep_two,
        give_two=give_two,
        gain_two=gain_two,
        one_got=one_got,
        one_keep=one_keep,
        dm_got=swap_chip(s["dm_other"]),
        dm_own=dm_own,
    )
    dh1, da_mine, gain_two = s["dh1"], s["da_mine"], s["gain_two"]
    one_own, one_sends = rest_sends([(s["one_keep"] + s["one_got"].astype(F32)).astype(BF)])
    two_own, two_send = over_core(s["keep_two"], swap_core(s["give_two"]))
    s = stage(
        da_got=swap_core(s["da_send"]),
        dm_one=both(s["dm_own"], s["dm_got"]),
        dm_two=both(s["dm_got"], s["dm_own"]),
        two_own=two_own,
        two_send=jnp.concatenate([two_send, give_kv], axis=0),
        y_send=y_send,
        one_own=one_own,
        one_sends=one_sends,
    )
    two_own, dm_two, one_own = s["two_own"], s["dm_two"], s["one_own"]

    qkv_rows = struct((4, size, 3 * PAIR), BF)
    dqkv0, dqkv1 = call(
        self_backward_body, (qkv_rows, qkv_rows), backward_scratch, "self_backward", 32
    )(
        scalars, q, k, v, a_mine, a_send, lse, da_mine, s["da_got"], specs=[SMEM] + [VM] * 8
    )
    s = stage(
        dqkv0=dqkv0,
        dqkv1=dqkv1,
        two_got=swap_chip(s["two_send"]),
        two_own=two_own,
        y_got=swap_chip(s["y_send"]),
        y_own=y_own,
        dm_spread=spread_rows(s["dm_one"]),
        dm_two=dm_two,
        keep_kv=keep_kv,
        one_own=one_own,
        one_got=rest_move(s["one_sends"]),
    )
    dqkv0, dqkv1, dm_two = s["dqkv0"], s["dqkv1"], s["dm_two"]
    two_total = jnp.concatenate(
        [
            s["two_own"] + s["two_got"][: 2 * wide].astype(F32),
            s["keep_kv"].astype(F32) + s["two_got"][2 * wide :].astype(F32),
        ],
        axis=0,
    )
    two_keep, two_send = halves(two_total, upper)
    s = stage(
        two_keep=two_keep,
        two_send=two_send,
        dm_picked=pick(s["dm_spread"].reshape(rows, -1, wide), inverse),
        y_own=s["y_own"],
        y_got=s["y_got"],
        one_piece=add_all(s["one_own"], s["one_got"]).astype(BF),
    )
    two_keep, y_own, y_got = s["two_keep"], s["y_own"], s["y_got"]

    dm_back = spread_rows(s["dm_picked"].reshape(memory.shape))
    one_pieces = rest_collect(s["one_piece"])
    qkv_gradient = (3 * wide, width)
    gain_row = struct((8, wide), F32)
    keep_qkv, give_qkv, gain_all = call(
        qkv_grad_body,
        (struct(qkv_gradient, F32), struct(qkv_gradient, BF), gain_row),
        [],
        "qkv_grad",
        8,
    )(dqkv0, dqkv1, *xs, gains, *wqkv, gain_two, gain_three, specs=[VM] * 11)
    s = stage(
        keep_qkv=keep_qkv,
        give_qkv=give_qkv,
        gain_all=gain_all,
        two_got=swap_row(s["two_send"], 1),
        two_keep=two_keep,
        dqkv0=dqkv0,
        dqkv1=dqkv1,
    )
    keep_qkv, gain_all = s["keep_qkv"], s["gain_all"]
    dqkv0, dqkv1 = s["dqkv0"], s["dqkv1"]

    qkv_got = swap_chip(s["give_qkv"])
    dn_mine, dn_send = call(
        back_to_input_body,
        (struct((2, size, wide), BF), struct((2, size, wide), BF)),
        [],
        "back_to_input",
        4,
    )(dqkv0, dqkv1, *wqkv, specs=[VM] * 4)
    s = stage(
        keep_qkv=keep_qkv,
        gain_all=gain_all,
        qkv_got=qkv_got,
        dn_mine=dn_mine,
        dn_send=dn_send,
        two_got=s["two_got"],
        two_keep=s["two_keep"],
        dm_back=dm_back,
        one_pieces=one_pieces,
    )
    dn_mine, dm_back, one_pieces = s["dn_mine"], s["dm_back"], s["one_pieces"]
    three_keep, three_send = halves(s["keep_qkv"] + s["qkv_got"].astype(F32), upper)
    s = stage(
        three_keep=three_keep,
        three_send=three_send,
        two_half=(s["two_keep"] + s["two_got"].astype(F32)).astype(BF),
        gain_all=s["gain_all"],
        dn_got=swap_core(s["dn_send"]),
    )
    two_half = s["two_half"]

    grad_own, grad_send = call(
        input_grad_body,
        (struct((size, wide), BF), struct((size, wide), BF)),
        [],
        "input_grad",
        5,
    )(dn_mine, s["dn_got"], *xs[:2], dh1, gains, specs=[VM] * 6)
    s = stage(
        three_got=swap_row(s["three_send"], 1),
        three_keep=s["three_keep"],
        gain_all=s["gain_all"] + swap_core(s["gain_all"]),
        grad_own=grad_own,
        grad_send=grad_send,
        y_own=y_own,
        y_got=y_got,
        dm_two=dm_two,
        dm_back=dm_back,
        one_pieces=one_pieces,
    )
    one_pieces, grad_own = s["one_pieces"], s["grad_own"]
    three_half = (s["three_keep"] + s["three_got"].astype(F32)).astype(BF)
    share_two, share_three = two_half.shape[0], three_half.shape[0]
    last_own, last_sends = rest_sends([two_half, three_half])

    y_first = both(s["y_own"], s["y_got"])
    y_second = both(s["y_got"], s["y_own"])
    grad_memory = s["dm_two"].astype(F32) + s["dm_back"].astype(F32)
    s = stage(
        last_own=last_own,
        last_got=rest_move(last_sends),
        gain_all=s["gain_all"] + swap_chip(s["gain_all"]),
        grad_own=grad_own,
        grad_send=s["grad_send"],
        one_half=rest_assemble(one_pieces),
        y_first=y_first,
        y_second=y_second,
        grad_memory=grad_memory,
    )
    one_half, grad_own = s["one_half"], s["grad_own"]
    y_first, y_second, grad_memory = s["y_first"], s["y_second"], s["grad_memory"]
    grad_got = swap_chip(s["grad_send"])
    one_other = swap_row(one_half, 1)
    gain_rows = 8 * wide // width
    last = jnp.concatenate(
        [
            add_all(s["last_own"], s["last_got"]).astype(BF),
            s["gain_all"].astype(BF).reshape(gain_rows, width),
        ],
        axis=0,
    )
    s = stage(pieces=rest_collect(last), one_half=one_half, one_other=one_other)
    half = rest_assemble(s["pieces"])
    other = swap_row(half, 1)
    flag = (row & 1)[None].astype(jnp.int32)
    grad_up, grad_down, grad_cross_out = call(
        finish_one_body,
        (struct((wide, units), F32), struct((units, wide), F32), struct((width, wide), F32)),
        [],
        "finish_one",
        2,
    )(flag, s["one_half"], s["one_other"], specs=[SMEM, VM, VM])
    slab = struct((wide, width), F32)
    group = (rows // 2, last.shape[0], width)
    grad_cross_q, grad_self_out, grad_kv, grad_qkv, gain_total = call(
        finish_rest_body,
        (
            slab,
            struct((width, wide), F32),
            struct((2 * wide, width), F32),
            struct((3 * wide, width), F32),
            struct((gain_rows, width), F32),
        ),
        [pltpu.VMEM((4 * wide, width), F32)],
        "finish_rest",
        2,
    )(flag, half.reshape(group), other.reshape(group), specs=[SMEM, VM, VM])
    grad_kv = grad_kv.reshape(wide, 2, width)
    grad_qkv = grad_qkv.reshape(3, wide, width).transpose(1, 0, 2)
    gain_total = gain_total.reshape(-1, wide)[:3]
    grad_gains = lax.dynamic_slice(gain_total, (0, me * width), (3, width))
    grad_first = both(grad_own, grad_got)
    return (
        y_first[None],
        y_second[None],
        grad_first[None],
        grad_memory[None],
        grad_gains,
        grad_qkv,
        grad_self_out,
        grad_cross_q,
        grad_kv,
        grad_cross_out,
        grad_up,
        grad_down,
    )


def solution(mesh):
    in_specs = (
        P("dp", "tensor", None),
        P("dp", "tensor", None),
        P("dp", "tensor", None),
        P("dp", "tensor", None),
        P("dp", "tensor", None),
        P("dp", None, None),
        P("dp", None),
        P(),
        P(),
        P(),
        P(None, None, "tensor"),
        P("tensor", None),
        P(None, "tensor"),
        P(None, None, "tensor"),
        P("tensor", None),
        P(None, "tensor"),
        P("tensor", None),
    )
    out_specs = (
        P("dp", "tensor", None),
        P("dp", "tensor", None),
        P("dp", "tensor", None),
        P("dp", "tensor", None),
        P(None, "tensor"),
        P(None, None, "tensor"),
        P("tensor", None),
        P(None, "tensor"),
        P(None, None, "tensor"),
        P("tensor", None),
        P(None, "tensor"),
        P("tensor", None),
    )
    return jax.shard_map(
        on_device, mesh=mesh, in_specs=in_specs, out_specs=out_specs, check_vma=False
    )
```

```python
import math
import types

import jax
import jax.numpy as jnp
from jax import lax
from jax.experimental import pallas as pl
from jax.experimental.pallas import tpu as pltpu
from jax.sharding import PartitionSpec as P

HEAD_DIM = 64
EPSILON = 1e-05
NEG_FILL = -1e30
DOCS = 16
PAIR = 2 * HEAD_DIM
BQ = 256
BK = 256
SELF_BK = 640
CROSS_BK = 512
ALIGN = 128
BF = jnp.bfloat16
F32 = jnp.float32
VMEM_BYTES = 56 * 1024 * 1024
LOG2E = 1.4426950408889634

ANY = pl.BlockSpec(memory_space=pl.ANY)
SMEM = pl.BlockSpec(memory_space=pltpu.SMEM)
VM = pl.BlockSpec(memory_space=pltpu.VMEM)


def dot(a, b):
    return lax.dot_general(a, b, (((1,), (0,)), ((), ())), preferred_element_type=F32)


def dot_nt(a, b):
    return lax.dot_general(a, b, (((1,), (1,)), ((), ())), preferred_element_type=F32)


def dot_tn(a, b):
    return lax.dot_general(a, b, (((0,), (0,)), ((), ())), preferred_element_type=F32)


def normalize(hidden):
    centred = hidden - jnp.mean(hidden, axis=-1, keepdims=True)
    inv_sigma = lax.rsqrt(jnp.mean(centred * centred, axis=-1, keepdims=True) + EPSILON)
    return centred * inv_sigma, inv_sigma


def normalize_back(grad_scaled, gain, normal, inv_sigma):
    grad_normal = grad_scaled * gain
    first_mean = jnp.mean(grad_normal, axis=-1, keepdims=True)
    second_mean = jnp.mean(grad_normal * normal, axis=-1, keepdims=True)
    return inv_sigma * (grad_normal - first_mean - normal * second_mean)


def call(body, outs, scratch, name, cost, grid=()):
    def run(*args, specs):
        moved = sum(a.size * a.dtype.itemsize for a in args)
        return pl.pallas_call(
            body,
            out_shape=outs,
            grid=grid,
            in_specs=specs,
            out_specs=jax.tree.map(lambda _: VM, outs),
            scratch_shapes=scratch,
            compiler_params=pltpu.CompilerParams(vmem_limit_bytes=VMEM_BYTES),
            cost_estimate=pl.CostEstimate(flops=int(cost * 1.15e9), bytes_accessed=moved, transcendentals=0),
            name=name,
        )(*args)

    return run


def struct(shape, dtype):
    return jax.ShapeDtypeStruct(shape, dtype)


QUERY_AT, KEY_AT, PLACE_AT = 0, DOCS + 2, 2 * (DOCS + 2)
ROW_AT = PLACE_AT + 4


def key_limits(scalars, key_at, length):
    place = lax.broadcasted_iota(jnp.int32, (1, length), 1)
    first = jnp.full((1, length), scalars[key_at], jnp.int32)
    after = jnp.full((1, length), scalars[key_at + 1], jnp.int32)
    for doc in range(1, DOCS + 1):
        inside = place >= scalars[QUERY_AT + doc]
        first = jnp.where(inside, scalars[key_at + doc], first)
        after = jnp.where(inside, scalars[key_at + doc + 1], after)
    return first, after


def window(scalars, key_at, begin, size):
    low = scalars[key_at]
    high = scalars[key_at + 1]
    for doc in range(1, DOCS + 1):
        low = jnp.where(begin >= scalars[QUERY_AT + doc], scalars[key_at + doc], low)
        high = jnp.where(
            begin + (BQ - 1) >= scalars[QUERY_AT + doc], scalars[key_at + doc + 1], high
        )
    low = (low // ALIGN) * ALIGN
    return low, (high - low + (size - 1)) // size


def two_heads(block):
    lane = lax.broadcasted_iota(jnp.int32, block.shape, 1)
    zero = jnp.zeros_like(block)
    return jnp.concatenate(
        [jnp.where(lane < HEAD_DIM, block, zero), jnp.where(lane >= HEAD_DIM, block, zero)], axis=0
    )


def attend_forward(scalars, key_at, key_block, pairs, q_s, k_s, vt_s, o_s, lse_s, first_s, after_s):
    length = q_s.shape[1]
    scale = LOG2E / math.sqrt(HEAD_DIM)
    first, after = key_limits(scalars, key_at, length)
    first_s[...] = first
    after_s[...] = after
    rows = lax.broadcasted_iota(jnp.int32, (key_block, BQ), 0)

    def one_block(index, unused):
        begin = pl.multiple_of(index * BQ, BQ)
        low, count = window(scalars, key_at, begin, key_block)
        first_row = first_s[:, pl.ds(begin, BQ)]
        after_row = after_s[:, pl.ds(begin, BQ)]
        queries = [two_heads(q_s[pair, pl.ds(begin, BQ), :]) for pair in pairs]

        def step(turn, carry):
            start = pl.multiple_of(low + turn * key_block, ALIGN)
            allowed = (rows >= first_row - start) & (rows < after_row - start)
            allowed = jnp.concatenate([allowed, allowed], axis=1)
            results = []
            for pair, query, (top, total, out) in zip(pairs, queries, carry):
                scores = dot_nt(k_s[pair, pl.ds(start, key_block), :], query) * scale
                scores = jnp.where(allowed, scores, NEG_FILL)
                new_top = jnp.maximum(top, jnp.max(scores, axis=0, keepdims=True))
                shrink = jnp.exp2(top - new_top)
                raised = jnp.exp2(scores - new_top)
                total = total * shrink + jnp.sum(raised, axis=0, keepdims=True)
                low_probs = raised.astype(BF)
                value = vt_s[pair, :, pl.ds(start, key_block)]
                out = [
                    out[0] * shrink[:, :BQ] + dot(value[:HEAD_DIM], low_probs[:, :BQ]),
                    out[1] * shrink[:, BQ:] + dot(value[HEAD_DIM:], low_probs[:, BQ:]),
                ]
                results.append((new_top, total, out))
            return results

        zero = jnp.zeros((HEAD_DIM, BQ), F32)
        fresh = (jnp.full((1, 2 * BQ), NEG_FILL, F32), jnp.zeros((1, 2 * BQ), F32), [zero, zero])
        results = lax.fori_loop(0, count, step, [fresh for unused_pair in pairs])
        for pair, (top, total, out) in zip(pairs, results):
            inverse = 1.0 / total
            out = jnp.concatenate([out[0] * inverse[:, :BQ], out[1] * inverse[:, BQ:]], axis=0)
            o_s[pl.ds(begin, BQ), pair * PAIR : (pair + 1) * PAIR] = out.T.astype(BF)
            log_total = top + jnp.log2(total)
            lse_s[pair, 0:1, pl.ds(begin, BQ)] = log_total[:, :BQ]
            lse_s[pair, 1:2, pl.ds(begin, BQ)] = log_total[:, BQ:]
        return unused

    lax.fori_loop(0, length // BQ, one_block, 0)


def attend_backward(
    scalars, key_at, pairs, q_s, k_s, kt_s, v_s, o_s, do_s, lse_s, dq_s, dk_s, dv_s, first_s, after_s
):
    length = q_s.shape[1]
    scale = LOG2E / math.sqrt(HEAD_DIM)
    first, after = key_limits(scalars, key_at, length)
    first_s[...] = first
    after_s[...] = after
    rows = lax.broadcasted_iota(jnp.int32, (BK, BQ), 0)
    dk_s[...] = jnp.zeros_like(dk_s)
    dv_s[...] = jnp.zeros_like(dv_s)
    ones = jnp.ones((8, PAIR), F32)

    def one_block(index, unused):
        begin = pl.multiple_of(index * BQ, BQ)
        low, count = window(scalars, key_at, begin, BK)
        first_row = first_s[:, pl.ds(begin, BQ)]
        after_row = after_s[:, pl.ds(begin, BQ)]
        fixed = []
        for pair in pairs:
            query = two_heads(q_s[pair, pl.ds(begin, BQ), :])
            grad = two_heads(do_s[pair, pl.ds(begin, BQ), :])
            out = o_s[pair, pl.ds(begin, BQ), :].astype(F32)
            product = grad.astype(F32) * jnp.concatenate([out, out], axis=0)
            centre = lax.dot_general(
                ones,
                product,
                (((1,), (1,)), ((), ())),
                precision=lax.Precision.HIGHEST,
                preferred_element_type=F32,
            )[:1]
            log_total = jnp.concatenate(
                [lse_s[pair, 0:1, pl.ds(begin, BQ)], lse_s[pair, 1:2, pl.ds(begin, BQ)]], axis=1
            )
            fixed.append((query, grad, centre, log_total))

        def step(turn, carry):
            start = pl.multiple_of(low + turn * BK, ALIGN)
            allowed = (rows >= first_row - start) & (rows < after_row - start)
            allowed = jnp.concatenate([allowed, allowed], axis=1)
            results = []
            for pair, (query, grad, centre, log_total), dq in zip(pairs, fixed, carry):
                scores = dot_nt(k_s[pair, pl.ds(start, BK), :], query) * scale
                probs = jnp.exp2(jnp.where(allowed, scores, NEG_FILL) - log_total)
                dprobs = dot_nt(v_s[pair, pl.ds(start, BK), :], grad)
                dscores = (probs * (dprobs - centre)).astype(BF)
                dv_s[pair, pl.ds(start, BK), :] += dot(probs.astype(BF), grad)
                dk_s[pair, pl.ds(start, BK), :] += dot(dscores, query)
                kt = kt_s[pair, :, pl.ds(start, BK)]
                results.append(
                    [
                        dq[0] + dot(kt[:HEAD_DIM], dscores[:, :BQ]),
                        dq[1] + dot(kt[HEAD_DIM:], dscores[:, BQ:]),
                    ]
                )
            return results

        zero = jnp.zeros((HEAD_DIM, BQ), F32)
        results = lax.fori_loop(0, count, step, [[zero, zero] for unused_pair in pairs])
        for pair, dq in zip(pairs, results):
            dq = jnp.concatenate(dq, axis=0) * (1.0 / math.sqrt(HEAD_DIM))
            dq_s[pair, pl.ds(begin, BQ), :] = dq.T.astype(BF)
        return unused

    lax.fori_loop(0, length // BQ, one_block, 0)


def block_of(scalars, slot, size):
    return pl.multiple_of(scalars[PLACE_AT + slot] * size, size)


def clear_padding(length, k_s, t_s, v_s=None):
    pairs, padded = k_s.shape[:2]
    extra = padded - length
    k_s[:, pl.ds(length, extra), :] = jnp.zeros((pairs, extra, PAIR), BF)
    t_s[:, :, pl.ds(length, extra)] = jnp.zeros((pairs, PAIR, extra), BF)
    if v_s is not None:
        v_s[:, pl.ds(length, extra), :] = jnp.zeros((pairs, extra, PAIR), BF)


def hand_out(scalars, o_s, mine_o, send_o):
    size = mine_o.shape[1]
    for slot in range(4):
        place = block_of(scalars, slot, size)
        (mine_o if slot < 2 else send_o)[slot % 2] = o_s[pl.ds(place, size), :]


def self_forward_body(
    scalars, x0, x1, x2, x3, gains, w0, w1, q_o, k_o, v_o, mine_o, send_o, lse_o, k_s, vt_s, o_s, first_s, after_s
):
    size = x0.shape[0]
    length = q_o.shape[1]
    gain = gains[0:1, :]
    clear_padding(length, k_s, vt_s)
    for slot, x in enumerate((x0, x1, x2, x3)):
        place = block_of(scalars, slot, size)
        normal, unused = normalize(x[...].astype(F32))
        normed = (normal * gain).astype(BF)
        for pair, w in enumerate((w0, w1)):
            packed = dot(normed, w[...]).astype(BF)
            keys, values = packed[:, PAIR : 2 * PAIR], packed[:, 2 * PAIR :]
            q_o[pair, pl.ds(place, size), :] = packed[:, :PAIR]
            k_s[pair, pl.ds(place, size), :] = keys
            k_o[pair, pl.ds(place, size), :] = keys
            v_o[pair, pl.ds(place, size), :] = values
            vt_s[pair, :, pl.ds(place, size)] = values.T
    attend_forward(scalars, QUERY_AT, SELF_BK, (0, 1), q_o, k_s, vt_s, o_s, lse_o, first_s, after_s)
    hand_out(scalars, o_s, mine_o, send_o)


def cross_forward_body(
    scalars, cq0, cq1, m0, m1, m2, m3, w0, w1, q_o, k_o, v_o, mine_o, send_o, lse_o, k_s, vt_s, o_s, first_s, after_s
):
    size = m0.shape[0]
    length = q_o.shape[1]
    clear_padding(length, k_s, vt_s)
    for slot, memory in enumerate((m0, m1, m2, m3)):
        place = block_of(scalars, slot, size)
        source = cq0 if slot < 2 else cq1
        for pair, w in enumerate((w0, w1)):
            packed = dot(memory[...], wide_rows(w, 0, memory.shape[1], 2)).astype(BF)
            keys, values = packed[:, :PAIR], packed[:, PAIR:]
            k_s[pair, pl.ds(place, size), :] = keys
            k_o[pair, pl.ds(place, size), :] = keys
            v_o[pair, pl.ds(place, size), :] = values
            vt_s[pair, :, pl.ds(place, size)] = values.T
            q_o[pair, pl.ds(place, size), :] = source[
                pl.ds((slot % 2) * size, size), pair * PAIR : (pair + 1) * PAIR
            ]
    attend_forward(scalars, KEY_AT, CROSS_BK, (0, 1), q_o, k_s, vt_s, o_s, lse_o, first_s, after_s)
    hand_out(scalars, o_s, mine_o, send_o)


def load_backward(scalars, pairs, k, v, a0, a1, da0, da1, k_s, kt_s, v_s, o_s, do_s):
    size = a0.shape[1]
    length = k.shape[1]
    clear_padding(length, k_s, kt_s, v_s)
    for pair in range(pairs):
        k_s[pair, pl.ds(0, length), :] = k[pair]
        v_s[pair, pl.ds(0, length), :] = v[pair]
        lanes = slice(pair * PAIR, (pair + 1) * PAIR)
        for begin in range(0, length, 512):
            kt_s[pair, :, begin : begin + 512] = k[pair, begin : begin + 512, :].T
        for slot in range(4):
            place = block_of(scalars, slot, size)
            within = pl.ds((slot % 2) * size, size)
            do_s[pair, pl.ds(place, size), :] = (da0 if slot < 2 else da1)[within, lanes]
            o_s[pair, pl.ds(place, size), :] = (a0 if slot < 2 else a1)[slot % 2, :, lanes]


def cross_backward_body(
    scalars, q, k, v, a0, a1, lse, da0, da1, mine_o, send_o, dk_o, dv_o,
    k_s, kt_s, v_s, o_s, do_s, dq_s, dk_s, dv_s, first_s, after_s,
):
    size = a0.shape[1]
    length = k.shape[1]
    load_backward(scalars, 2, k, v, a0, a1, da0, da1, k_s, kt_s, v_s, o_s, do_s)
    attend_backward(
        scalars, KEY_AT, (0, 1), q, k_s, kt_s, v_s, o_s, do_s, lse, dq_s, dk_s, dv_s, first_s, after_s
    )
    for slot in range(4):
        place = block_of(scalars, slot, size)
        for pair in range(2):
            (mine_o if slot < 2 else send_o)[slot % 2, :, pair * PAIR : (pair + 1) * PAIR] = dq_s[
                pair, pl.ds(place, size), :
            ]
    dk_o[...] = (dk_s[:, pl.ds(0, length), :] * (1.0 / math.sqrt(HEAD_DIM))).astype(BF)
    dv_o[...] = dv_s[:, pl.ds(0, length), :].astype(BF)


def self_backward_body(
    scalars, q, k, v, a0, a1, lse, da0, da1, dqkv0_o, dqkv1_o,
    k_s, kt_s, v_s, o_s, do_s, dq_s, dk_s, dv_s, first_s, after_s,
):
    size = a0.shape[1]
    load_backward(scalars, 2, k, v, a0, a1, da0, da1, k_s, kt_s, v_s, o_s, do_s)
    attend_backward(
        scalars, QUERY_AT, (0, 1), q, k_s, kt_s, v_s, o_s, do_s, lse, dq_s, dk_s, dv_s, first_s, after_s
    )
    for pair, out in enumerate((dqkv0_o, dqkv1_o)):
        for slot in range(4):
            place = block_of(scalars, slot, size)
            out[slot, :, 0:PAIR] = dq_s[pair, pl.ds(place, size), :]
            out[slot, :, PAIR : 2 * PAIR] = (
                dk_s[pair, pl.ds(place, size), :] * (1.0 / math.sqrt(HEAD_DIM))
            ).astype(BF)
            out[slot, :, 2 * PAIR :] = dv_s[pair, pl.ds(place, size), :].astype(BF)


def wide_rows(ref, begin, rows, count):
    return jnp.concatenate(
        [ref[begin + i * rows : begin + (i + 1) * rows, :] for i in range(count)], axis=1
    )


def after_self_body(x0, x1, a0, a1, p0, p1, p2, p3, gains, h_o, cq0_o, cq1_o):
    size, wide = x0.shape
    packs = (p0, p1, p2, p3)
    w0, w1, w2, w3 = [wide_rows(p, 0, PAIR, wide // PAIR) for p in packs]
    u0, u1, u2, u3 = [p[wide : 2 * wide, :] for p in packs]
    for slot, x in enumerate((x0, x1)):
        here = pl.ds(slot * size, size)
        hidden = x[...].astype(F32)
        mine, other = a0[slot], a1[slot]
        width = w0.shape[0]
        hidden += dot(mine[:, :width], w0) + dot(mine[:, width:], w1)
        hidden += dot(other[:, :width], w2) + dot(other[:, width:], w3)
        h_o[here, :] = hidden
        normal, unused = normalize(hidden)
        normed = (normal * gains[1:2, :]).astype(BF)
        cq0_o[here, :] = jnp.concatenate([dot(normed, u0), dot(normed, u1)], axis=1).astype(BF)
        cq1_o[here, :] = jnp.concatenate([dot(normed, u2), dot(normed, u3)], axis=1).astype(BF)


GELU_C = math.sqrt(2.0 / math.pi)


def middle_body(
    scalars, h, a0, a1, p0, p1, p2, p3, ud0, ud1, ud2, ud3, gains, cot0, cot1,
    y0_o, y1_o, dh_o, da0_o, da1_o, keep_o, give_o, gain_o,
    h_s, n_s, g_s, acc_s, dn_s,
):
    size = cot0.shape[0]
    used = scalars[QUERY_AT + DOCS]
    wide = h.shape[1]
    width = PAIR
    units = ud0.shape[0] * PAIR // (2 * wide)
    w0, w1, w2, w3 = [wide_rows(p, 0, width, wide // PAIR) for p in (p0, p1, p2, p3)]
    for slot, cot in enumerate((cot0, cot1)):
        here = pl.ds(slot * size, size)
        mine, other = a0[slot], a1[slot]
        hidden = h[here, :] + dot(mine[:, :width], w0) + dot(mine[:, width:], w1)
        hidden += dot(other[:, :width], w2) + dot(other[:, width:], w3)
        h_s[here, :] = hidden
        normal, unused = normalize(hidden)
        n_s[here, :] = (normal * gains[2:3, :]).astype(BF)
        place = lax.broadcasted_iota(jnp.int32, (size, 1), 0) + scalars[PLACE_AT + slot] * size
        g_s[here, :] = jnp.where(place < used, cot[...].astype(F32), 0.0).astype(BF)
    acc_s[...] = jnp.zeros_like(acc_s)
    dn_s[...] = jnp.zeros_like(dn_s)
    for shard, ud in enumerate((ud0, ud1, ud2, ud3)):
        w_up = wide_rows(ud, 0, wide, units // PAIR)
        w_down = wide_rows(ud, wide * units // PAIR, units, wide // PAIR)
        grad_up = jnp.zeros(w_up.shape, F32)
        grad_down = jnp.zeros(w_down.shape, F32)
        for begin in range(0, 2 * size, size):
            here = pl.ds(begin, size)
            normed = n_s[here, :]
            grad = g_s[here, :]
            upper = dot(normed, w_up)
            square = upper * upper
            inner_arg = GELU_C * upper * (1.0 + 0.044715 * square)
            bent = jnp.tanh(inner_arg)
            half = 0.5 * (1.0 + bent)
            inner = (upper * half).astype(BF)
            slope = half + 0.5 * upper * (1.0 - bent * bent) * (GELU_C * (1.0 + 3.0 * 0.044715 * square))
            acc_s[here, :] += dot(inner, w_down)
            d_upper = (dot_nt(grad, w_down) * slope).astype(BF)
            dn_s[here, :] += dot_nt(d_upper, w_up)
            grad_up += dot_tn(normed, d_upper)
            grad_down += dot_tn(inner, grad)
        out = keep_o if shard < 2 else give_o
        out[shard % 2, 0:wide, :] = grad_up.astype(BF)
        out[shard % 2, wide : wide + units, :] = grad_down.astype(BF)
    gain_total = jnp.zeros((1, h_s.shape[1]), F32)
    grad_heads = [jnp.zeros((width, h_s.shape[1]), F32) for unused in range(4)]
    for slot, y_o in enumerate((y0_o, y1_o)):
        here = pl.ds(slot * size, size)
        hidden = h_s[here, :]
        y_o[...] = (hidden + acc_s[here, :]).astype(BF)
        normal, inv_sigma = normalize(hidden)
        dn = dn_s[here, :]
        gain_total += jnp.sum(dn * normal, axis=0, keepdims=True)
        dh = g_s[here, :].astype(F32) + normalize_back(dn, gains[2:3, :], normal, inv_sigma)
        dh_o[here, :] = dh
        low = dh.astype(BF)
        da0_o[here, :] = jnp.concatenate([dot_nt(low, w0), dot_nt(low, w1)], axis=1).astype(BF)
        da1_o[here, :] = jnp.concatenate([dot_nt(low, w2), dot_nt(low, w3)], axis=1).astype(BF)
        mine, other = a0[slot], a1[slot]
        parts = (mine[:, :width], mine[:, width:], other[:, :width], other[:, width:])
        grad_heads = [total + dot_tn(part, low) for total, part in zip(grad_heads, parts)]
    for shard in range(4):
        out = keep_o if shard < 2 else give_o
        out[shard % 2, wide + units : wide + units + width, :] = grad_heads[shard].astype(BF)
    gain_o[...] = jnp.broadcast_to(gain_total, gain_o.shape)


def between_body(
    h, dh2, a0, a1, dq0, dq1, p0, p1, p2, p3, gains,
    dh_o, da0_o, da1_o, keep_o, give_o, gain_o,
):
    size = a0.shape[1]
    width = PAIR
    wide = h.shape[1]
    packs = (p0, p1, p2, p3)
    w0, w1, w2, w3 = [wide_rows(p, 0, width, wide // PAIR) for p in packs]
    u0, u1, u2, u3 = [p[wide : 2 * wide, :] for p in packs]
    gain_total = jnp.zeros((1, wide), F32)
    grad_out = [jnp.zeros((width, wide), F32) for unused in range(4)]
    grad_query = [jnp.zeros((wide, width), F32) for unused in range(4)]
    for slot in range(2):
        here = pl.ds(slot * size, size)
        normal, inv_sigma = normalize(h[here, :])
        normed = (normal * gains[1:2, :]).astype(BF)
        mine, other = dq0[slot], dq1[slot]
        pieces = (mine[:, :width], mine[:, width:], other[:, :width], other[:, width:])
        dn = jnp.zeros((size, wide), F32)
        for piece, u in zip(pieces, (u0, u1, u2, u3)):
            dn += dot_nt(piece, u)
        grad_query = [total + dot_tn(normed, piece) for total, piece in zip(grad_query, pieces)]
        gain_total += jnp.sum(dn * normal, axis=0, keepdims=True)
        dh = dh2[here, :] + normalize_back(dn, gains[1:2, :], normal, inv_sigma)
        dh_o[here, :] = dh
        low = dh.astype(BF)
        da0_o[here, :] = jnp.concatenate([dot_nt(low, w0), dot_nt(low, w1)], axis=1).astype(BF)
        da1_o[here, :] = jnp.concatenate([dot_nt(low, w2), dot_nt(low, w3)], axis=1).astype(BF)
        mine, other = a0[slot], a1[slot]
        parts = (mine[:, :width], mine[:, width:], other[:, :width], other[:, width:])
        grad_out = [total + dot_tn(part, low) for total, part in zip(grad_out, parts)]
    for shard in range(4):
        out = keep_o if shard < 2 else give_o
        out[shard % 2, 0:wide, :] = grad_query[shard].astype(BF)
        for part in range(wide // width):
            out[shard % 2, wide + part * width : wide + (part + 1) * width, :] = grad_out[shard][
                :, part * width : (part + 1) * width
            ].astype(BF)
    gain_o[...] = jnp.broadcast_to(gain_total, gain_o.shape)


def memory_back_body(scalars, dk, dv, m0, m1, m2, m3, w0, w1, mine_o, send_o, keep_o, give_o):
    size = m0.shape[0]
    wide = m0.shape[1]
    totals = [jnp.zeros((wide, 2 * PAIR), F32) for unused in range(2)]
    for slot, memory in enumerate((m0, m1, m2, m3)):
        place = block_of(scalars, slot, size)
        total = jnp.zeros((size, wide), F32)
        for pair, w in enumerate((w0, w1)):
            part = jnp.concatenate([dk[pair, pl.ds(place, size), :], dv[pair, pl.ds(place, size), :]], axis=1)
            total += dot_nt(part, wide_rows(w, 0, memory.shape[1], 2))
            totals[pair] += dot_tn(memory[...], part)
        (mine_o if slot < 2 else send_o)[slot % 2] = total.astype(BF)
    for total, out in zip(totals, (keep_o, give_o)):
        out[0:wide, :] = total[:, :PAIR].astype(BF)
        out[wide : 2 * wide, :] = total[:, PAIR:].astype(BF)


def qkv_grad_body(
    dqkv0, dqkv1, x0, x1, x2, x3, gains, w0, w1, gain_two, gain_three, keep_o, give_o, gain_o
):
    wide = x0.shape[1]
    totals = [jnp.zeros((wide, 3 * PAIR), F32) for unused in range(2)]
    for slot, x in enumerate((x0, x1, x2, x3)):
        normal, unused = normalize(x[...].astype(F32))
        normed = (normal * gains[0:1, :]).astype(BF)
        totals = [t + dot_tn(normed, d[slot]) for t, d in zip(totals, (dqkv0, dqkv1))]
    for part in range(3):
        here = slice(part * wide, (part + 1) * wide)
        lanes = slice(part * PAIR, (part + 1) * PAIR)
        keep_o[here, :] = totals[0][:, lanes]
        give_o[here, :] = totals[1][:, lanes].astype(BF)
    product = totals[0] * w0[...].astype(F32) + totals[1] * w1[...].astype(F32)
    gain = lax.dot_general(
        jnp.ones((8, 3 * PAIR), F32),
        product,
        (((1,), (1,)), ((), ())),
        precision=lax.Precision.HIGHEST,
        preferred_element_type=F32,
    ) / gains[0:1, :]
    gain_o[...] = jnp.concatenate(
        [gain[:1], gain_two[:1, :], gain_three[:1, :], jnp.zeros((5, wide), F32)], axis=0
    )


def back_to_input_body(dqkv0, dqkv1, w0, w1, mine_o, send_o):
    for slot in range(4):
        dn = dot_nt(dqkv0[slot], w0[...]) + dot_nt(dqkv1[slot], w1[...])
        (mine_o if slot < 2 else send_o)[slot % 2] = dn.astype(BF)


def input_grad_body(dn0, dn1, x0, x1, dh, gains, g0_o, g1_o):
    size = x0.shape[0]
    for slot, (x, g_o) in enumerate(((x0, g0_o), (x1, g1_o))):
        here = pl.ds(slot * size, size)
        normal, inv_sigma = normalize(x[...].astype(F32))
        dn = dn0[slot].astype(F32) + dn1[slot].astype(F32)
        g_o[...] = (dh[here, :] + normalize_back(dn, gains[0:1, :], normal, inv_sigma)).astype(BF)


def pick_body(order, source, out):
    def one(i, unused):
        out[i] = source[order[i]]
        return unused

    lax.fori_loop(0, source.shape[0], one, 0)


def pick(array, order):
    return call(pick_body, struct(array.shape, array.dtype), [], "pick", 1)(
        order, array, specs=[SMEM, VM]
    )


def pick_memory_body(order, source, out, digits_o):
    count, share = out.shape[:2]

    def one(i, unused):
        out[i] = source[order[i], 0:share, :]
        return unused

    lax.fori_loop(0, count, one, 0)
    digits_o[...] = source[order[order[count]], share:, :]


def spread_rows(block):
    return lax.all_to_all(block, "dp", split_axis=0, concat_axis=0, tiled=True)


def swap_chip(array):
    return lax.ppermute(array, "tensor", [(i, i ^ 2) for i in range(4)])


def swap_core(array):
    return lax.ppermute(array, "tensor", [(i, i ^ 1) for i in range(4)])


def pack_body(*refs):
    out = refs[-1]
    at = 0
    for ref in refs[:-1]:
        rows, lanes = ref.shape
        for begin in range(0, lanes, PAIR):
            out[at : at + rows, :] = ref[:, begin : begin + PAIR]
            at += rows


def pack(*arrays):
    rows = sum(a.size for a in arrays) // PAIR
    return call(pack_body, struct((rows, PAIR), arrays[0].dtype), [], "pack", 2)(
        *arrays, specs=[VM] * len(arrays)
    )


def swap_row(array, bit):
    return lax.ppermute(array, "dp", [(i, i ^ bit) for i in range(lax.axis_size("dp"))])


def halves(array, upper):
    half = array.shape[0] // 2
    low, high = array[:half], array[half:]
    return jnp.where(upper, high, low), jnp.where(upper, low, high).astype(BF)


def rest_groups():
    count = lax.axis_size("dp")
    return [[i for i in range(count) if i % 2 == part] for part in range(2)]


def rest_sends(arrays):
    group = lax.axis_size("dp") // 2
    width = arrays[0].shape[1]
    joint = jnp.concatenate([a.reshape(group, -1, width) for a in arrays], axis=1)
    me = lax.axis_index("dp") // 2

    def piece(index):
        return lax.dynamic_index_in_dim(joint, index, 0, keepdims=False)

    if group != 4:
        return piece(me), [joint.reshape(-1, width)]
    return piece(me), [piece(me ^ k) for k in (1, 2, 3)]


def rest_move(sends):
    if len(sends) == 3:
        return [swap_row(send, 2 * k) for k, send in zip((1, 2, 3), sends)]
    group = lax.axis_size("dp") // 2
    spread = lax.all_to_all(
        sends[0], "dp", split_axis=0, concat_axis=0, axis_index_groups=rest_groups(), tiled=True
    )
    return [spread.reshape(group, -1, spread.shape[1])]


def add_all(own, got):
    if got[0].ndim == own.ndim:
        return sum([g.astype(F32) for g in got], own.astype(F32))
    return jnp.sum(got[0].astype(F32), axis=0)


def rest_collect(piece):
    if lax.axis_size("dp") == 8:
        return [piece] + [swap_row(piece, 2 * k) for k in (1, 2, 3)]
    return [lax.all_gather(piece, "dp", axis=0, axis_index_groups=rest_groups(), tiled=True)]


def assemble_body(order, *refs):
    out = refs[-1]
    for index, ref in enumerate(refs[:-1]):
        out[order[index]] = ref[...]


def rest_assemble(pieces):
    if len(pieces) == 1:
        return pieces[0]
    me = lax.axis_index("dp") // 2
    order = (jnp.arange(4, dtype=jnp.int32) ^ me).astype(jnp.int32)
    return call(assemble_body, struct((4,) + pieces[0].shape, BF), [], "assemble", 1)(
        order, *pieces, specs=[SMEM] + [VM] * 4
    ).reshape(-1, pieces[0].shape[1])


def finish_one_body(flag, half, other, up_o, down_o, co_o):
    upper = flag[0] != 0
    low = jnp.where(upper, other[...], half[...]).astype(F32)
    high = jnp.where(upper, half[...], other[...]).astype(F32)
    wide, units = up_o.shape[0], down_o.shape[0]
    split = low.shape[0] - wide
    up_o[...] = low[:wide]
    down_o[0:split, :] = low[wide:]
    down_o[split:, :] = high[: units - split]
    co_o[...] = high[units - split :]


def finish_two(cq_o, so_o, kv_o, two_s):
    wide = cq_o.shape[0]
    cq_o[...] = two_s[0:wide, :]
    for i in range(wide // PAIR):
        so_o[:, i * PAIR : (i + 1) * PAIR] = two_s[wide + i * PAIR : wide + (i + 1) * PAIR, :]
    kv_o[pl.ds(0, wide, stride=2), :] = two_s[2 * wide : 3 * wide, :]
    kv_o[pl.ds(1, wide, stride=2), :] = two_s[3 * wide :, :]


def finish_rest_body(flag, half, other, cq_o, so_o, kv_o, qkv_o, gain_o, two_s):
    upper = flag[0] != 0
    group = half.shape[0]
    two, three = two_s.shape[0] // (2 * group), qkv_o.shape[0] // (2 * group)
    gain = jnp.zeros(gain_o.shape, F32)
    for index in range(group):
        low = jnp.where(upper, other[index], half[index]).astype(F32)
        high = jnp.where(upper, half[index], other[index]).astype(F32)
        for at, piece in ((index, low), (group + index, high)):
            two_s[at * two : (at + 1) * two, :] = piece[0:two]
            qkv_o[at * three : (at + 1) * three, :] = piece[two : two + three]
            gain += piece[two + three :]
    finish_two(cq_o, so_o, kv_o, two_s)
    gain_o[...] = gain


def finish_pieces_body(flag, order, p0, p1, p2, p3, r0, r1, r2, r3, cq_o, so_o, kv_o, qkv_o, gain_o, two_s):
    upper = flag[0] != 0
    two, three = two_s.shape[0] // 8, qkv_o.shape[0] // 8
    gain = jnp.zeros(gain_o.shape, F32)
    for index, (mine, other) in enumerate(((p0, r0), (p1, r1), (p2, r2), (p3, r3))):
        low = jnp.where(upper, other[...], mine[...]).astype(F32)
        high = jnp.where(upper, mine[...], other[...]).astype(F32)
        for first, piece in ((0, low), (4, high)):
            at = first + order[index]
            two_s[pl.ds(pl.multiple_of(at * two, two), two), :] = piece[0:two]
            qkv_o[pl.ds(pl.multiple_of(at * three, three), three), :] = piece[two : two + three]
            gain += piece[two + three :]
    finish_two(cq_o, so_o, kv_o, two_s)
    gain_o[...] = gain


def on_device(
    x_first,
    x_second,
    memory,
    cot_first,
    cot_second,
    seg_ids,
    lengths,
    perm,
    inverse,
    gains,
    w_self_qkv,
    w_self_out,
    w_cross_q,
    w_cross_kv,
    w_cross_out,
    w_up,
    w_down,
):
    length = seg_ids.shape[2]
    size = x_first.shape[1]
    wide = x_first.shape[2]
    width = w_self_out.shape[0]
    units = w_up.shape[1]
    mine = 2 * size
    heads = 2 * width
    me = lax.axis_index("tensor")
    row = lax.axis_index("dp")
    rows = perm.shape[0]
    share = size // rows
    first_step = me < 2
    upper = (row & 1) != 0

    def both(one, two):
        return jnp.where(first_step, one, two)

    def stage(**values):
        return types.SimpleNamespace(**lax.optimization_barrier(values))

    pair_array = struct((2, length, PAIR), BF)
    out_half = struct((2, size, heads), BF)
    lse_array = struct((2, 2, length), F32)
    limits = [pltpu.VMEM((1, length), jnp.int32), pltpu.VMEM((1, length), jnp.int32)]
    def forward_scratch(key_block):
        return [
            pltpu.VMEM((2, length + key_block - ALIGN, PAIR), BF),
            pltpu.VMEM((2, PAIR, length + key_block - ALIGN), BF),
            pltpu.VMEM((length, heads), BF),
        ] + limits

    whole = pl.BlockSpec(memory_space=pltpu.VMEM)

    def part_of(rows_of_block, index):
        return pl.BlockSpec((rows_of_block, PAIR), lambda i: (index, 0))

    x_first, x_second, memory = x_first[0], x_second[0], memory[0]
    x_got = swap_chip(both(x_second, x_first))
    wqkv_own = w_self_qkv.reshape(wide, -1)
    wqkv_got = swap_chip(wqkv_own)
    x_own = both(x_first, x_second)
    place = jnp.arange(length, dtype=jnp.int32)
    meta = jnp.where(place[None, :] < lengths[0][:, None], seg_ids[0], DOCS)
    docs = jnp.arange(DOCS + 2, dtype=jnp.int32)
    cuts = jnp.sum((meta[:, None, :] < docs[None, :, None]).astype(jnp.int32), axis=-1).reshape(-1)
    digits = jnp.stack([cuts // 64, cuts % 64]).astype(BF)
    digits = jnp.pad(digits, ((0, 14), (0, wide - cuts.shape[0])))
    payload = jnp.concatenate(
        [memory.reshape(rows, share, wide), jnp.broadcast_to(digits[None], (rows, 16, wide))], axis=1
    )
    x_sib0 = swap_core(x_own)
    pack_a = pack(w_self_out, w_cross_q, w_cross_kv.reshape(wide, -1), w_cross_out)
    pack_b = pack(w_up, w_down)
    spread = spread_rows(payload.reshape(-1, wide)).reshape(payload.shape)
    cot_own = both(cot_first[0], cot_second[0])
    cot_send = both(cot_second[0], cot_first[0])
    x_sib1 = swap_core(x_got)
    picked, digits = call(
        pick_memory_body,
        (struct((rows, share, wide), BF), struct((16, wide), BF)),
        [],
        "pick_memory",
        2,
    )(jnp.concatenate([perm, row[None].astype(jnp.int32)]), spread, specs=[SMEM, VM])
    s = stage(
        x_got=x_got,
        x_sib1=x_sib1,
        digits=digits,
        wqkv_own=wqkv_own,
        wqkv_got=wqkv_got,
        pack_a=pack_a,
        pack_b=pack_b,
        cot_own=cot_own,
        cot_send=cot_send,
        x_sib0=x_sib0,
        cuts=cuts,
        memory=memory,
    )
    pack_a, pack_b, cot_own, cot_send = (s.pack_a, s.pack_b, s.cot_own, s.cot_send)
    x_sib0, cuts, memory = s.x_sib0, s.cuts, s.memory
    x_got, x_sib1, wqkv_own, wqkv_got = (s.x_got, s.x_sib1, s.wqkv_own, s.wqkv_got)
    digits = s.digits
    digits = digits[:2, : cuts.shape[0]].astype(jnp.int32)
    cuts = both(digits[0] * 64 + digits[1], cuts)
    places = jnp.stack([me, me ^ 2, me ^ 1, me ^ 3]).astype(jnp.int32)
    s = stage(
        scalars=jnp.concatenate([cuts, places]),
        x0=x_own,
        x1=x_got,
        x2=x_sib0,
        x3=x_sib1,
        w0=wqkv_own,
        w1=wqkv_got,
        picked=picked,
        pack_a=pack_a,
        pack_b=pack_b,
        cot_own=cot_own,
        cot_send=cot_send,
        memory=memory,
    )
    scalars = s.scalars
    xs = (s.x0, s.x1, s.x2, s.x3)
    wqkv = (s.w0, s.w1)
    memory = s.memory

    memory_one = spread_rows(picked.reshape(memory.shape))
    q, k, v, a_mine, a_send, lse = call(
        self_forward_body,
        (pair_array, pair_array, pair_array, out_half, out_half, lse_array),
        forward_scratch(SELF_BK),
        "self_forward",
        4,
    )(scalars, *xs, gains, *wqkv, specs=[SMEM] + [VM] * 7)
    pack_a, pack_b = s.pack_a, s.pack_b
    s = stage(
        q=q,
        k=k,
        v=v,
        a_mine=a_mine,
        a_send=a_send,
        lse=lse,
        memory_one=memory_one,
        a_got=swap_chip(pack_a),
        cot_got=swap_chip(s.cot_send),
        pack_a2=swap_core(pack_a),
        pack_b2=swap_core(pack_b),
    )
    q, k, v, a_mine, a_send, lse = (s.q, s.k, s.v, s.a_mine, s.a_send, s.lse)
    pack_a1, pack_a2, pack_b2, cot_got = s.a_got, s.pack_a2, s.pack_b2, s.cot_got
    memory_one = s.memory_one
    m_got = swap_chip(both(memory, memory_one))
    s = stage(
        a_got=swap_core(a_send),
        pack_a3=swap_core(pack_a1),
        m_own=both(memory_one, memory),
    )
    a_got, m_own = s.a_got, s.m_own
    packs_a = (pack_a, pack_a1, pack_a2, s.pack_a3)

    so_cq = part_of(2 * wide, 0)
    h1, cq_mine, cq_send = call(
        after_self_body,
        (struct((mine, wide), F32), struct((mine, heads), BF), struct((mine, heads), BF)),
        [],
        "after_self",
        6,
        (1,),
    )(
        *xs[:2], a_mine, a_got, *packs_a, gains, specs=[whole] * 4 + [so_cq] * 4 + [whole]
    )
    h1, m_got = lax.optimization_barrier((h1, m_got))
    s = stage(
        h1=h1,
        cq_mine=cq_mine,
        cq_got=swap_core(cq_send),
        m1=m_got,
        m2=swap_core(m_own),
        m3=swap_core(m_got),
        pack_b=pack_b,
    )
    h1, cq_mine, cq_got, pack_b = s.h1, s.cq_mine, s.cq_got, s.pack_b
    ms = (m_own, s.m1, s.m2, s.m3)

    kv = part_of(2 * wide, 1)
    cq, ck, cv, b_mine, b_send, lse_b = call(
        cross_forward_body,
        (pair_array, pair_array, pair_array, out_half, out_half, lse_array),
        forward_scratch(CROSS_BK),
        "cross_forward",
        24,
        (1,),
    )(
        scalars,
        cq_mine,
        cq_got,
        *ms,
        pack_a,
        pack_a1,
        specs=[SMEM] + [whole] * 6 + [kv] * 2,
    )
    s = stage(
        cq=cq,
        ck=ck,
        cv=cv,
        b_mine=b_mine,
        b_send=b_send,
        lse_b=lse_b,
        pack_b1=swap_chip(pack_b),
    )
    cq, ck, cv, b_mine, b_send, lse_b = (s.cq, s.ck, s.cv, s.b_mine, s.b_send, s.lse_b)
    pack_b1 = s.pack_b1
    s = stage(b_got=swap_core(b_send), pack_b3=swap_core(pack_b1))

    co = part_of(wide, 4)
    rows_one = wide + units + width
    (
        y_own, y_send, dh2, db_mine, db_send, one_keep, one_give, gain_three,
    ) = call(
        middle_body,
        (
            struct((size, wide), BF),
            struct((size, wide), BF),
            struct((mine, wide), F32),
            struct((mine, heads), BF),
            struct((mine, heads), BF),
            struct((2, rows_one, wide), BF),
            struct((2, rows_one, wide), BF),
            struct((8, wide), F32),
        ),
        [
            pltpu.VMEM((mine, wide), F32),
            pltpu.VMEM((mine, wide), BF),
            pltpu.VMEM((mine, wide), BF),
            pltpu.VMEM((mine, wide), F32),
            pltpu.VMEM((mine, wide), F32),
        ],
        "middle",
        25,
        (1,),
    )(
        scalars,
        h1,
        b_mine,
        s.b_got,
        *packs_a,
        pack_b,
        pack_b1,
        pack_b2,
        s.pack_b3,
        gains,
        cot_own,
        cot_got,
        specs=[SMEM] + [whole] * 3 + [co] * 4 + [whole] * 7,
    )

    def over_core(keep, got):
        own = keep[0].astype(F32) + got[0].astype(F32)
        other = keep[1].astype(F32) + got[1].astype(F32)
        return own, other.astype(BF)

    one_own, one_send = over_core(one_keep, swap_core(one_give))
    s = stage(
        y_own=y_own,
        y_send=y_send,
        dh2=dh2,
        db_mine=db_mine,
        db_got=swap_core(db_send),
        one_own=one_own,
        one_send=one_send,
        gain_three=gain_three,
    )
    y_own, y_send, dh2, one_own = s.y_own, s.y_send, s.dh2, s.one_own
    gain_three = s.gain_three

    backward_scratch = [
        pltpu.VMEM((2, length + BK - ALIGN, PAIR), BF),
        pltpu.VMEM((2, PAIR, length + BK - ALIGN), BF),
        pltpu.VMEM((2, length + BK - ALIGN, PAIR), BF),
        pltpu.VMEM((2, length, PAIR), BF),
        pltpu.VMEM((2, length, PAIR), BF),
        pltpu.VMEM((2, length, PAIR), BF),
        pltpu.VMEM((2, length + BK - ALIGN, PAIR), F32),
        pltpu.VMEM((2, length + BK - ALIGN, PAIR), F32),
    ] + limits
    dcq_mine, dcq_send, dck, dcv = call(
        cross_backward_body,
        (out_half, out_half, pair_array, pair_array),
        backward_scratch,
        "cross_backward",
        27,
    )(
        scalars, cq, ck, cv, b_mine, b_send, lse_b, s.db_mine, s.db_got,
        specs=[SMEM] + [VM] * 8,
    )
    s = stage(
        dcq_mine=dcq_mine,
        dcq_send=dcq_send,
        dck=dck,
        dcv=dcv,
        one_got=swap_chip(s.one_send),
        one_own=one_own,
    )
    dcq_mine = s.dcq_mine
    one_keep, one_send = halves(s.one_own + s.one_got.astype(F32), upper)
    one_got = swap_row(one_send, 1)
    dm_mine, dm_send, keep_kv, give_kv = call(
        memory_back_body,
        (
            struct((2, size, wide), BF),
            struct((2, size, wide), BF),
            struct((2 * wide, width), BF),
            struct((2 * wide, width), BF),
        ),
        [],
        "memory_back",
        6,
        (1,),
    )(
        scalars, s.dck, s.dcv, *ms, pack_a, pack_a1, specs=[SMEM] + [whole] * 6 + [kv] * 2
    )
    dm_core = swap_core(dm_send)
    dm_own, dm_other = [
        (dm_mine[i].astype(F32) + dm_core[i].astype(F32)).astype(BF) for i in range(2)
    ]
    s = stage(
        dcq_got=swap_core(s.dcq_send),
        one_keep=one_keep,
        dm_own=dm_own,
        dm_other=dm_other,
        keep_kv=keep_kv,
        give_kv=give_kv,
    )
    one_keep, dm_own, keep_kv, give_kv = (s.one_keep, s.dm_own, s.keep_kv, s.give_kv)

    dh1, da_mine, da_send, keep_two, give_two, gain_two = call(
        between_body,
        (
            struct((mine, wide), F32),
            struct((mine, heads), BF),
            struct((mine, heads), BF),
            struct((2, 2 * wide, width), BF),
            struct((2, 2 * wide, width), BF),
            struct((8, wide), F32),
        ),
        [],
        "between",
        3,
        (1,),
    )(
        h1, dh2, a_mine, a_got, dcq_mine, s.dcq_got, *packs_a, gains,
        specs=[whole] * 6 + [so_cq] * 4 + [whole],
    )
    s = stage(
        dh1=dh1,
        da_mine=da_mine,
        da_send=da_send,
        keep_two=keep_two,
        give_two=give_two,
        gain_two=gain_two,
        one_got=one_got,
        one_keep=one_keep,
        dm_got=swap_chip(s.dm_other),
        dm_own=dm_own,
    )
    dh1, da_mine, gain_two = s.dh1, s.da_mine, s.gain_two
    one_own, one_sends = rest_sends([(s.one_keep + s.one_got.astype(F32)).astype(BF)])
    two_own, two_send = over_core(s.keep_two, swap_core(s.give_two))
    s = stage(
        da_got=swap_core(s.da_send),
        dm_one=both(s.dm_own, s.dm_got),
        dm_two=both(s.dm_got, s.dm_own),
        two_own=two_own,
        two_send=jnp.concatenate([two_send, give_kv], axis=0),
        y_send=y_send,
        one_own=one_own,
        one_sends=one_sends,
    )
    two_own, dm_two, one_own = s.two_own, s.dm_two, s.one_own

    qkv_rows = struct((4, size, 3 * PAIR), BF)
    dqkv0, dqkv1 = call(
        self_backward_body, (qkv_rows, qkv_rows), backward_scratch, "self_backward", 32
    )(
        scalars, q, k, v, a_mine, a_send, lse, da_mine, s.da_got, specs=[SMEM] + [VM] * 8
    )
    s = stage(
        dqkv0=dqkv0,
        dqkv1=dqkv1,
        two_got=swap_chip(s.two_send),
        two_own=two_own,
        y_got=swap_chip(s.y_send),
        y_own=y_own,
        dm_spread=spread_rows(s.dm_one),
        dm_two=dm_two,
        keep_kv=keep_kv,
        one_own=one_own,
        one_got=rest_move(s.one_sends),
    )
    dqkv0, dqkv1, dm_two = s.dqkv0, s.dqkv1, s.dm_two
    two_total = jnp.concatenate(
        [
            s.two_own + s.two_got[: 2 * wide].astype(F32),
            s.keep_kv.astype(F32) + s.two_got[2 * wide :].astype(F32),
        ],
        axis=0,
    )
    two_keep, two_send = halves(two_total, upper)
    s = stage(
        two_keep=two_keep,
        two_send=two_send,
        dm_picked=pick(s.dm_spread.reshape(rows, -1, wide), inverse),
        y_own=s.y_own,
        y_got=s.y_got,
        one_piece=add_all(s.one_own, s.one_got).astype(BF),
    )
    two_keep, y_own, y_got = s.two_keep, s.y_own, s.y_got

    dm_back = spread_rows(s.dm_picked.reshape(memory.shape))
    one_pieces = rest_collect(s.one_piece)
    qkv_gradient = (3 * wide, width)
    gain_row = struct((8, wide), F32)
    keep_qkv, give_qkv, gain_all = call(
        qkv_grad_body,
        (struct(qkv_gradient, F32), struct(qkv_gradient, BF), gain_row),
        [],
        "qkv_grad",
        8,
    )(dqkv0, dqkv1, *xs, gains, *wqkv, gain_two, gain_three, specs=[VM] * 11)
    s = stage(
        keep_qkv=keep_qkv,
        give_qkv=give_qkv,
        gain_all=gain_all,
        two_got=swap_row(s.two_send, 1),
        two_keep=two_keep,
        dqkv0=dqkv0,
        dqkv1=dqkv1,
    )
    keep_qkv, gain_all = s.keep_qkv, s.gain_all
    dqkv0, dqkv1 = s.dqkv0, s.dqkv1

    qkv_got = swap_chip(s.give_qkv)
    dn_mine, dn_send = call(
        back_to_input_body,
        (struct((2, size, wide), BF), struct((2, size, wide), BF)),
        [],
        "back_to_input",
        4,
    )(dqkv0, dqkv1, *wqkv, specs=[VM] * 4)
    s = stage(
        keep_qkv=keep_qkv,
        gain_all=gain_all,
        qkv_got=qkv_got,
        dn_mine=dn_mine,
        dn_send=dn_send,
        two_got=s.two_got,
        two_keep=s.two_keep,
        dm_back=dm_back,
        one_pieces=one_pieces,
    )
    dn_mine, dm_back, one_pieces = s.dn_mine, s.dm_back, s.one_pieces
    three_keep, three_send = halves(s.keep_qkv + s.qkv_got.astype(F32), upper)
    s = stage(
        three_keep=three_keep,
        three_send=three_send,
        two_half=(s.two_keep + s.two_got.astype(F32)).astype(BF),
        gain_all=s.gain_all,
        dn_got=swap_core(s.dn_send),
    )
    two_half = s.two_half

    grad_own, grad_send = call(
        input_grad_body,
        (struct((size, wide), BF), struct((size, wide), BF)),
        [],
        "input_grad",
        5,
    )(dn_mine, s.dn_got, *xs[:2], dh1, gains, specs=[VM] * 6)
    s = stage(
        three_got=swap_row(s.three_send, 1),
        three_keep=s.three_keep,
        gain_all=s.gain_all + swap_core(s.gain_all),
        grad_own=grad_own,
        grad_send=grad_send,
        y_own=y_own,
        y_got=y_got,
        dm_two=dm_two,
        dm_back=dm_back,
        one_half=rest_assemble(one_pieces),
    )
    one_half, grad_own = s.one_half, s.grad_own
    three_half = (s.three_keep + s.three_got.astype(F32)).astype(BF)
    share_two, share_three = two_half.shape[0], three_half.shape[0]
    last_own, last_sends = rest_sends([two_half, three_half])

    y_first = both(s.y_own, s.y_got)
    y_second = both(s.y_got, s.y_own)
    grad_memory = s.dm_two.astype(F32) + s.dm_back.astype(F32)
    s = stage(
        last_own=last_own,
        last_got=rest_move(last_sends),
        gain_all=s.gain_all + swap_chip(s.gain_all),
        grad_own=grad_own,
        grad_send=s.grad_send,
        one_half=one_half,
        one_other=swap_row(one_half, 1),
        y_first=y_first,
        y_second=y_second,
        grad_memory=grad_memory,
    )
    one_half, one_other, grad_own = s.one_half, s.one_other, s.grad_own
    y_first, y_second, grad_memory = s.y_first, s.y_second, s.grad_memory
    grad_got = swap_chip(s.grad_send)
    gain_rows = 8 * wide // width
    last = jnp.concatenate(
        [
            add_all(s.last_own, s.last_got).astype(BF),
            s.gain_all.astype(BF).reshape(gain_rows, width),
        ],
        axis=0,
    )
    pieces = rest_collect(last)
    others = [swap_row(piece, 1) for piece in pieces]
    flag = (row & 1)[None].astype(jnp.int32)
    grad_up, grad_down, grad_cross_out = call(
        finish_one_body,
        (struct((wide, units), F32), struct((units, wide), F32), struct((width, wide), F32)),
        [],
        "finish_one",
        2,
    )(flag, one_half, one_other, specs=[SMEM, VM, VM])
    slab = struct((wide, width), F32)
    group = (rows // 2, last.shape[0], width)
    if len(pieces) == 1:
        operands = [array[0].reshape(group) for array in (pieces, others)]
        specs = [SMEM, VM, VM]
    else:
        order = (jnp.arange(4, dtype=jnp.int32) ^ (row // 2)).astype(jnp.int32)
        operands = [order] + pieces + others
        specs = [SMEM, SMEM] + [VM] * 8
    grad_cross_q, grad_self_out, grad_kv, grad_qkv, gain_total = call(
        finish_rest_body if len(pieces) == 1 else finish_pieces_body,
        (
            slab,
            struct((width, wide), F32),
            struct((2 * wide, width), F32),
            struct((3 * wide, width), F32),
            struct((gain_rows, width), F32),
        ),
        [pltpu.VMEM((4 * wide, width), F32)],
        "finish_rest",
        2,
    )(flag, *operands, specs=specs)
    grad_kv = grad_kv.reshape(wide, 2, width)
    grad_qkv = grad_qkv.reshape(3, wide, width).transpose(1, 0, 2)
    gain_total = gain_total.reshape(-1, wide)[:3]
    grad_gains = lax.dynamic_slice(gain_total, (0, me * width), (3, width))
    grad_first = both(grad_own, grad_got)
    return (
        y_first[None],
        y_second[None],
        grad_first[None],
        grad_memory[None],
        grad_gains,
        grad_qkv,
        grad_self_out,
        grad_cross_q,
        grad_kv,
        grad_cross_out,
        grad_up,
        grad_down,
    )


def solution(mesh):
    in_specs = (
        P("dp", "tensor", None),
        P("dp", "tensor", None),
        P("dp", "tensor", None),
        P("dp", "tensor", None),
        P("dp", "tensor", None),
        P("dp", None, None),
        P("dp", None),
        P(),
        P(),
        P(),
        P(None, None, "tensor"),
        P("tensor", None),
        P(None, "tensor"),
        P(None, None, "tensor"),
        P("tensor", None),
        P(None, "tensor"),
        P("tensor", None),
    )
    out_specs = (
        P("dp", "tensor", None),
        P("dp", "tensor", None),
        P("dp", "tensor", None),
        P("dp", "tensor", None),
        P(None, "tensor"),
        P(None, None, "tensor"),
        P("tensor", None),
        P(None, "tensor"),
        P(None, None, "tensor"),
        P("tensor", None),
        P(None, "tensor"),
        P("tensor", None),
    )
    return jax.shard_map(
        on_device, mesh=mesh, in_specs=in_specs, out_specs=out_specs, check_vma=False
    )
```

```python
import math
import types

import jax
import jax.numpy as jnp
from jax import lax
from jax.experimental import pallas as pl
from jax.experimental.pallas import tpu as pltpu
from jax.sharding import PartitionSpec as P

HEAD_DIM = 64
EPSILON = 1e-05
NEG_FILL = -1e30
DOCS = 16
PAIR = 2 * HEAD_DIM
BQ = 256
BK = 256
SELF_BK = 640
CROSS_BK = 512
ALIGN = 128
BF = jnp.bfloat16
F32 = jnp.float32
VMEM_BYTES = 56 * 1024 * 1024
LOG2E = 1.4426950408889634

ANY = pl.BlockSpec(memory_space=pl.ANY)
SMEM = pl.BlockSpec(memory_space=pltpu.SMEM)
VM = pl.BlockSpec(memory_space=pltpu.VMEM)


def dot(a, b):
    return lax.dot_general(a, b, (((1,), (0,)), ((), ())), preferred_element_type=F32)


def dot_nt(a, b):
    return lax.dot_general(a, b, (((1,), (1,)), ((), ())), preferred_element_type=F32)


def dot_tn(a, b):
    return lax.dot_general(a, b, (((0,), (0,)), ((), ())), preferred_element_type=F32)


def normalize(hidden):
    centred = hidden - jnp.mean(hidden, axis=-1, keepdims=True)
    inv_sigma = lax.rsqrt(jnp.mean(centred * centred, axis=-1, keepdims=True) + EPSILON)
    return centred * inv_sigma, inv_sigma


def normalize_back(grad_scaled, gain, normal, inv_sigma):
    grad_normal = grad_scaled * gain
    first_mean = jnp.mean(grad_normal, axis=-1, keepdims=True)
    second_mean = jnp.mean(grad_normal * normal, axis=-1, keepdims=True)
    return inv_sigma * (grad_normal - first_mean - normal * second_mean)


def call(body, outs, scratch, name, cost, grid=()):
    def run(*args, specs):
        moved = sum(a.size * a.dtype.itemsize for a in args)
        return pl.pallas_call(
            body,
            out_shape=outs,
            grid=grid,
            in_specs=specs,
            out_specs=jax.tree.map(lambda _: VM, outs),
            scratch_shapes=scratch,
            compiler_params=pltpu.CompilerParams(vmem_limit_bytes=VMEM_BYTES),
            cost_estimate=pl.CostEstimate(flops=int(cost * 1.15e9), bytes_accessed=moved, transcendentals=0),
            name=name,
        )(*args)

    return run


def struct(shape, dtype):
    return jax.ShapeDtypeStruct(shape, dtype)


QUERY_AT, KEY_AT, PLACE_AT = 0, DOCS + 2, 2 * (DOCS + 2)
ROW_AT = PLACE_AT + 4


def key_limits(scalars, key_at, length):
    place = lax.broadcasted_iota(jnp.int32, (1, length), 1)
    first = jnp.full((1, length), scalars[key_at], jnp.int32)
    after = jnp.full((1, length), scalars[key_at + 1], jnp.int32)
    for doc in range(1, DOCS + 1):
        inside = place >= scalars[QUERY_AT + doc]
        first = jnp.where(inside, scalars[key_at + doc], first)
        after = jnp.where(inside, scalars[key_at + doc + 1], after)
    return first, after


def window(scalars, key_at, begin, size):
    low = scalars[key_at]
    high = scalars[key_at + 1]
    for doc in range(1, DOCS + 1):
        low = jnp.where(begin >= scalars[QUERY_AT + doc], scalars[key_at + doc], low)
        high = jnp.where(
            begin + (BQ - 1) >= scalars[QUERY_AT + doc], scalars[key_at + doc + 1], high
        )
    low = (low // ALIGN) * ALIGN
    return low, (high - low + (size - 1)) // size


def two_heads(block):
    lane = lax.broadcasted_iota(jnp.int32, block.shape, 1)
    zero = jnp.zeros_like(block)
    return jnp.concatenate(
        [jnp.where(lane < HEAD_DIM, block, zero), jnp.where(lane >= HEAD_DIM, block, zero)], axis=0
    )


def attend_forward(scalars, key_at, key_block, pairs, q_s, k_s, vt_s, o_s, lse_s, first_s, after_s):
    length = q_s.shape[1]
    scale = LOG2E / math.sqrt(HEAD_DIM)
    first, after = key_limits(scalars, key_at, length)
    first_s[...] = first
    after_s[...] = after
    rows = lax.broadcasted_iota(jnp.int32, (key_block, BQ), 0)

    def one_block(index, unused):
        begin = pl.multiple_of(index * BQ, BQ)
        low, count = window(scalars, key_at, begin, key_block)
        first_row = first_s[:, pl.ds(begin, BQ)]
        after_row = after_s[:, pl.ds(begin, BQ)]
        queries = [two_heads(q_s[pair, pl.ds(begin, BQ), :]) for pair in pairs]

        def step(turn, carry):
            start = pl.multiple_of(low + turn * key_block, ALIGN)
            allowed = (rows >= first_row - start) & (rows < after_row - start)
            allowed = jnp.concatenate([allowed, allowed], axis=1)
            results = []
            for pair, query, (top, total, out) in zip(pairs, queries, carry):
                scores = dot_nt(k_s[pair, pl.ds(start, key_block), :], query) * scale
                scores = jnp.where(allowed, scores, NEG_FILL)
                new_top = jnp.maximum(top, jnp.max(scores, axis=0, keepdims=True))
                shrink = jnp.exp2(top - new_top)
                raised = jnp.exp2(scores - new_top)
                total = total * shrink + jnp.sum(raised, axis=0, keepdims=True)
                low_probs = raised.astype(BF)
                value = vt_s[pair, :, pl.ds(start, key_block)]
                out = [
                    out[0] * shrink[:, :BQ] + dot(value[:HEAD_DIM], low_probs[:, :BQ]),
                    out[1] * shrink[:, BQ:] + dot(value[HEAD_DIM:], low_probs[:, BQ:]),
                ]
                results.append((new_top, total, out))
            return results

        zero = jnp.zeros((HEAD_DIM, BQ), F32)
        fresh = (jnp.full((1, 2 * BQ), NEG_FILL, F32), jnp.zeros((1, 2 * BQ), F32), [zero, zero])
        results = lax.fori_loop(0, count, step, [fresh for unused_pair in pairs])
        for pair, (top, total, out) in zip(pairs, results):
            inverse = 1.0 / total
            out = jnp.concatenate([out[0] * inverse[:, :BQ], out[1] * inverse[:, BQ:]], axis=0)
            o_s[pl.ds(begin, BQ), pair * PAIR : (pair + 1) * PAIR] = out.T.astype(BF)
            log_total = top + jnp.log2(total)
            lse_s[pair, 0:1, pl.ds(begin, BQ)] = log_total[:, :BQ]
            lse_s[pair, 1:2, pl.ds(begin, BQ)] = log_total[:, BQ:]
        return unused

    lax.fori_loop(0, length // BQ, one_block, 0)


def attend_backward(
    scalars, key_at, pairs, q_s, k_s, kt_s, v_s, o_s, do_s, lse_s, dq_s, dk_s, dv_s, first_s, after_s
):
    length = q_s.shape[1]
    scale = LOG2E / math.sqrt(HEAD_DIM)
    first, after = key_limits(scalars, key_at, length)
    first_s[...] = first
    after_s[...] = after
    rows = lax.broadcasted_iota(jnp.int32, (BK, BQ), 0)
    dk_s[...] = jnp.zeros_like(dk_s)
    dv_s[...] = jnp.zeros_like(dv_s)
    ones = jnp.ones((8, PAIR), F32)

    def one_block(index, unused):
        begin = pl.multiple_of(index * BQ, BQ)
        low, count = window(scalars, key_at, begin, BK)
        first_row = first_s[:, pl.ds(begin, BQ)]
        after_row = after_s[:, pl.ds(begin, BQ)]
        fixed = []
        for pair in pairs:
            query = two_heads(q_s[pair, pl.ds(begin, BQ), :])
            grad = two_heads(do_s[pair, pl.ds(begin, BQ), :])
            out = o_s[pair, pl.ds(begin, BQ), :].astype(F32)
            product = grad.astype(F32) * jnp.concatenate([out, out], axis=0)
            centre = lax.dot_general(
                ones,
                product,
                (((1,), (1,)), ((), ())),
                precision=lax.Precision.HIGHEST,
                preferred_element_type=F32,
            )[:1]
            log_total = jnp.concatenate(
                [lse_s[pair, 0:1, pl.ds(begin, BQ)], lse_s[pair, 1:2, pl.ds(begin, BQ)]], axis=1
            )
            fixed.append((query, grad, centre, log_total))

        def step(turn, carry):
            start = pl.multiple_of(low + turn * BK, ALIGN)
            allowed = (rows >= first_row - start) & (rows < after_row - start)
            allowed = jnp.concatenate([allowed, allowed], axis=1)
            results = []
            for pair, (query, grad, centre, log_total), dq in zip(pairs, fixed, carry):
                scores = dot_nt(k_s[pair, pl.ds(start, BK), :], query) * scale
                probs = jnp.exp2(jnp.where(allowed, scores, NEG_FILL) - log_total)
                dprobs = dot_nt(v_s[pair, pl.ds(start, BK), :], grad)
                dscores = (probs * (dprobs - centre)).astype(BF)
                dv_s[pair, pl.ds(start, BK), :] += dot(probs.astype(BF), grad)
                dk_s[pair, pl.ds(start, BK), :] += dot(dscores, query)
                kt = kt_s[pair, :, pl.ds(start, BK)]
                results.append(
                    [
                        dq[0] + dot(kt[:HEAD_DIM], dscores[:, :BQ]),
                        dq[1] + dot(kt[HEAD_DIM:], dscores[:, BQ:]),
                    ]
                )
            return results

        zero = jnp.zeros((HEAD_DIM, BQ), F32)
        results = lax.fori_loop(0, count, step, [[zero, zero] for unused_pair in pairs])
        for pair, dq in zip(pairs, results):
            dq = jnp.concatenate(dq, axis=0) * (1.0 / math.sqrt(HEAD_DIM))
            dq_s[pair, pl.ds(begin, BQ), :] = dq.T.astype(BF)
        return unused

    lax.fori_loop(0, length // BQ, one_block, 0)


def block_of(scalars, slot, size):
    return pl.multiple_of(scalars[PLACE_AT + slot] * size, size)


def clear_padding(length, k_s, t_s, v_s=None):
    pairs, padded = k_s.shape[:2]
    extra = padded - length
    k_s[:, pl.ds(length, extra), :] = jnp.zeros((pairs, extra, PAIR), BF)
    t_s[:, :, pl.ds(length, extra)] = jnp.zeros((pairs, PAIR, extra), BF)
    if v_s is not None:
        v_s[:, pl.ds(length, extra), :] = jnp.zeros((pairs, extra, PAIR), BF)


def hand_out(scalars, o_s, mine_o, send_o):
    size = mine_o.shape[1]
    for slot in range(4):
        place = block_of(scalars, slot, size)
        (mine_o if slot < 2 else send_o)[slot % 2] = o_s[pl.ds(place, size), :]


def self_forward_body(
    scalars, x0, x1, x2, x3, gains, w0, w1, q_o, k_o, v_o, mine_o, send_o, lse_o, k_s, vt_s, o_s, first_s, after_s
):
    size = x0.shape[0]
    length = q_o.shape[1]
    gain = gains[0:1, :]
    clear_padding(length, k_s, vt_s)
    for slot, x in enumerate((x0, x1, x2, x3)):
        place = block_of(scalars, slot, size)
        normal, unused = normalize(x[...].astype(F32))
        normed = (normal * gain).astype(BF)
        for pair, w in enumerate((w0, w1)):
            packed = dot(normed, w[...]).astype(BF)
            keys, values = packed[:, PAIR : 2 * PAIR], packed[:, 2 * PAIR :]
            q_o[pair, pl.ds(place, size), :] = packed[:, :PAIR]
            k_s[pair, pl.ds(place, size), :] = keys
            k_o[pair, pl.ds(place, size), :] = keys
            v_o[pair, pl.ds(place, size), :] = values
            vt_s[pair, :, pl.ds(place, size)] = values.T
    attend_forward(scalars, QUERY_AT, SELF_BK, (0, 1), q_o, k_s, vt_s, o_s, lse_o, first_s, after_s)
    hand_out(scalars, o_s, mine_o, send_o)


def cross_forward_body(
    scalars, cq0, cq1, m0, m1, m2, m3, w0, w1, q_o, k_o, v_o, mine_o, send_o, lse_o, k_s, vt_s, o_s, first_s, after_s
):
    size = m0.shape[0]
    length = q_o.shape[1]
    clear_padding(length, k_s, vt_s)
    for slot, memory in enumerate((m0, m1, m2, m3)):
        place = block_of(scalars, slot, size)
        source = cq0 if slot < 2 else cq1
        for pair, w in enumerate((w0, w1)):
            packed = dot(memory[...], wide_rows(w, 0, memory.shape[1], 2)).astype(BF)
            keys, values = packed[:, :PAIR], packed[:, PAIR:]
            k_s[pair, pl.ds(place, size), :] = keys
            k_o[pair, pl.ds(place, size), :] = keys
            v_o[pair, pl.ds(place, size), :] = values
            vt_s[pair, :, pl.ds(place, size)] = values.T
            q_o[pair, pl.ds(place, size), :] = source[
                pl.ds((slot % 2) * size, size), pair * PAIR : (pair + 1) * PAIR
            ]
    attend_forward(scalars, KEY_AT, CROSS_BK, (0, 1), q_o, k_s, vt_s, o_s, lse_o, first_s, after_s)
    hand_out(scalars, o_s, mine_o, send_o)


def load_backward(scalars, pairs, k, v, a0, a1, da0, da1, k_s, kt_s, v_s, o_s, do_s):
    size = a0.shape[1]
    length = k.shape[1]
    clear_padding(length, k_s, kt_s, v_s)
    for pair in range(pairs):
        k_s[pair, pl.ds(0, length), :] = k[pair]
        v_s[pair, pl.ds(0, length), :] = v[pair]
        lanes = slice(pair * PAIR, (pair + 1) * PAIR)
        for begin in range(0, length, 512):
            kt_s[pair, :, begin : begin + 512] = k[pair, begin : begin + 512, :].T
        for slot in range(4):
            place = block_of(scalars, slot, size)
            within = pl.ds((slot % 2) * size, size)
            do_s[pair, pl.ds(place, size), :] = (da0 if slot < 2 else da1)[within, lanes]
            o_s[pair, pl.ds(place, size), :] = (a0 if slot < 2 else a1)[slot % 2, :, lanes]


def cross_backward_body(
    scalars, q, k, v, a0, a1, lse, da0, da1, mine_o, send_o, dk_o, dv_o,
    k_s, kt_s, v_s, o_s, do_s, dq_s, dk_s, dv_s, first_s, after_s,
):
    size = a0.shape[1]
    length = k.shape[1]
    load_backward(scalars, 2, k, v, a0, a1, da0, da1, k_s, kt_s, v_s, o_s, do_s)
    attend_backward(
        scalars, KEY_AT, (0, 1), q, k_s, kt_s, v_s, o_s, do_s, lse, dq_s, dk_s, dv_s, first_s, after_s
    )
    for slot in range(4):
        place = block_of(scalars, slot, size)
        for pair in range(2):
            (mine_o if slot < 2 else send_o)[slot % 2, :, pair * PAIR : (pair + 1) * PAIR] = dq_s[
                pair, pl.ds(place, size), :
            ]
    dk_o[...] = (dk_s[:, pl.ds(0, length), :] * (1.0 / math.sqrt(HEAD_DIM))).astype(BF)
    dv_o[...] = dv_s[:, pl.ds(0, length), :].astype(BF)


def self_backward_body(
    scalars, q, k, v, a0, a1, lse, da0, da1, dqkv0_o, dqkv1_o,
    k_s, kt_s, v_s, o_s, do_s, dq_s, dk_s, dv_s, first_s, after_s,
):
    size = a0.shape[1]
    load_backward(scalars, 2, k, v, a0, a1, da0, da1, k_s, kt_s, v_s, o_s, do_s)
    attend_backward(
        scalars, QUERY_AT, (0, 1), q, k_s, kt_s, v_s, o_s, do_s, lse, dq_s, dk_s, dv_s, first_s, after_s
    )
    for pair, out in enumerate((dqkv0_o, dqkv1_o)):
        for slot in range(4):
            place = block_of(scalars, slot, size)
            out[slot, :, 0:PAIR] = dq_s[pair, pl.ds(place, size), :]
            out[slot, :, PAIR : 2 * PAIR] = (
                dk_s[pair, pl.ds(place, size), :] * (1.0 / math.sqrt(HEAD_DIM))
            ).astype(BF)
            out[slot, :, 2 * PAIR :] = dv_s[pair, pl.ds(place, size), :].astype(BF)


def wide_rows(ref, begin, rows, count):
    return jnp.concatenate(
        [ref[begin + i * rows : begin + (i + 1) * rows, :] for i in range(count)], axis=1
    )


def after_self_body(x0, x1, a0, a1, p0, p1, p2, p3, gains, h_o, cq0_o, cq1_o):
    size, wide = x0.shape
    packs = (p0, p1, p2, p3)
    w0, w1, w2, w3 = [wide_rows(p, 0, PAIR, wide // PAIR) for p in packs]
    u0, u1, u2, u3 = [p[wide : 2 * wide, :] for p in packs]
    for slot, x in enumerate((x0, x1)):
        here = pl.ds(slot * size, size)
        hidden = x[...].astype(F32)
        mine, other = a0[slot], a1[slot]
        width = w0.shape[0]
        hidden += dot(mine[:, :width], w0) + dot(mine[:, width:], w1)
        hidden += dot(other[:, :width], w2) + dot(other[:, width:], w3)
        h_o[here, :] = hidden
        normal, unused = normalize(hidden)
        normed = (normal * gains[1:2, :]).astype(BF)
        cq0_o[here, :] = jnp.concatenate([dot(normed, u0), dot(normed, u1)], axis=1).astype(BF)
        cq1_o[here, :] = jnp.concatenate([dot(normed, u2), dot(normed, u3)], axis=1).astype(BF)


GELU_C = math.sqrt(2.0 / math.pi)


def middle_body(
    scalars, h, a0, a1, p0, p1, p2, p3, ud0, ud1, ud2, ud3, gains, cot0, cot1,
    y0_o, y1_o, dh_o, da0_o, da1_o, keep_o, give_o, gain_o,
    h_s, n_s, g_s, acc_s, dn_s,
):
    size = cot0.shape[0]
    used = scalars[QUERY_AT + DOCS]
    wide = h.shape[1]
    width = PAIR
    units = ud0.shape[0] * PAIR // (2 * wide)
    w0, w1, w2, w3 = [wide_rows(p, 0, width, wide // PAIR) for p in (p0, p1, p2, p3)]
    for slot, cot in enumerate((cot0, cot1)):
        here = pl.ds(slot * size, size)
        mine, other = a0[slot], a1[slot]
        hidden = h[here, :] + dot(mine[:, :width], w0) + dot(mine[:, width:], w1)
        hidden += dot(other[:, :width], w2) + dot(other[:, width:], w3)
        h_s[here, :] = hidden
        normal, unused = normalize(hidden)
        n_s[here, :] = (normal * gains[2:3, :]).astype(BF)
        place = lax.broadcasted_iota(jnp.int32, (size, 1), 0) + scalars[PLACE_AT + slot] * size
        g_s[here, :] = jnp.where(place < used, cot[...].astype(F32), 0.0).astype(BF)
    acc_s[...] = jnp.zeros_like(acc_s)
    dn_s[...] = jnp.zeros_like(dn_s)
    for shard, ud in enumerate((ud0, ud1, ud2, ud3)):
        w_up = wide_rows(ud, 0, wide, units // PAIR)
        w_down = wide_rows(ud, wide * units // PAIR, units, wide // PAIR)
        grad_up = jnp.zeros(w_up.shape, F32)
        grad_down = jnp.zeros(w_down.shape, F32)
        for begin in range(0, 2 * size, size):
            here = pl.ds(begin, size)
            normed = n_s[here, :]
            grad = g_s[here, :]
            upper = dot(normed, w_up)
            square = upper * upper
            inner_arg = GELU_C * upper * (1.0 + 0.044715 * square)
            bent = jnp.tanh(inner_arg)
            half = 0.5 * (1.0 + bent)
            inner = (upper * half).astype(BF)
            slope = half + 0.5 * upper * (1.0 - bent * bent) * (GELU_C * (1.0 + 3.0 * 0.044715 * square))
            acc_s[here, :] += dot(inner, w_down)
            d_upper = (dot_nt(grad, w_down) * slope).astype(BF)
            dn_s[here, :] += dot_nt(d_upper, w_up)
            grad_up += dot_tn(normed, d_upper)
            grad_down += dot_tn(inner, grad)
        out = keep_o if shard < 2 else give_o
        out[shard % 2, 0:wide, :] = grad_up.astype(BF)
        out[shard % 2, wide : wide + units, :] = grad_down.astype(BF)
    gain_total = jnp.zeros((1, h_s.shape[1]), F32)
    grad_heads = [jnp.zeros((width, h_s.shape[1]), F32) for unused in range(4)]
    for slot, y_o in enumerate((y0_o, y1_o)):
        here = pl.ds(slot * size, size)
        hidden = h_s[here, :]
        y_o[...] = (hidden + acc_s[here, :]).astype(BF)
        normal, inv_sigma = normalize(hidden)
        dn = dn_s[here, :]
        gain_total += jnp.sum(dn * normal, axis=0, keepdims=True)
        dh = g_s[here, :].astype(F32) + normalize_back(dn, gains[2:3, :], normal, inv_sigma)
        dh_o[here, :] = dh
        low = dh.astype(BF)
        da0_o[here, :] = jnp.concatenate([dot_nt(low, w0), dot_nt(low, w1)], axis=1).astype(BF)
        da1_o[here, :] = jnp.concatenate([dot_nt(low, w2), dot_nt(low, w3)], axis=1).astype(BF)
        mine, other = a0[slot], a1[slot]
        parts = (mine[:, :width], mine[:, width:], other[:, :width], other[:, width:])
        grad_heads = [total + dot_tn(part, low) for total, part in zip(grad_heads, parts)]
    for shard in range(4):
        out = keep_o if shard < 2 else give_o
        out[shard % 2, wide + units : wide + units + width, :] = grad_heads[shard].astype(BF)
    gain_o[...] = jnp.broadcast_to(gain_total, gain_o.shape)


def between_body(
    h, dh2, a0, a1, dq0, dq1, p0, p1, p2, p3, gains,
    dh_o, da0_o, da1_o, keep_o, give_o, gain_o,
):
    size = a0.shape[1]
    width = PAIR
    wide = h.shape[1]
    packs = (p0, p1, p2, p3)
    w0, w1, w2, w3 = [wide_rows(p, 0, width, wide // PAIR) for p in packs]
    u0, u1, u2, u3 = [p[wide : 2 * wide, :] for p in packs]
    gain_total = jnp.zeros((1, wide), F32)
    grad_out = [jnp.zeros((width, wide), F32) for unused in range(4)]
    grad_query = [jnp.zeros((wide, width), F32) for unused in range(4)]
    for slot in range(2):
        here = pl.ds(slot * size, size)
        normal, inv_sigma = normalize(h[here, :])
        normed = (normal * gains[1:2, :]).astype(BF)
        mine, other = dq0[slot], dq1[slot]
        pieces = (mine[:, :width], mine[:, width:], other[:, :width], other[:, width:])
        dn = jnp.zeros((size, wide), F32)
        for piece, u in zip(pieces, (u0, u1, u2, u3)):
            dn += dot_nt(piece, u)
        grad_query = [total + dot_tn(normed, piece) for total, piece in zip(grad_query, pieces)]
        gain_total += jnp.sum(dn * normal, axis=0, keepdims=True)
        dh = dh2[here, :] + normalize_back(dn, gains[1:2, :], normal, inv_sigma)
        dh_o[here, :] = dh
        low = dh.astype(BF)
        da0_o[here, :] = jnp.concatenate([dot_nt(low, w0), dot_nt(low, w1)], axis=1).astype(BF)
        da1_o[here, :] = jnp.concatenate([dot_nt(low, w2), dot_nt(low, w3)], axis=1).astype(BF)
        mine, other = a0[slot], a1[slot]
        parts = (mine[:, :width], mine[:, width:], other[:, :width], other[:, width:])
        grad_out = [total + dot_tn(part, low) for total, part in zip(grad_out, parts)]
    for shard in range(4):
        out = keep_o if shard < 2 else give_o
        out[shard % 2, 0:wide, :] = grad_query[shard].astype(BF)
        for part in range(wide // width):
            out[shard % 2, wide + part * width : wide + (part + 1) * width, :] = grad_out[shard][
                :, part * width : (part + 1) * width
            ].astype(BF)
    gain_o[...] = jnp.broadcast_to(gain_total, gain_o.shape)


def memory_back_body(scalars, dk, dv, m0, m1, m2, m3, w0, w1, mine_o, send_o, keep_o, give_o):
    size = m0.shape[0]
    wide = m0.shape[1]
    totals = [jnp.zeros((wide, 2 * PAIR), F32) for unused in range(2)]
    for slot, memory in enumerate((m0, m1, m2, m3)):
        place = block_of(scalars, slot, size)
        total = jnp.zeros((size, wide), F32)
        for pair, w in enumerate((w0, w1)):
            part = jnp.concatenate([dk[pair, pl.ds(place, size), :], dv[pair, pl.ds(place, size), :]], axis=1)
            total += dot_nt(part, wide_rows(w, 0, memory.shape[1], 2))
            totals[pair] += dot_tn(memory[...], part)
        (mine_o if slot < 2 else send_o)[slot % 2] = total.astype(BF)
    for total, out in zip(totals, (keep_o, give_o)):
        out[0:wide, :] = total[:, :PAIR].astype(BF)
        out[wide : 2 * wide, :] = total[:, PAIR:].astype(BF)


def qkv_grad_body(
    dqkv0, dqkv1, x0, x1, x2, x3, gains, w0, w1, gain_two, gain_three, keep_o, give_o, gain_o
):
    wide = x0.shape[1]
    totals = [jnp.zeros((wide, 3 * PAIR), F32) for unused in range(2)]
    for slot, x in enumerate((x0, x1, x2, x3)):
        normal, unused = normalize(x[...].astype(F32))
        normed = (normal * gains[0:1, :]).astype(BF)
        totals = [t + dot_tn(normed, d[slot]) for t, d in zip(totals, (dqkv0, dqkv1))]
    for part in range(3):
        here = slice(part * wide, (part + 1) * wide)
        lanes = slice(part * PAIR, (part + 1) * PAIR)
        keep_o[here, :] = totals[0][:, lanes]
        give_o[here, :] = totals[1][:, lanes].astype(BF)
    product = totals[0] * w0[...].astype(F32) + totals[1] * w1[...].astype(F32)
    gain = lax.dot_general(
        jnp.ones((8, 3 * PAIR), F32),
        product,
        (((1,), (1,)), ((), ())),
        precision=lax.Precision.HIGHEST,
        preferred_element_type=F32,
    ) / gains[0:1, :]
    gain_o[...] = jnp.concatenate(
        [gain[:1], gain_two[:1, :], gain_three[:1, :], jnp.zeros((5, wide), F32)], axis=0
    )


def back_to_input_body(dqkv0, dqkv1, w0, w1, mine_o, send_o):
    for slot in range(4):
        dn = dot_nt(dqkv0[slot], w0[...]) + dot_nt(dqkv1[slot], w1[...])
        (mine_o if slot < 2 else send_o)[slot % 2] = dn.astype(BF)


def input_grad_body(dn0, dn1, x0, x1, dh, gains, g0_o, g1_o):
    size = x0.shape[0]
    for slot, (x, g_o) in enumerate(((x0, g0_o), (x1, g1_o))):
        here = pl.ds(slot * size, size)
        normal, inv_sigma = normalize(x[...].astype(F32))
        dn = dn0[slot].astype(F32) + dn1[slot].astype(F32)
        g_o[...] = (dh[here, :] + normalize_back(dn, gains[0:1, :], normal, inv_sigma)).astype(BF)


def pick_body(order, source, out):
    def one(i, unused):
        out[i] = source[order[i]]
        return unused

    lax.fori_loop(0, source.shape[0], one, 0)


def pick(array, order):
    return call(pick_body, struct(array.shape, array.dtype), [], "pick", 1)(
        order, array, specs=[SMEM, VM]
    )


def pick_memory_body(order, source, out, digits_o):
    count, share = out.shape[:2]

    def one(i, unused):
        out[i] = source[order[i], 0:share, :]
        return unused

    lax.fori_loop(0, count, one, 0)
    digits_o[...] = source[order[order[count]], share:, :]


def spread_rows(block):
    return lax.all_to_all(block, "dp", split_axis=0, concat_axis=0, tiled=True)


def swap_chip(array):
    return lax.ppermute(array, "tensor", [(i, i ^ 2) for i in range(4)])


def swap_core(array):
    return lax.ppermute(array, "tensor", [(i, i ^ 1) for i in range(4)])


def pack_body(*refs):
    out = refs[-1]
    at = 0
    for ref in refs[:-1]:
        rows, lanes = ref.shape
        for begin in range(0, lanes, PAIR):
            out[at : at + rows, :] = ref[:, begin : begin + PAIR]
            at += rows


def pack(*arrays, cost):
    rows = sum(a.size for a in arrays) // PAIR
    return call(pack_body, struct((rows, PAIR), arrays[0].dtype), [], "pack", cost)(
        *arrays, specs=[VM] * len(arrays)
    )


def swap_row(array, bit):
    return lax.ppermute(array, "dp", [(i, i ^ bit) for i in range(lax.axis_size("dp"))])


def halves(array, upper):
    half = array.shape[0] // 2
    low, high = array[:half], array[half:]
    return jnp.where(upper, high, low), jnp.where(upper, low, high).astype(BF)


def rest_groups():
    count = lax.axis_size("dp")
    return [[i for i in range(count) if i % 2 == part] for part in range(2)]


def rest_sends(arrays):
    group = lax.axis_size("dp") // 2
    width = arrays[0].shape[1]
    joint = jnp.concatenate([a.reshape(group, -1, width) for a in arrays], axis=1)
    me = lax.axis_index("dp") // 2

    def piece(index):
        return lax.dynamic_index_in_dim(joint, index, 0, keepdims=False)

    if group != 4:
        return piece(me), [joint.reshape(-1, width)]
    return piece(me), [piece(me ^ k) for k in (1, 2, 3)]


def rest_move(sends):
    if len(sends) == 3:
        return [swap_row(send, 2 * k) for k, send in zip((1, 2, 3), sends)]
    group = lax.axis_size("dp") // 2
    spread = lax.all_to_all(
        sends[0], "dp", split_axis=0, concat_axis=0, axis_index_groups=rest_groups(), tiled=True
    )
    return [spread.reshape(group, -1, spread.shape[1])]


def add_all(own, got):
    if got[0].ndim == own.ndim:
        return sum([g.astype(F32) for g in got], own.astype(F32))
    return jnp.sum(got[0].astype(F32), axis=0)


def rest_collect(piece):
    if lax.axis_size("dp") == 8:
        return [piece] + [swap_row(piece, 2 * k) for k in (1, 2, 3)]
    return [lax.all_gather(piece, "dp", axis=0, axis_index_groups=rest_groups(), tiled=True)]


def assemble_body(order, *refs):
    out = refs[-1]
    for index, ref in enumerate(refs[:-1]):
        out[order[index]] = ref[...]


def rest_assemble(pieces):
    if len(pieces) == 1:
        return pieces[0]
    me = lax.axis_index("dp") // 2
    order = (jnp.arange(4, dtype=jnp.int32) ^ me).astype(jnp.int32)
    return call(assemble_body, struct((4,) + pieces[0].shape, BF), [], "assemble", 1)(
        order, *pieces, specs=[SMEM] + [VM] * 4
    ).reshape(-1, pieces[0].shape[1])


def finish_one_body(flag, half, other, up_o, down_o, co_o):
    upper = flag[0] != 0
    low = jnp.where(upper, other[...], half[...]).astype(F32)
    high = jnp.where(upper, half[...], other[...]).astype(F32)
    wide, units = up_o.shape[0], down_o.shape[0]
    split = low.shape[0] - wide
    up_o[...] = low[:wide]
    down_o[0:split, :] = low[wide:]
    down_o[split:, :] = high[: units - split]
    co_o[...] = high[units - split :]


def finish_two(cq_o, so_o, kv_o, two_s):
    wide = cq_o.shape[0]
    cq_o[...] = two_s[0:wide, :]
    for i in range(wide // PAIR):
        so_o[:, i * PAIR : (i + 1) * PAIR] = two_s[wide + i * PAIR : wide + (i + 1) * PAIR, :]
    kv_o[pl.ds(0, wide, stride=2), :] = two_s[2 * wide : 3 * wide, :]
    kv_o[pl.ds(1, wide, stride=2), :] = two_s[3 * wide :, :]


def finish_rest_body(flag, half, other, cq_o, so_o, kv_o, qkv_o, gain_o, two_s):
    upper = flag[0] != 0
    group = half.shape[0]
    two, three = two_s.shape[0] // (2 * group), qkv_o.shape[0] // (2 * group)
    gain = jnp.zeros(gain_o.shape, F32)
    for index in range(group):
        low = jnp.where(upper, other[index], half[index]).astype(F32)
        high = jnp.where(upper, half[index], other[index]).astype(F32)
        for at, piece in ((index, low), (group + index, high)):
            two_s[at * two : (at + 1) * two, :] = piece[0:two]
            qkv_o[at * three : (at + 1) * three, :] = piece[two : two + three]
            gain += piece[two + three :]
    finish_two(cq_o, so_o, kv_o, two_s)
    gain_o[...] = gain


def finish_pieces_body(flag, order, p0, p1, p2, p3, r0, r1, r2, r3, cq_o, so_o, kv_o, qkv_o, gain_o, two_s):
    upper = flag[0] != 0
    two, three = two_s.shape[0] // 8, qkv_o.shape[0] // 8
    gain = jnp.zeros(gain_o.shape, F32)
    for index, (mine, other) in enumerate(((p0, r0), (p1, r1), (p2, r2), (p3, r3))):
        low = jnp.where(upper, other[...], mine[...]).astype(F32)
        high = jnp.where(upper, mine[...], other[...]).astype(F32)
        for first, piece in ((0, low), (4, high)):
            at = first + order[index]
            two_s[pl.ds(pl.multiple_of(at * two, two), two), :] = piece[0:two]
            qkv_o[pl.ds(pl.multiple_of(at * three, three), three), :] = piece[two : two + three]
            gain += piece[two + three :]
    finish_two(cq_o, so_o, kv_o, two_s)
    gain_o[...] = gain


def on_device(
    x_first,
    x_second,
    memory,
    cot_first,
    cot_second,
    seg_ids,
    lengths,
    perm,
    inverse,
    gains,
    w_self_qkv,
    w_self_out,
    w_cross_q,
    w_cross_kv,
    w_cross_out,
    w_up,
    w_down,
):
    length = seg_ids.shape[2]
    size = x_first.shape[1]
    wide = x_first.shape[2]
    width = w_self_out.shape[0]
    units = w_up.shape[1]
    mine = 2 * size
    heads = 2 * width
    me = lax.axis_index("tensor")
    row = lax.axis_index("dp")
    rows = perm.shape[0]
    share = size // rows
    first_step = me < 2
    upper = (row & 1) != 0

    def both(one, two):
        return jnp.where(first_step, one, two)

    def stage(**values):
        return types.SimpleNamespace(**lax.optimization_barrier(values))

    pair_array = struct((2, length, PAIR), BF)
    out_half = struct((2, size, heads), BF)
    lse_array = struct((2, 2, length), F32)
    limits = [pltpu.VMEM((1, length), jnp.int32), pltpu.VMEM((1, length), jnp.int32)]
    def forward_scratch(key_block):
        return [
            pltpu.VMEM((2, length + key_block - ALIGN, PAIR), BF),
            pltpu.VMEM((2, PAIR, length + key_block - ALIGN), BF),
            pltpu.VMEM((length, heads), BF),
        ] + limits

    whole = pl.BlockSpec(memory_space=pltpu.VMEM)

    def part_of(rows_of_block, index):
        return pl.BlockSpec((rows_of_block, PAIR), lambda i: (index, 0))

    x_first, x_second, memory = x_first[0], x_second[0], memory[0]
    x_got = swap_chip(both(x_second, x_first))
    wqkv_own = w_self_qkv.reshape(wide, -1)
    wqkv_got = swap_chip(wqkv_own)
    x_own = both(x_first, x_second)
    place = jnp.arange(length, dtype=jnp.int32)
    meta = jnp.where(place[None, :] < lengths[0][:, None], seg_ids[0], DOCS)
    docs = jnp.arange(DOCS + 2, dtype=jnp.int32)
    cuts = jnp.sum((meta[:, None, :] < docs[None, :, None]).astype(jnp.int32), axis=-1).reshape(-1)
    digits = jnp.stack([cuts // 64, cuts % 64]).astype(BF)
    digits = jnp.pad(digits, ((0, 14), (0, wide - cuts.shape[0])))
    payload = jnp.concatenate(
        [memory.reshape(rows, share, wide), jnp.broadcast_to(digits[None], (rows, 16, wide))], axis=1
    )
    x_sib0 = swap_core(x_own)
    x_got, wqkv_got, own_out = lax.optimization_barrier((x_got, wqkv_got, w_self_out))
    pack_a = pack(own_out, w_cross_q, w_cross_kv.reshape(wide, -1), w_cross_out, cost=30)
    pack_b = pack(w_up, w_down, cost=2)
    spread = spread_rows(payload.reshape(-1, wide)).reshape(payload.shape)
    cot_own = both(cot_first[0], cot_second[0])
    cot_send = both(cot_second[0], cot_first[0])
    x_sib1 = swap_core(x_got)
    picked, digits = call(
        pick_memory_body,
        (struct((rows, share, wide), BF), struct((16, wide), BF)),
        [],
        "pick_memory",
        2,
    )(jnp.concatenate([perm, row[None].astype(jnp.int32)]), spread, specs=[SMEM, VM])
    s = stage(
        x_got=x_got,
        x_sib1=x_sib1,
        digits=digits,
        wqkv_own=wqkv_own,
        wqkv_got=wqkv_got,
        pack_a=pack_a,
        pack_b=pack_b,
        cot_own=cot_own,
        cot_send=cot_send,
        x_sib0=x_sib0,
        cuts=cuts,
        memory=memory,
    )
    pack_a, pack_b, cot_own, cot_send = (s.pack_a, s.pack_b, s.cot_own, s.cot_send)
    x_sib0, cuts, memory = s.x_sib0, s.cuts, s.memory
    x_got, x_sib1, wqkv_own, wqkv_got = (s.x_got, s.x_sib1, s.wqkv_own, s.wqkv_got)
    digits = s.digits
    digits = digits[:2, : cuts.shape[0]].astype(jnp.int32)
    cuts = both(digits[0] * 64 + digits[1], cuts)
    places = jnp.stack([me, me ^ 2, me ^ 1, me ^ 3]).astype(jnp.int32)
    s = stage(
        scalars=jnp.concatenate([cuts, places]),
        x0=x_own,
        x1=x_got,
        x2=x_sib0,
        x3=x_sib1,
        w0=wqkv_own,
        w1=wqkv_got,
        picked=picked,
        pack_a=pack_a,
        pack_b=pack_b,
        cot_own=cot_own,
        cot_send=cot_send,
        memory=memory,
    )
    scalars = s.scalars
    xs = (s.x0, s.x1, s.x2, s.x3)
    wqkv = (s.w0, s.w1)
    memory = s.memory

    memory_one = spread_rows(picked.reshape(memory.shape))
    q, k, v, a_mine, a_send, lse = call(
        self_forward_body,
        (pair_array, pair_array, pair_array, out_half, out_half, lse_array),
        forward_scratch(SELF_BK),
        "self_forward",
        4,
    )(scalars, *xs, gains, *wqkv, specs=[SMEM] + [VM] * 7)
    pack_a, pack_b = s.pack_a, s.pack_b
    s = stage(
        q=q,
        k=k,
        v=v,
        a_mine=a_mine,
        a_send=a_send,
        lse=lse,
        memory_one=memory_one,
        a_got=swap_chip(pack_a),
        cot_got=swap_chip(s.cot_send),
        pack_a2=swap_core(pack_a),
        pack_b2=swap_core(pack_b),
    )
    q, k, v, a_mine, a_send, lse = (s.q, s.k, s.v, s.a_mine, s.a_send, s.lse)
    pack_a1, pack_a2, pack_b2, cot_got = s.a_got, s.pack_a2, s.pack_b2, s.cot_got
    memory_one = s.memory_one
    m_got = swap_chip(both(memory, memory_one))
    s = stage(
        a_got=swap_core(a_send),
        pack_a3=swap_core(pack_a1),
        m_own=both(memory_one, memory),
    )
    a_got, m_own = s.a_got, s.m_own
    packs_a = (pack_a, pack_a1, pack_a2, s.pack_a3)

    so_cq = part_of(2 * wide, 0)
    h1, cq_mine, cq_send = call(
        after_self_body,
        (struct((mine, wide), F32), struct((mine, heads), BF), struct((mine, heads), BF)),
        [],
        "after_self",
        6,
        (1,),
    )(
        *xs[:2], a_mine, a_got, *packs_a, gains, specs=[whole] * 4 + [so_cq] * 4 + [whole]
    )
    h1, m_got = lax.optimization_barrier((h1, m_got))
    s = stage(
        h1=h1,
        cq_mine=cq_mine,
        cq_got=swap_core(cq_send),
        m1=m_got,
        m2=swap_core(m_own),
        m3=swap_core(m_got),
        pack_b=pack_b,
    )
    h1, cq_mine, cq_got, pack_b = s.h1, s.cq_mine, s.cq_got, s.pack_b
    ms = (m_own, s.m1, s.m2, s.m3)

    kv = part_of(2 * wide, 1)
    cq, ck, cv, b_mine, b_send, lse_b = call(
        cross_forward_body,
        (pair_array, pair_array, pair_array, out_half, out_half, lse_array),
        forward_scratch(CROSS_BK),
        "cross_forward",
        24,
        (1,),
    )(
        scalars,
        cq_mine,
        cq_got,
        *ms,
        pack_a,
        pack_a1,
        specs=[SMEM] + [whole] * 6 + [kv] * 2,
    )
    s = stage(
        cq=cq,
        ck=ck,
        cv=cv,
        b_mine=b_mine,
        b_send=b_send,
        lse_b=lse_b,
        pack_b1=swap_chip(pack_b),
    )
    cq, ck, cv, b_mine, b_send, lse_b = (s.cq, s.ck, s.cv, s.b_mine, s.b_send, s.lse_b)
    pack_b1 = s.pack_b1
    s = stage(b_got=swap_core(b_send), pack_b3=swap_core(pack_b1))

    co = part_of(wide, 4)
    rows_one = wide + units + width
    (
        y_own, y_send, dh2, db_mine, db_send, one_keep, one_give, gain_three,
    ) = call(
        middle_body,
        (
            struct((size, wide), BF),
            struct((size, wide), BF),
            struct((mine, wide), F32),
            struct((mine, heads), BF),
            struct((mine, heads), BF),
            struct((2, rows_one, wide), BF),
            struct((2, rows_one, wide), BF),
            struct((8, wide), F32),
        ),
        [
            pltpu.VMEM((mine, wide), F32),
            pltpu.VMEM((mine, wide), BF),
            pltpu.VMEM((mine, wide), BF),
            pltpu.VMEM((mine, wide), F32),
            pltpu.VMEM((mine, wide), F32),
        ],
        "middle",
        25,
        (1,),
    )(
        scalars,
        h1,
        b_mine,
        s.b_got,
        *packs_a,
        pack_b,
        pack_b1,
        pack_b2,
        s.pack_b3,
        gains,
        cot_own,
        cot_got,
        specs=[SMEM] + [whole] * 3 + [co] * 4 + [whole] * 7,
    )

    def over_core(keep, got):
        own = keep[0].astype(F32) + got[0].astype(F32)
        other = keep[1].astype(F32) + got[1].astype(F32)
        return own, other.astype(BF)

    one_own, one_send = over_core(one_keep, swap_core(one_give))
    s = stage(
        y_own=y_own,
        y_send=y_send,
        dh2=dh2,
        db_mine=db_mine,
        db_got=swap_core(db_send),
        one_own=one_own,
        one_send=one_send,
        gain_three=gain_three,
    )
    y_own, y_send, dh2, one_own = s.y_own, s.y_send, s.dh2, s.one_own
    gain_three = s.gain_three

    backward_scratch = [
        pltpu.VMEM((2, length + BK - ALIGN, PAIR), BF),
        pltpu.VMEM((2, PAIR, length + BK - ALIGN), BF),
        pltpu.VMEM((2, length + BK - ALIGN, PAIR), BF),
        pltpu.VMEM((2, length, PAIR), BF),
        pltpu.VMEM((2, length, PAIR), BF),
        pltpu.VMEM((2, length, PAIR), BF),
        pltpu.VMEM((2, length + BK - ALIGN, PAIR), F32),
        pltpu.VMEM((2, length + BK - ALIGN, PAIR), F32),
    ] + limits
    dcq_mine, dcq_send, dck, dcv = call(
        cross_backward_body,
        (out_half, out_half, pair_array, pair_array),
        backward_scratch,
        "cross_backward",
        27,
    )(
        scalars, cq, ck, cv, b_mine, b_send, lse_b, s.db_mine, s.db_got,
        specs=[SMEM] + [VM] * 8,
    )
    s = stage(
        dcq_mine=dcq_mine,
        dcq_send=dcq_send,
        dck=dck,
        dcv=dcv,
        one_got=swap_chip(s.one_send),
        one_own=one_own,
    )
    dcq_mine = s.dcq_mine
    one_keep, one_send = halves(s.one_own + s.one_got.astype(F32), upper)
    one_got = swap_row(one_send, 1)
    dm_mine, dm_send, keep_kv, give_kv = call(
        memory_back_body,
        (
            struct((2, size, wide), BF),
            struct((2, size, wide), BF),
            struct((2 * wide, width), BF),
            struct((2 * wide, width), BF),
        ),
        [],
        "memory_back",
        6,
        (1,),
    )(
        scalars, s.dck, s.dcv, *ms, pack_a, pack_a1, specs=[SMEM] + [whole] * 6 + [kv] * 2
    )
    dm_core = swap_core(dm_send)
    dm_own, dm_other = [
        (dm_mine[i].astype(F32) + dm_core[i].astype(F32)).astype(BF) for i in range(2)
    ]
    s = stage(
        dcq_got=swap_core(s.dcq_send),
        one_keep=one_keep,
        dm_own=dm_own,
        dm_other=dm_other,
        keep_kv=keep_kv,
        give_kv=give_kv,
    )
    one_keep, dm_own, keep_kv, give_kv = (s.one_keep, s.dm_own, s.keep_kv, s.give_kv)

    dh1, da_mine, da_send, keep_two, give_two, gain_two = call(
        between_body,
        (
            struct((mine, wide), F32),
            struct((mine, heads), BF),
            struct((mine, heads), BF),
            struct((2, 2 * wide, width), BF),
            struct((2, 2 * wide, width), BF),
            struct((8, wide), F32),
        ),
        [],
        "between",
        3,
        (1,),
    )(
        h1, dh2, a_mine, a_got, dcq_mine, s.dcq_got, *packs_a, gains,
        specs=[whole] * 6 + [so_cq] * 4 + [whole],
    )
    s = stage(
        dh1=dh1,
        da_mine=da_mine,
        da_send=da_send,
        keep_two=keep_two,
        give_two=give_two,
        gain_two=gain_two,
        one_got=one_got,
        one_keep=one_keep,
        dm_got=swap_chip(s.dm_other),
        dm_own=dm_own,
    )
    dh1, da_mine, gain_two = s.dh1, s.da_mine, s.gain_two
    one_own, one_sends = rest_sends([(s.one_keep + s.one_got.astype(F32)).astype(BF)])
    two_own, two_send = over_core(s.keep_two, swap_core(s.give_two))
    s = stage(
        da_got=swap_core(s.da_send),
        dm_one=both(s.dm_own, s.dm_got),
        dm_two=both(s.dm_got, s.dm_own),
        two_own=two_own,
        two_send=jnp.concatenate([two_send, give_kv], axis=0),
        y_send=y_send,
        one_own=one_own,
        one_sends=one_sends,
    )
    two_own, dm_two, one_own = s.two_own, s.dm_two, s.one_own

    qkv_rows = struct((4, size, 3 * PAIR), BF)
    dqkv0, dqkv1 = call(
        self_backward_body, (qkv_rows, qkv_rows), backward_scratch, "self_backward", 32
    )(
        scalars, q, k, v, a_mine, a_send, lse, da_mine, s.da_got, specs=[SMEM] + [VM] * 8
    )
    s = stage(
        dqkv0=dqkv0,
        dqkv1=dqkv1,
        two_got=swap_chip(s.two_send),
        two_own=two_own,
        y_got=swap_chip(s.y_send),
        y_own=y_own,
        dm_spread=spread_rows(s.dm_one),
        dm_two=dm_two,
        keep_kv=keep_kv,
        one_own=one_own,
        one_got=rest_move(s.one_sends),
    )
    dqkv0, dqkv1, dm_two = s.dqkv0, s.dqkv1, s.dm_two
    two_total = jnp.concatenate(
        [
            s.two_own + s.two_got[: 2 * wide].astype(F32),
            s.keep_kv.astype(F32) + s.two_got[2 * wide :].astype(F32),
        ],
        axis=0,
    )
    two_keep, two_send = halves(two_total, upper)
    s = stage(
        two_keep=two_keep,
        two_send=two_send,
        dm_picked=pick(s.dm_spread.reshape(rows, -1, wide), inverse),
        y_own=s.y_own,
        y_got=s.y_got,
        one_piece=add_all(s.one_own, s.one_got).astype(BF),
    )
    two_keep, y_own, y_got = s.two_keep, s.y_own, s.y_got

    dm_back = spread_rows(s.dm_picked.reshape(memory.shape))
    one_pieces = rest_collect(s.one_piece)
    qkv_gradient = (3 * wide, width)
    gain_row = struct((8, wide), F32)
    keep_qkv, give_qkv, gain_all = call(
        qkv_grad_body,
        (struct(qkv_gradient, F32), struct(qkv_gradient, BF), gain_row),
        [],
        "qkv_grad",
        8,
    )(dqkv0, dqkv1, *xs, gains, *wqkv, gain_two, gain_three, specs=[VM] * 11)
    s = stage(
        keep_qkv=keep_qkv,
        give_qkv=give_qkv,
        gain_all=gain_all,
        two_got=swap_row(s.two_send, 1),
        two_keep=two_keep,
        dqkv0=dqkv0,
        dqkv1=dqkv1,
    )
    keep_qkv, gain_all = s.keep_qkv, s.gain_all
    dqkv0, dqkv1 = s.dqkv0, s.dqkv1

    qkv_got = swap_chip(s.give_qkv)
    dn_mine, dn_send = call(
        back_to_input_body,
        (struct((2, size, wide), BF), struct((2, size, wide), BF)),
        [],
        "back_to_input",
        4,
    )(dqkv0, dqkv1, *wqkv, specs=[VM] * 4)
    s = stage(
        keep_qkv=keep_qkv,
        gain_all=gain_all,
        qkv_got=qkv_got,
        dn_mine=dn_mine,
        dn_send=dn_send,
        two_got=s.two_got,
        two_keep=s.two_keep,
        dm_back=dm_back,
        one_pieces=one_pieces,
    )
    dn_mine, dm_back, one_pieces = s.dn_mine, s.dm_back, s.one_pieces
    three_keep, three_send = halves(s.keep_qkv + s.qkv_got.astype(F32), upper)
    s = stage(
        three_keep=three_keep,
        three_send=three_send,
        two_half=(s.two_keep + s.two_got.astype(F32)).astype(BF),
        gain_all=s.gain_all,
        dn_got=swap_core(s.dn_send),
    )
    two_half = s.two_half

    grad_own, grad_send = call(
        input_grad_body,
        (struct((size, wide), BF), struct((size, wide), BF)),
        [],
        "input_grad",
        5,
    )(dn_mine, s.dn_got, *xs[:2], dh1, gains, specs=[VM] * 6)
    s = stage(
        three_got=swap_row(s.three_send, 1),
        three_keep=s.three_keep,
        gain_all=s.gain_all + swap_core(s.gain_all),
        grad_own=grad_own,
        grad_send=grad_send,
        y_own=y_own,
        y_got=y_got,
        dm_two=dm_two,
        dm_back=dm_back,
        one_half=rest_assemble(one_pieces),
    )
    one_half, grad_own = s.one_half, s.grad_own
    three_half = (s.three_keep + s.three_got.astype(F32)).astype(BF)
    share_two, share_three = two_half.shape[0], three_half.shape[0]
    last_own, last_sends = rest_sends([two_half, three_half])

    y_first = both(s.y_own, s.y_got)
    y_second = both(s.y_got, s.y_own)
    grad_memory = s.dm_two.astype(F32) + s.dm_back.astype(F32)
    s = stage(
        last_own=last_own,
        last_got=rest_move(last_sends),
        gain_all=s.gain_all + swap_chip(s.gain_all),
        grad_own=grad_own,
        grad_send=s.grad_send,
        one_half=one_half,
        one_other=swap_row(one_half, 1),
        y_first=y_first,
        y_second=y_second,
        grad_memory=grad_memory,
    )
    one_half, one_other, grad_own = s.one_half, s.one_other, s.grad_own
    y_first, y_second, grad_memory = s.y_first, s.y_second, s.grad_memory
    grad_got = swap_chip(s.grad_send)
    gain_rows = 8 * wide // width
    last = jnp.concatenate(
        [
            add_all(s.last_own, s.last_got).astype(BF),
            s.gain_all.astype(BF).reshape(gain_rows, width),
        ],
        axis=0,
    )
    pieces = rest_collect(last)
    others = [swap_row(piece, 1) for piece in pieces]
    flag = (row & 1)[None].astype(jnp.int32)
    grad_up, grad_down, grad_cross_out = call(
        finish_one_body,
        (struct((wide, units), F32), struct((units, wide), F32), struct((width, wide), F32)),
        [],
        "finish_one",
        2,
    )(flag, one_half, one_other, specs=[SMEM, VM, VM])
    slab = struct((wide, width), F32)
    group = (rows // 2, last.shape[0], width)
    if len(pieces) == 1:
        operands = [array[0].reshape(group) for array in (pieces, others)]
        specs = [SMEM, VM, VM]
    else:
        order = (jnp.arange(4, dtype=jnp.int32) ^ (row // 2)).astype(jnp.int32)
        operands = [order] + pieces + others
        specs = [SMEM, SMEM] + [VM] * 8
    grad_cross_q, grad_self_out, grad_kv, grad_qkv, gain_total = call(
        finish_rest_body if len(pieces) == 1 else finish_pieces_body,
        (
            slab,
            struct((width, wide), F32),
            struct((2 * wide, width), F32),
            struct((3 * wide, width), F32),
            struct((gain_rows, width), F32),
        ),
        [pltpu.VMEM((4 * wide, width), F32)],
        "finish_rest",
        2,
    )(flag, *operands, specs=specs)
    grad_kv = grad_kv.reshape(wide, 2, width)
    grad_qkv = grad_qkv.reshape(3, wide, width).transpose(1, 0, 2)
    gain_total = gain_total.reshape(-1, wide)[:3]
    grad_gains = lax.dynamic_slice(gain_total, (0, me * width), (3, width))
    grad_first = both(grad_own, grad_got)
    return (
        y_first[None],
        y_second[None],
        grad_first[None],
        grad_memory[None],
        grad_gains,
        grad_qkv,
        grad_self_out,
        grad_cross_q,
        grad_kv,
        grad_cross_out,
        grad_up,
        grad_down,
    )


def solution(mesh):
    in_specs = (
        P("dp", "tensor", None),
        P("dp", "tensor", None),
        P("dp", "tensor", None),
        P("dp", "tensor", None),
        P("dp", "tensor", None),
        P("dp", None, None),
        P("dp", None),
        P(),
        P(),
        P(),
        P(None, None, "tensor"),
        P("tensor", None),
        P(None, "tensor"),
        P(None, None, "tensor"),
        P("tensor", None),
        P(None, "tensor"),
        P("tensor", None),
    )
    out_specs = (
        P("dp", "tensor", None),
        P("dp", "tensor", None),
        P("dp", "tensor", None),
        P("dp", "tensor", None),
        P(None, "tensor"),
        P(None, None, "tensor"),
        P("tensor", None),
        P(None, "tensor"),
        P(None, None, "tensor"),
        P("tensor", None),
        P(None, "tensor"),
        P("tensor", None),
    )
    return jax.shard_map(
        on_device, mesh=mesh, in_specs=in_specs, out_specs=out_specs, check_vma=False
    )
```
